32 devices in a mesh: group: 2 (over y), ctx: 4 (over x, core), tp: 4 (over z).
Axes of the slice: x: 2, y: 2, z: 4, core: 2. Of those that a mesh axis runs over, the one named last changes fastest.
Arguments:
- tokens: bfloat16 [1024, 5376], P(('group', 'ctx'), 'tp'), parts along dimension 0
- positions: int32 [1024], P(('group', 'ctx')), parts along dimension 0, may hold values from 0 to 383, as said below
- first_key: int32 [1024], P(('group', 'ctx')), parts along dimension 0, may hold values from 0 to 511, as said below
- input_gain: float32 [5376], replicated, may hold values from 0.1 to 1.9
- query_weight: bfloat16 [5376, 4096], P(None, 'tp'), may hold values from -0.078125 to 0.078125
- kv_weight: bfloat16 [2, 5376, 2048], P(None, None, 'tp'), may hold values from -0.078125 to 0.078125
- query_gain: float32 [128], replicated, may hold values from 0.1 to 1.9
- key_gain: float32 [128], replicated, may hold values from 0.1 to 1.9
- out_weight: bfloat16 [4096, 5376], P('tp'), may hold values from -0.125 to 0.125
- post_gain: float32 [5376], replicated, may hold values from 0.1 to 1.9
Outputs:
- layer_out: bfloat16 [1024, 5376], P(('group', 'ctx'), 'tp'), parts along dimension 0
The draws below stay inside these ranges and needn't reach their ends.
There are 2 independent parts, one for each index of `group`. The reference program is written for one: setup_inputs(seed, part) draws one part's arguments, and reference() takes and returns one part's arrays. A program takes and returns all parts, laid end to end along the dimension named above; an argument that names none is the same for every part. Nothing has to cross between parts.
Inputs may be any that keep to these rules, and one draw needn't show every extreme that they name: `positions`: A token's position is its offset within its document. Documents are contiguous runs of tokens; exactly one of them is 384 tokens long, every other one is shorter, and the last token forms a document of its own. first_key[i] is the larger of i - 1023 and the index of the first token of i's document (documents as described for positions).
All inputs are finite; a program needn't handle non-finite values.
Results may differ from the reference program's by a relative error of at most 0.014.
Values may be sent and summed in bfloat16 or wider, within the bound.
A program may use at most 128 MiB of HBM per device.

```python
import math
import jax
import jax.numpy as jnp
from jax import lax

D = 5376
H = 32
KVH = 16
HD = 128
WINDOW = 1024
SEQ = 512
N_TP = 4


def draw_tokens(key, part):
    base_key, row_key, col_key = jax.random.split(key, 3)
    col_place = jnp.arange(D, dtype=jnp.float32) / D
    col_jitter = jax.random.uniform(col_key, (D,), jnp.float32)
    row_level = jax.random.uniform(row_key, (SEQ, 1), jnp.float32)
    base = jax.random.normal(base_key, (SEQ, D), jnp.float32)
    col_level = 0.5 * col_place + 0.5 * col_jitter - 0.5
    values = base * jnp.power(10.0, row_level - 0.5) * jnp.power(10.0, col_level)[None, :]
    return values.astype(jnp.bfloat16)


def document_starts(key):
    offset_key, cut_key = jax.random.split(jax.random.fold_in(key, 11))
    quarter = SEQ // 4
    long_start = jax.random.randint(offset_key, (), 0, quarter)
    token_index = jnp.arange(SEQ, dtype=jnp.int32)
    cut_here = jax.random.randint(cut_key, (SEQ,), 0, 32) == 0
    inside = (token_index >= long_start) & (token_index < long_start + SEQ - quarter)
    begins = cut_here & jnp.logical_not(inside) | (token_index == long_start) | (token_index == long_start + SEQ - quarter) | (token_index == 0) | (token_index == SEQ - 1)
    marker = jnp.where(begins, token_index, 0).astype(jnp.int32)
    return (token_index, lax.cummax(marker))


def draw_positions(key, part):
    token_index, start_of = document_starts(key)
    return (token_index - start_of).astype(jnp.int32)


def draw_first_key(key, part):
    token_index, start_of = document_starts(key)
    return jnp.maximum(start_of, token_index - WINDOW + 1).astype(jnp.int32)


def with_spikes(drawn, stream_key, source, target, blocks, factor):
    owner, partner = [(jnp.arange(drawn.shape[position]) // (drawn.shape[position] // blocks)).reshape([-1 if axis == position else 1 for axis in range(drawn.ndim)]) for position in (source, target)]
    chosen = jax.random.permutation(stream_key, blocks)[partner]
    strong = (owner == chosen) | (owner == (partner + blocks // 2) % blocks)
    return jnp.where(strong, factor * drawn, drawn)


def block_levels(stream_key, dims, pieces, least, high):
    level = 1.0
    for position, blocks in pieces:
        steps = jax.random.uniform(jax.random.fold_in(jax.random.fold_in(stream_key, 6), position), (blocks,), jnp.float32, least / len(pieces), high / len(pieces))
        level = level * jnp.repeat(jnp.exp(steps), dims[position] // blocks).reshape((-1,) + (1,) * (len(dims) - 1 - position))
    return level


def normal_values(rng, shape, deviation, bound, pieces=(), kind=jnp.bfloat16):
    loudness = block_levels(rng, shape, pieces, -0.22, 0.18) if pieces else 1.0
    drawn = jax.random.normal(rng, shape, jnp.float32) * deviation * loudness
    return jnp.minimum(jnp.maximum(drawn, -bound), bound).astype(kind)


def bell_draw_with(rng, extent, width, most, cuts, heavy, kind=jnp.bfloat16):
    array = width * jax.random.normal(rng, extent, jnp.float32)
    if cuts:
        array = array * block_levels(rng, extent, cuts, -0.22, 0.18)
    return jnp.clip(with_spikes(array, jax.random.fold_in(rng, 3), *heavy), -most, most).astype(kind)


def setup_inputs(seed: int = 0, part: int = 0) -> dict:
    arg_keys = jax.random.split(jax.random.key(seed), 11)
    part_splits = jax.random.split(jax.random.fold_in(arg_keys[10], part), 11)
    return {
        "tokens": draw_tokens(jax.random.fold_in(jax.random.fold_in(arg_keys[10], part), 71), part),
        "positions": draw_positions(jax.random.fold_in(jax.random.fold_in(arg_keys[10], part), 71), part),
        "first_key": draw_first_key(jax.random.fold_in(jax.random.fold_in(arg_keys[10], part), 71), part),
        "input_gain": jnp.clip(1.0 + 0.18 * jax.random.normal(arg_keys[3], (D,), jnp.float32), 0.1, 1.9),
        "query_weight": normal_values(arg_keys[4], (D, H * HD), D ** -0.5, 0.078125, ((1, 4),)),
        "kv_weight": normal_values(arg_keys[5], (2, D, KVH * HD), D ** -0.5, 0.078125, ((2, 4),)),
        "query_gain": jnp.clip(1.0 + 0.18 * jax.random.normal(arg_keys[6], (HD,), jnp.float32), 0.1, 1.9),
        "key_gain": jnp.clip(1.0 + 0.18 * jax.random.normal(arg_keys[7], (HD,), jnp.float32), 0.1, 1.9),
        "out_weight": bell_draw_with(arg_keys[8], (H * HD, D), (H * HD) ** -0.5, 0.125, ((0, 4),), (0, 1, 4, 2.0)),
        "post_gain": jnp.clip(1.0 + 0.18 * jax.random.normal(arg_keys[9], (D,), jnp.float32), 0.1, 1.9),
    }


EPSILON = 1e-06

def rms_norm(values, gain_vec):
    return values * lax.rsqrt(lax.optimization_barrier(jnp.mean(values * values, axis=-1, keepdims=True)) + EPSILON) * gain_vec

def rotate(values, positions_in):
    half_dim = values.shape[-1] // 2
    frequency = jnp.exp(jnp.arange(half_dim, dtype=jnp.float32) * (-2.0 * math.log(10000.0) / values.shape[-1]))
    angles = positions_in.astype(jnp.float32)[:, None] * frequency[None, :]
    cosines = jnp.cos(angles)[:, None, :]
    sine_part = jnp.sin(angles)[:, None, :]
    lower_half = values[..., :half_dim]
    upper_half = values[..., half_dim:]
    return jnp.concatenate([lower_half * cosines - upper_half * sine_part, upper_half * cosines + lower_half * sine_part], axis=-1)

def reference(tokens, positions, first_key, input_gain, query_weight, kv_weight, query_gain, key_gain, out_weight, post_gain):
    seq_len = tokens.shape[0]
    token_x = tokens.astype(jnp.float32)
    normed = rms_norm(token_x, input_gain).astype(jnp.bfloat16)
    query_raw = jnp.dot(normed, query_weight, preferred_element_type=jnp.float32).reshape(seq_len, H, HD)
    key_raw = jnp.dot(normed, kv_weight[0], preferred_element_type=jnp.float32).reshape(seq_len, KVH, HD)
    value_raw = jnp.dot(normed, kv_weight[1], preferred_element_type=jnp.float32).reshape(seq_len, KVH, HD)
    queries = (rotate(rms_norm(query_raw, query_gain), positions) * (D // H) ** (-0.5)).astype(jnp.bfloat16)
    keys = rotate(rms_norm(key_raw, key_gain), positions).astype(jnp.bfloat16)
    values_b = value_raw.astype(jnp.bfloat16)
    token_index = jnp.arange(seq_len, dtype=jnp.int32)
    visible = (token_index[None, :] >= first_key[:, None]) & (token_index[None, :] <= token_index[:, None])

    def one_head(head):
        query_h = lax.dynamic_index_in_dim(queries, head, 1, keepdims=False)
        key_h = lax.dynamic_index_in_dim(keys, head // 2, 1, keepdims=False)
        value_h = lax.dynamic_index_in_dim(values_b, head // 2, 1, keepdims=False)
        scores = jnp.dot(query_h, key_h.T, preferred_element_type=jnp.float32)
        scores = jnp.where(visible, scores, -1e+30)
        row_max = lax.optimization_barrier(jnp.max(scores, axis=1, keepdims=True))
        weights = jnp.exp(scores - row_max)
        denominator = lax.optimization_barrier(jnp.sum(weights, axis=1, keepdims=True))
        mixed_out = jnp.dot(weights.astype(jnp.bfloat16), value_h, preferred_element_type=jnp.float32)
        return (mixed_out / denominator).astype(jnp.bfloat16)
    heads_out = lax.map(one_head, jnp.arange(H, dtype=jnp.int32))
    attn = jnp.transpose(heads_out, (1, 0, 2)).reshape(seq_len, H * HD)
    group_rows = H * HD // N_TP

    def add_group(running, group_id):
        attn_part = lax.dynamic_slice_in_dim(attn, group_id * group_rows, group_rows, 1)
        weight_part = lax.dynamic_slice_in_dim(out_weight, group_id * group_rows, group_rows, 0)
        partial_value = jnp.dot(attn_part, weight_part, preferred_element_type=jnp.float32).astype(jnp.bfloat16)
        partial_value = lax.optimization_barrier(partial_value)
        return (running + partial_value.astype(jnp.float32), None)
    summed, unused = lax.scan(add_group, jnp.zeros((seq_len, D), jnp.float32), jnp.arange(N_TP, dtype=jnp.int32))
    return (token_x + rms_norm(summed, post_gain)).astype(jnp.bfloat16)
```

```python
import math

import jax
import jax.numpy as jnp
from jax import lax
from jax.experimental import pallas as pl
from jax.experimental.pallas import tpu as pltpu
from jax.sharding import PartitionSpec as P

D = 5376
H = 32
WINDOW = 1024


EPSILON = 1e-06


def from_partner(array, axis, distance):
    return lax.ppermute(array, axis, [(i, i ^ 1 << distance) for i in range(lax.axis_size(axis))])


def passed_along(block, axis, distance):
    devices = range(lax.axis_size(axis))
    route = [(i - distance, i) for i in devices if i - distance in devices]
    return lax.ppermute(block, axis, route)


def rms_norm(values, gain_vec):
    return (
        values * lax.rsqrt(jnp.mean(values * values, axis=-1, keepdims=True) + EPSILON) * gain_vec
    )


def rotate(values, positions_in):
    half_dim = values.shape[-1] // 2
    frequency = jnp.exp(
        jnp.arange(half_dim, dtype=jnp.float32) * (-2.0 * math.log(10000.0) / values.shape[-1])
    )
    angles = positions_in.astype(jnp.float32)[:, None] * frequency[None, :]
    cosines = jnp.cos(angles)[:, None, :]
    sine_part = jnp.sin(angles)[:, None, :]
    lower_half = values[..., :half_dim]
    upper_half = values[..., half_dim:]
    return jnp.concatenate(
        [
            lower_half * cosines - upper_half * sine_part,
            upper_half * cosines + lower_half * sine_part,
        ],
        axis=-1,
    )


def per_device(
    tokens,
    positions,
    first_key,
    input_gain,
    query_weight,
    kv_weight,
    query_gain,
    key_gain,
    out_weight,
    post_gain,
):
    tok_rows = tokens.shape[0]
    feat_dev = tokens.shape[1]
    head_dim = query_gain.shape[0]
    heads_dev = query_weight.shape[1] // head_dim
    tp_index = lax.axis_index("tp")
    ctx_index = lax.axis_index("ctx")
    ctx_count = lax.axis_size("ctx")
    local_x = tokens.astype(jnp.float32)
    kv_full = kv_weight
    if heads_dev == 1:
        partner = from_partner(kv_weight, "tp", 0)
        is_even = tp_index % 2 == 0
        kv_full = jnp.where(
            is_even,
            jnp.concatenate([kv_weight, partner], axis=2),
            jnp.concatenate([partner, kv_weight], axis=2),
        )
    gathered = lax.all_gather(tokens, "tp", axis=1, tiled=True).astype(jnp.float32)
    normed = rms_norm(gathered, input_gain).astype(jnp.bfloat16)
    query_raw = jnp.dot(normed, query_weight, preferred_element_type=jnp.float32)
    key_raw = jnp.dot(normed, kv_full[0], preferred_element_type=jnp.float32)
    value_raw = jnp.dot(normed, kv_full[1], preferred_element_type=jnp.float32)
    kv_heads = key_raw.shape[1] // head_dim
    group_size = heads_dev // kv_heads
    queries = (
        rotate(rms_norm(query_raw.reshape(tok_rows, heads_dev, head_dim), query_gain), positions)
        * (D // H) ** (-0.5)
    ).astype(jnp.bfloat16)
    keys = rotate(
        rms_norm(key_raw.reshape(tok_rows, kv_heads, head_dim), key_gain), positions
    ).astype(jnp.bfloat16)
    values_b = value_raw.reshape(tok_rows, kv_heads, head_dim).astype(jnp.bfloat16)
    kv_block = jnp.stack([keys, values_b])
    reach_blocks = min(ctx_count - 1, (WINDOW + tok_rows - 2) // tok_rows)
    received = []
    moving = kv_block
    for offset in range(reach_blocks):
        moving = passed_along(moving, "ctx", 1)
        received.append(moving)
    blocks = received[::-1] + [kv_block]
    keys_all = jnp.concatenate(blocks, axis=1)
    key_count = keys_all.shape[1]
    key_index = (ctx_index - reach_blocks) * tok_rows + jnp.arange(key_count, dtype=jnp.int32)
    query_index = ctx_index * tok_rows + jnp.arange(tok_rows, dtype=jnp.int32)
    visible = (key_index[None, :] >= first_key[:, None]) & (
        key_index[None, :] <= query_index[:, None]
    )
    grouped = queries.reshape(tok_rows, kv_heads, group_size, head_dim)
    scores = jnp.einsum("qkgd,tkd->kgqt", grouped, keys_all[0], preferred_element_type=jnp.float32)
    scores = jnp.where(visible[None, None], scores, -1e30)
    row_max = jnp.max(scores, axis=-1, keepdims=True)
    weights = jnp.exp(scores - row_max)
    denominator = jnp.sum(weights, axis=-1)
    mixed_out = jnp.einsum(
        "kgqt,tkd->qkgd",
        weights.astype(jnp.bfloat16),
        keys_all[1],
        preferred_element_type=jnp.float32,
    )
    mixed_out = mixed_out / jnp.transpose(denominator, (2, 0, 1))[..., None]
    attn = mixed_out.astype(jnp.bfloat16).reshape(tok_rows, heads_dev * head_dim)
    partial_value = jnp.dot(attn, out_weight, preferred_element_type=jnp.float32)
    summed = lax.psum(partial_value.astype(jnp.bfloat16), "tp").astype(jnp.float32)
    post_normed = rms_norm(summed, post_gain)
    own_cols = lax.dynamic_slice_in_dim(post_normed, tp_index * feat_dev, feat_dev, 1)
    return (local_x + own_cols).astype(jnp.bfloat16)


MESH = pl.DeviceIdType.MESH
F32 = jnp.float32
BF16 = jnp.bfloat16
TP = 4
CTX = 4
PHASES = 2
HALVES = 2
HOPS = 4
RS_CHUNKS = 2
PRESCALE = 2.0**-10


def fused_kernel(
    tok_ref, pos_ref, fk_ref, ig_ref, qg_ref, kg_ref, pg_ref, qw_hbm, kvw_hbm, ow_hbm, out_ref,
    xbuf, xg_ref, w_ref, wo_ref, gain_in, gain_post, gain_out, ssq_ref, acc_ref, cos_ref, sin_ref,
    meta_mine, meta_ref, kvbuf, q_ref, attn_ref, part, rup, rdn, own, fin_mine, fin_ref, sq_mine, sq_all,
    w_sem, wo_sem, x_send, ag_up, ag_dn, ag_pt, ag_recv, meta_send, meta_recv, kv_send, kv_recv,
    at_send, at_recv, rs_up_send, rs_dn_send, rs_up_recv, rs_dn_recv, fin_send, fin_recv, sq_send, sq_recv,
):
    feat, rows = tok_ref.shape
    half = feat // HALVES
    hop = feat // HOPS
    per_half = HOPS // HALVES
    chunk = half // RS_CHUNKS
    hd = qg_ref.shape[1]
    kv_cols = kvbuf.shape[3]
    kv_heads = kv_cols // hd
    q_cols = w_ref.shape[1] - 2 * kv_cols
    q_heads = q_cols // hd
    model = feat * TP
    z = lax.axis_index("tp")
    c = lax.axis_index("ctx")
    side = c // 2
    core = c % 2
    carrier = side == core
    partner = c + 1 - 2 * core
    far = lax.rem(c + 2, CTX)
    edge = (z == 0) | (z == TP - 1)
    up = {"tp": lax.rem(z + 1, TP)}
    down = {"tp": lax.rem(z + TP - 1, TP)}

    barrier = pltpu.get_barrier_semaphore()

    @pl.when(z < TP - 1)
    def _():
        pl.semaphore_signal(barrier, inc=1, device_id=up, device_id_type=MESH)

    @pl.when(z > 0)
    def _():
        pl.semaphore_signal(barrier, inc=1, device_id=down, device_id_type=MESH)

    for other in (far, partner, CTX - 1 - c):
        pl.semaphore_signal(barrier, inc=1, device_id={"ctx": other}, device_id_type=MESH)

    def half_span(spot):
        return pl.ds(pl.multiple_of(spot * half, 32), half)

    def weight_copies(spot):
        span = half_span(spot)
        kv_from = pl.ds(pl.multiple_of(core * kv_cols, 128), kv_cols)
        q_from = pl.ds(pl.multiple_of(core * q_cols, 128), q_cols)
        return (
            pltpu.make_async_copy(
                kvw_hbm.at[0, span, kv_from], w_ref.at[span, 0:kv_cols], w_sem.at[spot, 0]
            ),
            pltpu.make_async_copy(
                kvw_hbm.at[1, span, kv_from], w_ref.at[span, kv_cols : 2 * kv_cols], w_sem.at[spot, 1]
            ),
            pltpu.make_async_copy(
                qw_hbm.at[span, q_from], w_ref.at[span, 2 * kv_cols :], w_sem.at[spot, 2]
            ),
        )

    def source(i):
        second = jnp.where(z % 2 == 0, 1, 2)
        third = jnp.where(z == 0, 2, jnp.where(z == 1, 0, jnp.where(z == 2, 3, 1)))
        fourth = jnp.where(z < TP // 2, TP - 1, 0)
        return jnp.where(i == 0, z, jnp.where(i == 1, second, jnp.where(i == 2, third, fourth)))

    extra = half % 128
    turns = 128 // extra
    wide = half + 128 - extra

    def turn_of(dest):
        return (dest * HALVES + core) % turns

    def wo_copy(dest):
        start = pl.multiple_of((dest * HALVES + core) * half - turn_of(dest) * extra, 128)
        return pltpu.make_async_copy(ow_hbm.at[:, pl.ds(start, wide)], wo_ref.at[dest], wo_sem.at[dest])

    def out_order(i):
        outer = TP - 1 - i
        inner = jnp.where(i == 0, 3, jnp.where(i == 1, 0, jnp.where(i == 2, 2, 1)))
        dest = jnp.where(edge, outer, inner)
        return jnp.where(z < TP // 2, dest, TP - 1 - dest)

    def begin_weights(i, carry):
        for g in range(HALVES):
            for copy in weight_copies(source(i) * HALVES + g):
                copy.start()
        return carry

    lax.fori_loop(0, TP, begin_weights, 0)

    def begin_wo(i, carry):
        wo_copy(out_order(i)).start()
        return carry

    lax.fori_loop(0, TP, begin_wo, 0)

    meta_mine[0:1] = pos_ref[...]
    meta_mine[1:2] = fk_ref[...]

    @pl.when(carrier)
    def _():
        xbuf[side, z] = tok_ref[...]
        meta_ref[side] = meta_mine[...]

    pl.semaphore_wait(barrier, jnp.where(edge, 4, 5))

    def hop_span(ch):
        return pl.ds(pl.multiple_of(ch * hop, 16), hop)

    def x_copy(ch):
        return pltpu.make_async_remote_copy(
            src_ref=tok_ref.at[hop_span(ch)],
            dst_ref=xbuf.at[side, z, hop_span(ch)],
            send_sem=x_send.at[ch],
            recv_sem=ag_recv.at[side, z, ch],
            device_id={"ctx": far},
            device_id_type=MESH,
        )

    def ag_copy(p, src, ch, send, target):
        here = xbuf.at[p, src, hop_span(ch)]
        return pltpu.make_async_remote_copy(
            src_ref=here,
            dst_ref=here,
            send_sem=send.at[p, src, ch],
            recv_sem=ag_recv.at[p, src, ch],
            device_id=target,
            device_id_type=MESH,
        )

    def meta_copy(j, target):
        return pltpu.make_async_remote_copy(
            src_ref=meta_mine,
            dst_ref=meta_ref.at[side],
            send_sem=meta_send.at[j],
            recv_sem=meta_recv.at[side],
            device_id={"ctx": target},
            device_id_type=MESH,
        )

    def forward(p, src, ch):
        @pl.when(carrier & (src <= z) & (z < TP - 1))
        def _():
            ag_copy(p, src, ch, ag_up, up).start()

        @pl.when(carrier & (src >= z) & (z > 0))
        def _():
            ag_copy(p, src, ch, ag_dn, down).start()

        @pl.when(carrier)
        def _():
            ag_copy(p, src, ch, ag_pt, {"ctx": partner}).start()

    @pl.when(jnp.logical_not(carrier))
    def _():
        for ch in range(HOPS):
            x_copy(ch).start()
        meta_copy(0, far).start()
        meta_copy(1, CTX - 1 - c).start()

    @pl.when(carrier)
    def _():
        meta_copy(0, partner).start()

    ssq_ref[...] = jnp.zeros_like(ssq_ref)
    acc_ref[...] = jnp.zeros_like(acc_ref)
    r_iota = lax.broadcasted_iota(jnp.int32, (rows, rows), 0)
    c_iota = lax.broadcasted_iota(jnp.int32, (rows, rows), 1)
    diagonal = r_iota == c_iota

    def as_column(row):
        return jnp.sum(jnp.where(diagonal, row, 0.0), axis=1, keepdims=True)

    def prepare_gains():
        gains = ig_ref[...].reshape(1, model) * PRESCALE
        for i in range(TP * HALVES):
            gain_in[i] = gains[:, i * half : (i + 1) * half]

    def prepare_trig(p, carry):
        @pl.when(jnp.logical_not(carrier & (side == p)))
        def _():
            pltpu.make_async_copy(meta_mine, meta_ref.at[p], meta_recv.at[p]).wait()

        lane = lax.broadcasted_iota(jnp.int32, (rows, hd), 1)
        place = jnp.where(lane < hd // 2, lane, lane - hd // 2).astype(F32)
        angles = as_column(meta_ref[p, 0:1].astype(F32)) * jnp.exp(
            place * (-2.0 * math.log(10000.0) / hd)
        )
        cos_ref[p] = jnp.cos(angles)
        sines = jnp.sin(angles)
        sin_ref[p] = jnp.where(lane < hd // 2, -sines, sines)
        return carry

    def arrive(p, i, g):
        src = source(i)
        for j in range(per_half):
            ch = g * per_half + j
            local = carrier & (i == 0) & ((side == p) if p == 0 else True)

            @pl.when(jnp.logical_not(local))
            def _():
                ag_copy(p, src, ch, ag_pt, {"ctx": partner}).wait_recv()

            @pl.when((p == 0) | (i > 0))
            def _():
                forward(p, src, ch)

    def begin_second():
        for ch in range(HOPS):
            @pl.when(carrier & (side == 0))
            def _():
                ag_copy(1, z, ch, ag_pt, {"ctx": partner}).wait_recv()

            forward(1, z, ch)

    kv_width = 2 * kv_cols

    def project(p, i, g):
        src = source(i)
        spot = src * HALVES + g
        x_t = xbuf[p, src, pl.ds(pl.multiple_of(g * half, 32), half)].astype(F32)
        ssq_ref[p] += jnp.sum(x_t * x_t, axis=0, keepdims=True)
        xg_ref[...] = (x_t.T * gain_in[spot]).astype(BF16)
        last = (i == TP - 1) & (g == HALVES - 1)
        if p == 0:
            for copy in weight_copies(spot):
                copy.wait()

        @pl.when(jnp.logical_not(last))
        def _():
            acc_ref[p] += jnp.dot(xg_ref[...], w_ref[half_span(spot)], preferred_element_type=F32)

        @pl.when(last)
        def _():
            acc_ref[p, :, 0:kv_width] += jnp.dot(
                xg_ref[...], w_ref[half_span(spot), 0:kv_width], preferred_element_type=F32
            )

    def first_gather(step, carry):
        i = step // HALVES
        g = step % HALVES
        arrive(0, i, g)

        @pl.when((g == HALVES - 1) & (i == jnp.where(edge, 1, TP - 1)))
        def _():
            begin_second()

        @pl.when(step == 0)
        def _():
            prepare_gains()

        project(0, i, g)

        @pl.when(step == 1)
        def _():
            lax.fori_loop(0, PHASES, prepare_trig, 0)

        return carry

    lax.fori_loop(0, TP * HALVES, first_gather, 0)

    def kv_copy(p):
        block = 2 * p + side
        return pltpu.make_async_remote_copy(
            src_ref=kvbuf.at[block],
            dst_ref=kvbuf.at[block],
            send_sem=kv_send.at[p],
            recv_sem=kv_recv.at[block],
            device_id={"ctx": far},
            device_id_type=MESH,
        )

    def kv_arrived(block):
        pltpu.make_async_copy(kvbuf.at[block], kvbuf.at[block], kv_recv.at[block]).wait()

    def attn_copy(p, h):
        here = attn_ref.at[p, kv_heads * core + h]
        return pltpu.make_async_remote_copy(
            src_ref=here,
            dst_ref=here,
            send_sem=at_send.at[p, h],
            recv_sem=at_recv.at[p, h],
            device_id={"ctx": partner},
            device_id_type=MESH,
        )

    def attend(p, blocks):
        first = as_column(meta_ref[p, 1:2].astype(F32)).astype(jnp.int32)
        shape = (rows, blocks * rows)
        key_index = lax.broadcasted_iota(jnp.int32, shape, 1)
        query_index = (blocks - 1) * rows + lax.broadcasted_iota(jnp.int32, shape, 0)
        visible = (key_index >= first) & (key_index <= query_index)
        bias = jnp.where(visible, 0.0, -1e30)
        bias = jnp.concatenate([bias, bias], axis=0)
        for h in range(kv_heads):
            cols = slice(h * hd, (h + 1) * hd)
            s = jnp.concatenate(
                [
                    lax.dot_general(
                        q_ref[h], kvbuf[j, 0, :, cols], (((1,), (1,)), ((), ())),
                        preferred_element_type=F32,
                    )
                    for j in range(blocks)
                ],
                axis=1,
            ) + bias
            weights = jnp.exp(s - jnp.max(s, axis=1, keepdims=True))
            total = jnp.sum(weights, axis=1, keepdims=True)
            weights = weights.astype(BF16)
            mixed = sum(
                jnp.dot(
                    weights[:, j * rows : (j + 1) * rows], kvbuf[j, 1, :, cols],
                    preferred_element_type=F32,
                )
                for j in range(blocks)
            )
            mixed = (mixed / total).astype(BF16)
            attn_ref[p, kv_heads * core + h] = jnp.concatenate([mixed[:rows], mixed[rows:]], axis=1)
            attn_copy(p, h).start()

    def attention(p):
        inv = lax.rsqrt(as_column(ssq_ref[p]) * (1.0 / model) + EPSILON) * (1.0 / PRESCALE)

        def normed_rotated(raw, gain_vec):
            raw = raw * inv
            scaled = raw * lax.rsqrt(jnp.mean(raw * raw, axis=1, keepdims=True) + EPSILON) * gain_vec
            return scaled * cos_ref[p] + pltpu.roll(scaled, hd // 2, 1) * sin_ref[p]

        block = 2 * p + side
        for h in range(kv_heads):
            cols = slice(h * hd, (h + 1) * hd)
            kvbuf[block, 0, :, cols] = normed_rotated(acc_ref[p, :, cols], kg_ref[...]).astype(BF16)
        kvbuf[block, 1] = (acc_ref[p, :, kv_cols:kv_width] * inv).astype(BF16)

        @pl.when((p == 0) | (side == 0))
        def _():
            kv_copy(p).start()

        spot = source(TP - 1) * HALVES + HALVES - 1
        acc_ref[p, :, kv_width:] += jnp.dot(
            xg_ref[...], w_ref[half_span(spot), kv_width:], preferred_element_type=F32
        )
        for h in range(q_heads):
            cols = slice(kv_width + h * hd, kv_width + (h + 1) * hd)
            q_ref[h // 2, (h % 2) * rows : (h % 2 + 1) * rows] = (
                normed_rotated(acc_ref[p, :, cols], qg_ref[...]) * (D // H) ** (-0.5)
            ).astype(BF16)

        @pl.when(side == 0)
        def _():
            if p == 1:
                kv_arrived(1)
            attend(p, 2 * p + 1)

        @pl.when(side == 1)
        def _():
            kv_arrived(2 * p)
            attend(p, 2 * p + 2)

    def rs_copy(p, dest, ch, buf, send, recv, target):
        start = pl.multiple_of(turn_of(dest) * extra + ch * chunk, 16)
        return pltpu.make_async_remote_copy(
            src_ref=part.at[p, dest, pl.ds(start, chunk)],
            dst_ref=buf.at[p, dest, pl.ds(pl.multiple_of(ch * chunk, 16), chunk)],
            send_sem=send.at[p, dest, ch],
            recv_sem=recv.at[p, dest, ch],
            device_id=target,
            device_id_type=MESH,
        )

    def rs_up(p, dest, ch):
        return rs_copy(p, dest, ch, rup, rs_up_send, rs_up_recv, up)

    def rs_dn(p, dest, ch):
        return rs_copy(p, dest, ch, rdn, rs_dn_send, rs_dn_recv, down)

    def output_terms(p):
        for h in range(kv_heads):
            attn_copy(p, h).wait_recv()

        def out_step(i, carry):
            dest = out_order(i)
            if p == 0:
                wo_copy(dest).wait()
            mixed = jnp.concatenate([attn_ref[p, j] for j in range(2 * kv_heads)], axis=1)
            part[p, dest] = jnp.dot(mixed, wo_ref[dest], preferred_element_type=F32).T.astype(BF16)

            for ch in range(RS_CHUNKS):
                @pl.when((z == 0) & (dest > 0))
                def _():
                    rs_up(p, dest, ch).start()

                @pl.when((z == TP - 1) & (dest < TP - 1))
                def _():
                    rs_dn(p, dest, ch).start()

            return carry

        lax.fori_loop(0, TP, out_step, 0)
        own[p] = part[p, z, pl.ds(pl.multiple_of(turn_of(z) * extra, 16), half)].astype(F32)

    def fin_copy(p, ch):
        span = pl.ds(pl.multiple_of(ch * chunk, 16), chunk)
        return pltpu.make_async_remote_copy(
            src_ref=fin_mine.at[p, span],
            dst_ref=fin_ref.at[core, span],
            send_sem=fin_send.at[p, ch],
            recv_sem=fin_recv.at[core, ch],
            device_id={"ctx": 2 * p + side},
            device_id_type=MESH,
        )

    def sq_copy(p, d):
        return pltpu.make_async_remote_copy(
            src_ref=sq_mine.at[p],
            dst_ref=sq_all.at[HALVES * z + core],
            send_sem=sq_send.at[p, d],
            recv_sem=sq_recv.at[HALVES * z + core],
            device_id={"ctx": 2 * p + side, "tp": lax.rem(z + d, TP)},
            device_id_type=MESH,
        )

    def sum_terms(p):
        mine = c == 2 * p + side

        def sum_step(k, carry):
            from_low = z + TP - 1 - k
            from_high = z + k - (TP - 1)
            for ch in range(RS_CHUNKS):
                span = slice(ch * chunk, (ch + 1) * chunk)
                for dest, has, buf, copy in (
                    (from_low, (z > 0) & (from_low < TP), rup, rs_up),
                    (from_high, (z < TP - 1) & (from_high >= 0), rdn, rs_dn),
                ):
                    @pl.when(has)
                    def _():
                        copy(p, dest, ch).wait_recv()

                        @pl.when(dest != z)
                        def _():
                            start = pl.multiple_of(turn_of(dest) * extra + ch * chunk, 16)
                            there = pl.ds(start, chunk)
                            part[p, dest, there] = (
                                part[p, dest, there].astype(F32) + buf[p, dest, span].astype(F32)
                            ).astype(BF16)
                            copy(p, dest, ch).start()

                        @pl.when(dest == z)
                        def _():
                            own[p, span] += buf[p, dest, span].astype(F32)

                @pl.when(k == TP - 1)
                def _():
                    rounded = own[p, span].astype(BF16)

                    @pl.when(mine)
                    def _():
                        fin_ref[core, span] = rounded

                    @pl.when(jnp.logical_not(mine))
                    def _():
                        fin_mine[p, span] = rounded
                        fin_copy(p, ch).start()

            return carry

        lax.fori_loop(1, TP, sum_step, 0)
        as_row = jnp.sum(own[p] * own[p], axis=0, keepdims=True)
        sq_mine[p] = jnp.broadcast_to(as_row, sq_mine.shape[1:])

        @pl.when(mine)
        def _():
            sq_all[HALVES * z + core] = sq_mine[p]

        @pl.when(jnp.logical_not(mine))
        def _():
            sq_copy(p, 0).start()

        for d in range(1, TP):
            sq_copy(p, d).start()

    attention(0)
    for g in range(HALVES):
        arrive(1, 1, g)
    output_terms(0)

    def second_gather(step, carry):
        i = step // HALVES
        g = step % HALVES

        @pl.when(i != 1)
        def _():
            arrive(1, i, g)

        project(1, i, g)
        return carry

    lax.fori_loop(0, TP * HALVES, second_gather, 0)
    attention(1)
    output_terms(1)
    post_gains = pg_ref[...].reshape(1, model)
    for i in range(TP):
        gain_post[i] = post_gains[:, i * feat : (i + 1) * feat]
    gain_out[...] = jnp.broadcast_to(gain_post[z], (rows, feat)).T
    sum_terms(0)
    sum_terms(1)

    source_side = c % 2

    def collect(i, carry):
        zz = i // HALVES
        kk = i % HALVES

        @pl.when(jnp.logical_not((zz == z) & (2 * source_side + kk == c)))
        def _():
            pltpu.make_async_copy(sq_mine.at[0], sq_all.at[i], sq_recv.at[i]).wait()

        return carry

    lax.fori_loop(0, TP * HALVES, collect, 0)
    total = jnp.sum(sq_all[...], axis=0)[0:1]
    inv_post = lax.rsqrt(total * (1.0 / model) + EPSILON)
    for kk in range(HALVES):
        for ch in range(RS_CHUNKS):
            @pl.when(2 * source_side + kk != c)
            def _():
                there = fin_ref.at[kk, slice(ch * chunk, (ch + 1) * chunk)]
                pltpu.make_async_copy(there, there, fin_recv.at[kk, ch]).wait()

            span = slice(kk * half + ch * chunk, kk * half + (ch + 1) * chunk)
            summed = fin_ref[kk, ch * chunk : (ch + 1) * chunk].astype(F32)
            out_ref[span] = (
                tok_ref[span].astype(F32) + summed * inv_post * gain_out[span]
            ).astype(BF16)

    @pl.when(jnp.logical_not(carrier))
    def _():
        for ch in range(HOPS):
            x_copy(ch).wait_send()
        meta_copy(0, far).wait_send()
        meta_copy(1, CTX - 1 - c).wait_send()

    @pl.when(carrier)
    def _():
        meta_copy(0, partner).wait_send()

    for p in range(PHASES):
        def settle(i, carry):
            @pl.when(carrier)
            def _():
                for ch in range(HOPS):
                    @pl.when((z < TP - 1) & (i <= z))
                    def _():
                        ag_copy(p, i, ch, ag_up, up).wait_send()

                    @pl.when((z > 0) & (i >= z))
                    def _():
                        ag_copy(p, i, ch, ag_dn, down).wait_send()

                    ag_copy(p, i, ch, ag_pt, {"ctx": partner}).wait_send()

            for ch in range(RS_CHUNKS):
                @pl.when(i > z)
                def _():
                    rs_up(p, i, ch).wait_send()

                @pl.when(i < z)
                def _():
                    rs_dn(p, i, ch).wait_send()

            return carry

        lax.fori_loop(0, TP, settle, 0)

        @pl.when((p == 0) | (side == 0))
        def _():
            kv_copy(p).wait_send()

        for h in range(kv_heads):
            attn_copy(p, h).wait_send()

        @pl.when(c != 2 * p + side)
        def _():
            for ch in range(RS_CHUNKS):
                fin_copy(p, ch).wait_send()
            sq_copy(p, 0).wait_send()

        for d in range(1, TP):
            sq_copy(p, d).wait_send()


def per_device_fused(
    tokens, positions, first_key, input_gain, query_weight, kv_weight, query_gain, key_gain,
    out_weight, post_gain,
):
    feat, rows = tokens.shape[1], tokens.shape[0]
    half = feat // HALVES
    hd = query_gain.shape[0]
    model = query_weight.shape[0]
    q_cols = query_weight.shape[1] // 2
    kv_cols = kv_weight.shape[2] // 2
    kv_heads = kv_cols // hd
    wide = half + 128 - half % 128
    vmem = pl.BlockSpec(memory_space=pltpu.VMEM)
    anywhere = pl.BlockSpec(memory_space=pl.ANY)
    dma = pltpu.SemaphoreType.DMA
    return pl.pallas_call(
        fused_kernel,
        out_shape=jax.ShapeDtypeStruct((feat, rows), BF16),
        in_specs=[vmem] * 7 + [anywhere] * 3,
        out_specs=vmem,
        scratch_shapes=[
            pltpu.VMEM((PHASES, TP, feat, rows), BF16),
            pltpu.VMEM((rows, half), BF16),
            pltpu.VMEM((model, q_cols + 2 * kv_cols), BF16),
            pltpu.VMEM((TP, 2 * q_cols, wide), BF16),
            pltpu.VMEM((TP * HALVES, 1, half), F32),
            pltpu.VMEM((TP, 1, feat), F32),
            pltpu.VMEM((feat, rows), F32),
            pltpu.VMEM((PHASES, 1, rows), F32),
            pltpu.VMEM((PHASES, rows, q_cols + 2 * kv_cols), F32),
            pltpu.VMEM((PHASES, rows, hd), F32),
            pltpu.VMEM((PHASES, rows, hd), F32),
            pltpu.VMEM((8, rows), jnp.int32),
            pltpu.VMEM((PHASES, 8, rows), jnp.int32),
            pltpu.VMEM((CTX, 2, rows, kv_cols), BF16),
            pltpu.VMEM((kv_heads, 2 * rows, hd), BF16),
            pltpu.VMEM((PHASES, 2 * kv_heads, rows, 2 * hd), BF16),
            pltpu.VMEM((PHASES, TP, wide, rows), BF16),
            pltpu.VMEM((PHASES, TP, half, rows), BF16),
            pltpu.VMEM((PHASES, TP, half, rows), BF16),
            pltpu.VMEM((PHASES, half, rows), F32),
            pltpu.VMEM((PHASES, half, rows), BF16),
            pltpu.VMEM((HALVES, half, rows), BF16),
            pltpu.VMEM((PHASES, 8, rows), F32),
            pltpu.VMEM((TP * HALVES, 8, rows), F32),
            dma((TP * HALVES, 3)),
            dma((TP,)),
            dma((HOPS,)),
            dma((PHASES, TP, HOPS)),
            dma((PHASES, TP, HOPS)),
            dma((PHASES, TP, HOPS)),
            dma((PHASES, TP, HOPS)),
            dma((2,)),
            dma((PHASES,)),
            dma((PHASES,)),
            dma((CTX,)),
            dma((PHASES, kv_heads)),
            dma((PHASES, kv_heads)),
            dma((PHASES, TP, RS_CHUNKS)),
            dma((PHASES, TP, RS_CHUNKS)),
            dma((PHASES, TP, RS_CHUNKS)),
            dma((PHASES, TP, RS_CHUNKS)),
            dma((PHASES, RS_CHUNKS)),
            dma((HALVES, RS_CHUNKS)),
            dma((PHASES, TP)),
            dma((TP * HALVES,)),
        ],
        compiler_params=pltpu.CompilerParams(
            collective_id=0, has_side_effects=True, vmem_limit_bytes=60 * 1024 * 1024
        ),
    )(
        tokens.T,
        positions.reshape(1, rows),
        first_key.reshape(1, rows),
        input_gain,
        query_gain.reshape(1, hd),
        key_gain.reshape(1, hd),
        post_gain,
        query_weight,
        kv_weight,
        out_weight,
    ).T


def solution(mesh):
    fused = mesh.shape["tp"] == TP and mesh.shape["ctx"] == CTX
    return jax.shard_map(
        per_device_fused if fused else per_device,
        mesh=mesh,
        in_specs=(
            P(("group", "ctx"), "tp"),
            P(("group", "ctx")),
            P(("group", "ctx")),
            P(),
            P(None, "tp"),
            P(None, None, "tp"),
            P(),
            P(),
            P("tp", None),
            P(),
        ),
        out_specs=P(("group", "ctx"), "tp"),
        check_vma=False,
    )
```

```python
import math

import jax
import jax.numpy as jnp
from jax import lax
from jax.experimental import pallas as pl
from jax.experimental.pallas import tpu as pltpu
from jax.sharding import PartitionSpec as P

D = 5376
H = 32
WINDOW = 1024


EPSILON = 1e-06


def from_partner(array, axis, distance):
    return lax.ppermute(array, axis, [(i, i ^ 1 << distance) for i in range(lax.axis_size(axis))])


def passed_along(block, axis, distance):
    devices = range(lax.axis_size(axis))
    route = [(i - distance, i) for i in devices if i - distance in devices]
    return lax.ppermute(block, axis, route)


def rms_norm(values, gain_vec):
    return (
        values * lax.rsqrt(jnp.mean(values * values, axis=-1, keepdims=True) + EPSILON) * gain_vec
    )


def rotate(values, positions_in):
    half_dim = values.shape[-1] // 2
    frequency = jnp.exp(
        jnp.arange(half_dim, dtype=jnp.float32) * (-2.0 * math.log(10000.0) / values.shape[-1])
    )
    angles = positions_in.astype(jnp.float32)[:, None] * frequency[None, :]
    cosines = jnp.cos(angles)[:, None, :]
    sine_part = jnp.sin(angles)[:, None, :]
    lower_half = values[..., :half_dim]
    upper_half = values[..., half_dim:]
    return jnp.concatenate(
        [
            lower_half * cosines - upper_half * sine_part,
            upper_half * cosines + lower_half * sine_part,
        ],
        axis=-1,
    )


def per_device(
    tokens,
    positions,
    first_key,
    input_gain,
    query_weight,
    kv_weight,
    query_gain,
    key_gain,
    out_weight,
    post_gain,
):
    tok_rows = tokens.shape[0]
    feat_dev = tokens.shape[1]
    head_dim = query_gain.shape[0]
    heads_dev = query_weight.shape[1] // head_dim
    tp_index = lax.axis_index("tp")
    ctx_index = lax.axis_index("ctx")
    ctx_count = lax.axis_size("ctx")
    local_x = tokens.astype(jnp.float32)
    kv_full = kv_weight
    if heads_dev == 1:
        partner = from_partner(kv_weight, "tp", 0)
        is_even = tp_index % 2 == 0
        kv_full = jnp.where(
            is_even,
            jnp.concatenate([kv_weight, partner], axis=2),
            jnp.concatenate([partner, kv_weight], axis=2),
        )
    gathered = lax.all_gather(tokens, "tp", axis=1, tiled=True).astype(jnp.float32)
    normed = rms_norm(gathered, input_gain).astype(jnp.bfloat16)
    query_raw = jnp.dot(normed, query_weight, preferred_element_type=jnp.float32)
    key_raw = jnp.dot(normed, kv_full[0], preferred_element_type=jnp.float32)
    value_raw = jnp.dot(normed, kv_full[1], preferred_element_type=jnp.float32)
    kv_heads = key_raw.shape[1] // head_dim
    group_size = heads_dev // kv_heads
    queries = (
        rotate(rms_norm(query_raw.reshape(tok_rows, heads_dev, head_dim), query_gain), positions)
        * (D // H) ** (-0.5)
    ).astype(jnp.bfloat16)
    keys = rotate(
        rms_norm(key_raw.reshape(tok_rows, kv_heads, head_dim), key_gain), positions
    ).astype(jnp.bfloat16)
    values_b = value_raw.reshape(tok_rows, kv_heads, head_dim).astype(jnp.bfloat16)
    kv_block = jnp.stack([keys, values_b])
    reach_blocks = min(ctx_count - 1, (WINDOW + tok_rows - 2) // tok_rows)
    received = []
    moving = kv_block
    for offset in range(reach_blocks):
        moving = passed_along(moving, "ctx", 1)
        received.append(moving)
    blocks = received[::-1] + [kv_block]
    keys_all = jnp.concatenate(blocks, axis=1)
    key_count = keys_all.shape[1]
    key_index = (ctx_index - reach_blocks) * tok_rows + jnp.arange(key_count, dtype=jnp.int32)
    query_index = ctx_index * tok_rows + jnp.arange(tok_rows, dtype=jnp.int32)
    visible = (key_index[None, :] >= first_key[:, None]) & (
        key_index[None, :] <= query_index[:, None]
    )
    grouped = queries.reshape(tok_rows, kv_heads, group_size, head_dim)
    scores = jnp.einsum("qkgd,tkd->kgqt", grouped, keys_all[0], preferred_element_type=jnp.float32)
    scores = jnp.where(visible[None, None], scores, -1e30)
    row_max = jnp.max(scores, axis=-1, keepdims=True)
    weights = jnp.exp(scores - row_max)
    denominator = jnp.sum(weights, axis=-1)
    mixed_out = jnp.einsum(
        "kgqt,tkd->qkgd",
        weights.astype(jnp.bfloat16),
        keys_all[1],
        preferred_element_type=jnp.float32,
    )
    mixed_out = mixed_out / jnp.transpose(denominator, (2, 0, 1))[..., None]
    attn = mixed_out.astype(jnp.bfloat16).reshape(tok_rows, heads_dev * head_dim)
    partial_value = jnp.dot(attn, out_weight, preferred_element_type=jnp.float32)
    summed = lax.psum(partial_value.astype(jnp.bfloat16), "tp").astype(jnp.float32)
    post_normed = rms_norm(summed, post_gain)
    own_cols = lax.dynamic_slice_in_dim(post_normed, tp_index * feat_dev, feat_dev, 1)
    return (local_x + own_cols).astype(jnp.bfloat16)


MESH = pl.DeviceIdType.MESH
F32 = jnp.float32
BF16 = jnp.bfloat16
TP = 4
CTX = 4
PHASES = 2
HALVES = 2
HOPS = 4
RS_CHUNKS = 2
PRESCALE = 2.0**-10


def fused_kernel(
    tok_ref, pos_ref, fk_ref, ig_ref, qg_ref, kg_ref, pg_ref, qw_hbm, kvw_hbm, ow_hbm, out_ref,
    xbuf, xg_ref, w_ref, wo_ref, gain_in, gain_post, gain_out, ssq_ref, acc_ref, cos_ref, sin_ref,
    meta_mine, meta_ref, kvbuf, q_ref, attn_ref, part, rup, rdn, own, fin_mine, fin_ref, sq_mine, sq_all,
    w_sem, wo_sem, x_send, ag_up, ag_dn, ag_pt, ag_recv, meta_send, meta_recv, kv_send, kv_recv,
    at_send, at_recv, rs_send, rs_up_recv, rs_dn_recv, fin_send, fin_recv, sq_send, sq_recv,
):
    feat, rows = tok_ref.shape
    half = feat // HALVES
    hop = feat // HOPS
    per_half = HOPS // HALVES
    chunk = half // RS_CHUNKS
    hd = qg_ref.shape[1]
    kv_heads = kvbuf.shape[1]
    kv_cols = kv_heads * hd
    q_cols = w_ref.shape[1] - 2 * kv_cols
    q_heads = q_cols // hd
    model = feat * TP
    z = lax.axis_index("tp")
    c = lax.axis_index("ctx")
    side = c // 2
    core = c % 2
    carrier = side == core
    partner = c + 1 - 2 * core
    far = lax.rem(c + 2, CTX)
    edge = (z == 0) | (z == TP - 1)
    up = {"tp": lax.rem(z + 1, TP)}
    down = {"tp": lax.rem(z + TP - 1, TP)}

    barrier = pltpu.get_barrier_semaphore()

    @pl.when(z < TP - 1)
    def _():
        pl.semaphore_signal(barrier, inc=1, device_id=up, device_id_type=MESH)

    @pl.when(z > 0)
    def _():
        pl.semaphore_signal(barrier, inc=1, device_id=down, device_id_type=MESH)

    for other in (far, partner, CTX - 1 - c):
        pl.semaphore_signal(barrier, inc=1, device_id={"ctx": other}, device_id_type=MESH)

    def half_span(spot):
        return pl.ds(pl.multiple_of(spot * half, 32), half)

    def weight_copies(spot):
        span = half_span(spot)
        kv_from = pl.ds(pl.multiple_of(core * kv_cols, 128), kv_cols)
        q_from = pl.ds(pl.multiple_of(core * q_cols, 128), q_cols)
        return (
            pltpu.make_async_copy(
                kvw_hbm.at[0, span, kv_from], w_ref.at[span, 0:kv_cols], w_sem.at[spot]
            ),
            pltpu.make_async_copy(
                kvw_hbm.at[1, span, kv_from], w_ref.at[span, kv_cols : 2 * kv_cols], w_sem.at[spot]
            ),
            pltpu.make_async_copy(
                qw_hbm.at[span, q_from], w_ref.at[span, 2 * kv_cols :], w_sem.at[spot]
            ),
        )

    def source(i):
        second = jnp.where(z % 2 == 0, 1, 2)
        third = jnp.where(z == 0, 2, jnp.where(z == 1, 0, jnp.where(z == 2, 3, 1)))
        fourth = jnp.where(z < TP // 2, TP - 1, 0)
        return jnp.where(i == 0, z, jnp.where(i == 1, second, jnp.where(i == 2, third, fourth)))

    extra = half % 128
    turns = 128 // extra
    wide = half + 128 - extra

    def turn_of(dest):
        return (dest * HALVES + core) % turns

    def wo_copy(dest):
        start = pl.multiple_of((dest * HALVES + core) * half - turn_of(dest) * extra, 128)
        return pltpu.make_async_copy(ow_hbm.at[:, pl.ds(start, wide)], wo_ref.at[dest], wo_sem.at[dest])

    def out_order(i):
        outer = TP - 1 - i
        inner = jnp.where(i == 0, 3, jnp.where(i == 1, 0, jnp.where(i == 2, 2, 1)))
        dest = jnp.where(edge, outer, inner)
        return jnp.where(z < TP // 2, dest, TP - 1 - dest)

    def begin_weights(i, carry):
        for g in range(HALVES):
            for copy in weight_copies(source(i) * HALVES + g):
                copy.start()
        return carry

    lax.fori_loop(0, TP, begin_weights, 0)

    def begin_wo(i, carry):
        wo_copy(out_order(i)).start()
        return carry

    lax.fori_loop(0, TP, begin_wo, 0)

    meta_mine[0:1] = pos_ref[...]
    meta_mine[1:2] = fk_ref[...]

    @pl.when(carrier)
    def _():
        xbuf[side, z] = tok_ref[...]
        meta_ref[side] = meta_mine[...]

    pl.semaphore_wait(barrier, jnp.where(edge, 4, 5))

    def hop_span(ch):
        return pl.ds(pl.multiple_of(ch * hop, 16), hop)

    def x_copy(ch):
        return pltpu.make_async_remote_copy(
            src_ref=tok_ref.at[hop_span(ch)],
            dst_ref=xbuf.at[side, z, hop_span(ch)],
            send_sem=x_send,
            recv_sem=ag_recv.at[side, z, ch],
            device_id={"ctx": far},
            device_id_type=MESH,
        )

    def ag_copy(p, src, ch, send, target):
        here = xbuf.at[p, src, hop_span(ch)]
        return pltpu.make_async_remote_copy(
            src_ref=here,
            dst_ref=here,
            send_sem=send.at[p, src],
            recv_sem=ag_recv.at[p, src, ch],
            device_id=target,
            device_id_type=MESH,
        )

    def meta_copy(target):
        return pltpu.make_async_remote_copy(
            src_ref=meta_mine,
            dst_ref=meta_ref.at[side],
            send_sem=meta_send,
            recv_sem=meta_recv.at[side],
            device_id={"ctx": target},
            device_id_type=MESH,
        )

    def forward(p, src, ch):
        @pl.when(carrier & (src <= z) & (z < TP - 1))
        def _():
            ag_copy(p, src, ch, ag_up, up).start()

        @pl.when(carrier & (src >= z) & (z > 0))
        def _():
            ag_copy(p, src, ch, ag_dn, down).start()

        @pl.when(carrier)
        def _():
            ag_copy(p, src, ch, ag_pt, {"ctx": partner}).start()

    @pl.when(jnp.logical_not(carrier))
    def _():
        for ch in range(HOPS):
            x_copy(ch).start()
        meta_copy(far).start()
        meta_copy(CTX - 1 - c).start()

    @pl.when(carrier)
    def _():
        meta_copy(partner).start()

    ssq_ref[...] = jnp.zeros_like(ssq_ref)
    acc_ref[...] = jnp.zeros_like(acc_ref)
    r_iota = lax.broadcasted_iota(jnp.int32, (rows, rows), 0)
    c_iota = lax.broadcasted_iota(jnp.int32, (rows, rows), 1)
    diagonal = r_iota == c_iota

    def as_column(row):
        return jnp.sum(jnp.where(diagonal, row, 0.0), axis=1, keepdims=True)

    def prepare_gains():
        gains = ig_ref[...].reshape(1, model) * PRESCALE
        for i in range(TP * HALVES):
            gain_in[i] = gains[:, i * half : (i + 1) * half]

    def prepare_trig(p, carry):
        @pl.when(jnp.logical_not(carrier & (side == p)))
        def _():
            pltpu.make_async_copy(meta_mine, meta_ref.at[p], meta_recv.at[p]).wait()

        lane = lax.broadcasted_iota(jnp.int32, (rows, hd), 1)
        place = jnp.where(lane < hd // 2, lane, lane - hd // 2).astype(F32)
        angles = as_column(meta_ref[p, 0:1].astype(F32)) * jnp.exp(
            place * (-2.0 * math.log(10000.0) / hd)
        )
        cos_ref[p] = jnp.cos(angles)
        sines = jnp.sin(angles)
        sin_ref[p] = jnp.where(lane < hd // 2, -sines, sines)
        return carry

    def arrive(p, i, g):
        src = source(i)
        for j in range(per_half):
            ch = g * per_half + j
            local = carrier & (i == 0) & ((side == p) if p == 0 else True)

            @pl.when(jnp.logical_not(local))
            def _():
                ag_copy(p, src, ch, ag_pt, {"ctx": partner}).wait_recv()

            @pl.when((p == 0) | (i > 0))
            def _():
                forward(p, src, ch)

    def begin_second():
        for ch in range(HOPS):
            @pl.when(carrier & (side == 0))
            def _():
                ag_copy(1, z, ch, ag_pt, {"ctx": partner}).wait_recv()

            forward(1, z, ch)

    kv_width = 2 * kv_cols

    def project(p, i, g):
        src = source(i)
        spot = src * HALVES + g
        x_t = xbuf[p, src, pl.ds(pl.multiple_of(g * half, 32), half)].astype(F32)
        ssq_ref[p] += jnp.sum(x_t * x_t, axis=0, keepdims=True)
        xg_ref[...] = (x_t.T * gain_in[spot]).astype(BF16)
        last = (i == TP - 1) & (g == HALVES - 1)
        if p == 0:
            loaded = w_ref.at[half_span(spot)]
            pltpu.make_async_copy(loaded, loaded, w_sem.at[spot]).wait()

        @pl.when(jnp.logical_not(last))
        def _():
            acc_ref[p] += jnp.dot(xg_ref[...], w_ref[half_span(spot)], preferred_element_type=F32)

        @pl.when(last)
        def _():
            acc_ref[p, :, 0:kv_width] += jnp.dot(
                xg_ref[...], w_ref[half_span(spot), 0:kv_width], preferred_element_type=F32
            )

    def first_gather(step, carry):
        i = step // HALVES
        g = step % HALVES
        arrive(0, i, g)

        @pl.when((g == HALVES - 1) & (i == jnp.where(edge, 1, TP - 1)))
        def _():
            begin_second()

        @pl.when(step == 0)
        def _():
            prepare_gains()

        project(0, i, g)

        @pl.when(step == 1)
        def _():
            lax.fori_loop(0, PHASES, prepare_trig, 0)

        return carry

    lax.fori_loop(0, TP * HALVES, first_gather, 0)

    def kv_copy(p, h):
        here = kvbuf.at[2 * p + side, h]
        return pltpu.make_async_remote_copy(
            src_ref=here,
            dst_ref=here,
            send_sem=kv_send.at[p],
            recv_sem=kv_recv.at[2 * p + side, h],
            device_id={"ctx": far},
            device_id_type=MESH,
        )

    def kv_arrived(block, h):
        there = kvbuf.at[block, h]
        pltpu.make_async_copy(there, there, kv_recv.at[block, h]).wait()

    def attn_copy(p, h):
        here = attn_ref.at[p, kv_heads * core + h]
        return pltpu.make_async_remote_copy(
            src_ref=here,
            dst_ref=here,
            send_sem=at_send.at[p],
            recv_sem=at_recv.at[p],
            device_id={"ctx": partner},
            device_id_type=MESH,
        )

    def attn_wait(p, owner, sem):
        both = attn_ref.at[p, pl.ds(kv_heads * owner, kv_heads)]
        pltpu.make_async_copy(both, both, sem.at[p]).wait()

    def attend(p, ready, late):
        own_block = ready[0]
        first = as_column(meta_ref[p, 1:2].astype(F32)).astype(jnp.int32)

        def hidden(block):
            visible = block * rows + c_iota >= first
            if block == own_block:
                visible = visible & (c_iota <= r_iota)
            bias = jnp.where(visible, 0.0, -1e30)
            return jnp.concatenate([bias, bias], axis=0)

        def score(h, block, bias):
            return bias + lax.dot_general(
                q_ref[h], kvbuf[block, h, 0], (((1,), (1,)), ((), ())), preferred_element_type=F32
            )

        def mix(h, weights, blocks):
            weights = weights.astype(BF16)
            return sum(
                jnp.dot(
                    weights[:, j * rows : (j + 1) * rows], kvbuf[block, h, 1],
                    preferred_element_type=F32,
                )
                for j, block in enumerate(blocks)
            )

        biases = [hidden(block) for block in ready]
        states = []
        for h in range(kv_heads):
            s = jnp.concatenate([score(h, b, bias) for b, bias in zip(ready, biases)], axis=1)
            top = jnp.max(s, axis=1, keepdims=True)
            weights = jnp.exp(s - top)
            states.append((top, jnp.sum(weights, axis=1, keepdims=True), mix(h, weights, ready)))
        late_bias = None if late is None else hidden(late)
        for h in range(kv_heads):
            top, total, mixed = states[h]
            if late is not None:
                kv_arrived(late, h)
                s = score(h, late, late_bias)
                higher = jnp.maximum(top, jnp.max(s, axis=1, keepdims=True))
                fade = jnp.exp(top - higher)
                weights = jnp.exp(s - higher)
                total = total * fade + jnp.sum(weights, axis=1, keepdims=True)
                mixed = mixed * fade + mix(h, weights, [late])
            mixed = (mixed / total).astype(BF16)
            attn_ref[p, kv_heads * core + h] = jnp.concatenate([mixed[:rows], mixed[rows:]], axis=1)
            attn_copy(p, h).start()

    def attention(p):
        inv = lax.rsqrt(as_column(ssq_ref[p]) * (1.0 / model) + EPSILON) * (1.0 / PRESCALE)

        def normed_rotated(raw, gain_vec):
            raw = raw * inv
            scaled = raw * lax.rsqrt(jnp.mean(raw * raw, axis=1, keepdims=True) + EPSILON) * gain_vec
            return scaled * cos_ref[p] + pltpu.roll(scaled, hd // 2, 1) * sin_ref[p]

        block = 2 * p + side
        for h in range(kv_heads):
            k_cols = slice(h * hd, (h + 1) * hd)
            v_cols = slice(kv_cols + h * hd, kv_cols + (h + 1) * hd)
            kvbuf[block, h, 0] = normed_rotated(acc_ref[p, :, k_cols], kg_ref[...]).astype(BF16)
            kvbuf[block, h, 1] = (acc_ref[p, :, v_cols] * inv).astype(BF16)

            @pl.when((p == 0) | (side == 0))
            def _():
                kv_copy(p, h).start()

        spot = source(TP - 1) * HALVES + HALVES - 1
        acc_ref[p, :, kv_width:] += jnp.dot(
            xg_ref[...], w_ref[half_span(spot), kv_width:], preferred_element_type=F32
        )
        for h in range(q_heads):
            cols = slice(kv_width + h * hd, kv_width + (h + 1) * hd)
            q_ref[h // 2, (h % 2) * rows : (h % 2 + 1) * rows] = (
                normed_rotated(acc_ref[p, :, cols], qg_ref[...]) * (D // H) ** (-0.5)
            ).astype(BF16)

        @pl.when(side == 0)
        def _():
            if p == 1:
                for h in range(kv_heads):
                    kv_arrived(1, h)
            attend(p, [2 * p, *range(2 * p)], None)

        @pl.when(side == 1)
        def _():
            attend(p, [2 * p + 1, *range(2 * p)], 2 * p)

    def rs_copy(p, dest, ch, buf, recv, target):
        start = pl.multiple_of(turn_of(dest) * extra + ch * chunk, 16)
        return pltpu.make_async_remote_copy(
            src_ref=part.at[p, dest, pl.ds(start, chunk)],
            dst_ref=buf.at[p, dest, pl.ds(pl.multiple_of(ch * chunk, 16), chunk)],
            send_sem=rs_send.at[p, dest],
            recv_sem=recv.at[p, dest, ch],
            device_id=target,
            device_id_type=MESH,
        )

    def rs_up(p, dest, ch):
        return rs_copy(p, dest, ch, rup, rs_up_recv, up)

    def rs_dn(p, dest, ch):
        return rs_copy(p, dest, ch, rdn, rs_dn_recv, down)

    def output_terms(p):
        attn_wait(p, 1 - core, at_recv)

        def out_step(i, carry):
            dest = out_order(i)
            if p == 0:
                wo_copy(dest).wait()
            mixed = jnp.concatenate([attn_ref[p, j] for j in range(2 * kv_heads)], axis=1)
            part[p, dest] = jnp.dot(mixed, wo_ref[dest], preferred_element_type=F32).T.astype(BF16)

            for ch in range(RS_CHUNKS):
                @pl.when((z == 0) & (dest > 0))
                def _():
                    rs_up(p, dest, ch).start()

                @pl.when((z == TP - 1) & (dest < TP - 1))
                def _():
                    rs_dn(p, dest, ch).start()

            return carry

        lax.fori_loop(0, TP, out_step, 0)
        own[p] = part[p, z, pl.ds(pl.multiple_of(turn_of(z) * extra, 16), half)].astype(F32)

    def fin_copy(p, ch):
        span = pl.ds(pl.multiple_of(ch * chunk, 16), chunk)
        return pltpu.make_async_remote_copy(
            src_ref=fin_mine.at[p, span],
            dst_ref=fin_ref.at[core, span],
            send_sem=fin_send.at[p],
            recv_sem=fin_recv.at[core, ch],
            device_id={"ctx": 2 * p + side},
            device_id_type=MESH,
        )

    def sq_copy(p, d):
        return pltpu.make_async_remote_copy(
            src_ref=sq_mine.at[p],
            dst_ref=sq_all.at[HALVES * z + core],
            send_sem=sq_send.at[p],
            recv_sem=sq_recv,
            device_id={"ctx": 2 * p + side, "tp": lax.rem(z + d, TP)},
            device_id_type=MESH,
        )

    def sum_terms(p, begin, end):
        mine = c == 2 * p + side

        def sum_step(k, carry):
            from_low = z + TP - 1 - k
            from_high = z + k - (TP - 1)
            for ch in range(RS_CHUNKS):
                span = slice(ch * chunk, (ch + 1) * chunk)
                for dest, has, buf, copy in (
                    (from_low, (z > 0) & (from_low < TP), rup, rs_up),
                    (from_high, (z < TP - 1) & (from_high >= 0), rdn, rs_dn),
                ):
                    @pl.when(has)
                    def _():
                        copy(p, dest, ch).wait_recv()

                        @pl.when(dest != z)
                        def _():
                            start = pl.multiple_of(turn_of(dest) * extra + ch * chunk, 16)
                            there = pl.ds(start, chunk)
                            part[p, dest, there] = (
                                part[p, dest, there].astype(F32) + buf[p, dest, span].astype(F32)
                            ).astype(BF16)
                            copy(p, dest, ch).start()

                        @pl.when(dest == z)
                        def _():
                            own[p, span] += buf[p, dest, span].astype(F32)

                @pl.when(k == TP - 1)
                def _():
                    rounded = own[p, span].astype(BF16)

                    @pl.when(mine)
                    def _():
                        fin_ref[core, span] = rounded

                    @pl.when(jnp.logical_not(mine))
                    def _():
                        fin_mine[p, span] = rounded
                        fin_copy(p, ch).start()

            return carry

        lax.fori_loop(begin, end, sum_step, 0)

    def send_squares(p):
        mine = c == 2 * p + side
        as_row = jnp.sum(own[p] * own[p], axis=0, keepdims=True)
        sq_mine[p] = jnp.broadcast_to(as_row, sq_mine.shape[1:])

        @pl.when(mine)
        def _():
            sq_all[HALVES * z + core] = sq_mine[p]

        @pl.when(jnp.logical_not(mine))
        def _():
            sq_copy(p, 0).start()

        for d in range(1, TP):
            sq_copy(p, d).start()

    attention(0)
    for g in range(HALVES):
        arrive(1, 1, g)
    output_terms(0)

    def second_gather(step, carry):
        i = step // HALVES
        g = step % HALVES

        @pl.when(i != 1)
        def _():
            arrive(1, i, g)

        project(1, i, g)
        return carry

    lax.fori_loop(0, TP * HALVES, second_gather, 0)
    sum_terms(0, 1, TP - 1)
    attention(1)
    output_terms(1)
    sum_terms(0, TP - 1, TP)
    send_squares(0)
    post_gains = pg_ref[...].reshape(1, model)
    for i in range(TP):
        gain_post[i] = post_gains[:, i * feat : (i + 1) * feat]
    gain_out[...] = jnp.broadcast_to(gain_post[z], (rows, feat)).T
    sum_terms(1, 1, TP - 1)

    def landed(whole, sem):
        pltpu.make_async_copy(whole, whole, sem).wait()

    @pl.when(jnp.logical_not(carrier))
    def _():
        landed(tok_ref, x_send)
        landed(meta_ref, meta_send)

    @pl.when(carrier)
    def _():
        landed(meta_mine, meta_send)

    for p in range(PHASES):
        @pl.when(carrier)
        def _():
            def settle(i, carry):
                @pl.when((z < TP - 1) & (i <= z))
                def _():
                    landed(xbuf.at[p, i], ag_up.at[p, i])

                @pl.when((z > 0) & (i >= z))
                def _():
                    landed(xbuf.at[p, i], ag_dn.at[p, i])

                landed(xbuf.at[p, i], ag_pt.at[p, i])
                return carry

            lax.fori_loop(0, TP, settle, 0)

        @pl.when((p == 0) | (side == 0))
        def _():
            landed(kvbuf.at[2 * p + side], kv_send.at[p])

        attn_wait(p, core, at_send)

    sum_terms(1, TP - 1, TP)
    send_squares(1)

    source_side = c % 2
    count = TP * HALVES - 1

    @pl.when(carrier)
    def _():
        landed(sq_all.at[0:count], sq_recv)

    @pl.when(jnp.logical_not(carrier))
    def _():
        landed(sq_all, sq_recv)

    total = jnp.sum(sq_all[...], axis=0)[0:1]
    inv_post = lax.rsqrt(total * (1.0 / model) + EPSILON)
    for kk in range(HALVES):
        for ch in range(RS_CHUNKS):
            @pl.when(2 * source_side + kk != c)
            def _():
                landed(fin_ref.at[kk, slice(ch * chunk, (ch + 1) * chunk)], fin_recv.at[kk, ch])

            span = slice(kk * half + ch * chunk, kk * half + (ch + 1) * chunk)
            summed = fin_ref[kk, ch * chunk : (ch + 1) * chunk].astype(F32)
            out_ref[span] = (
                tok_ref[span].astype(F32) + summed * inv_post * gain_out[span]
            ).astype(BF16)

    for p in range(PHASES):
        def settle(i, carry):
            @pl.when(i != z)
            def _():
                landed(rup.at[p, i], rs_send.at[p, i])

            return carry

        lax.fori_loop(0, TP, settle, 0)

        @pl.when(c != 2 * p + side)
        def _():
            landed(fin_mine.at[p], fin_send.at[p])
            landed(sq_all.at[0:TP], sq_send.at[p])

        @pl.when(c == 2 * p + side)
        def _():
            landed(sq_all.at[0 : TP - 1], sq_send.at[p])


def per_device_fused(
    tokens, positions, first_key, input_gain, query_weight, kv_weight, query_gain, key_gain,
    out_weight, post_gain,
):
    feat, rows = tokens.shape[1], tokens.shape[0]
    half = feat // HALVES
    hd = query_gain.shape[0]
    model = query_weight.shape[0]
    q_cols = query_weight.shape[1] // 2
    kv_cols = kv_weight.shape[2] // 2
    kv_heads = kv_cols // hd
    wide = half + 128 - half % 128
    vmem = pl.BlockSpec(memory_space=pltpu.VMEM)
    anywhere = pl.BlockSpec(memory_space=pl.ANY)
    dma = pltpu.SemaphoreType.DMA
    return pl.pallas_call(
        fused_kernel,
        out_shape=jax.ShapeDtypeStruct((feat, rows), BF16),
        in_specs=[vmem] * 7 + [anywhere] * 3,
        out_specs=vmem,
        scratch_shapes=[
            pltpu.VMEM((PHASES, TP, feat, rows), BF16),
            pltpu.VMEM((rows, half), BF16),
            pltpu.VMEM((model, q_cols + 2 * kv_cols), BF16),
            pltpu.VMEM((TP, 2 * q_cols, wide), BF16),
            pltpu.VMEM((TP * HALVES, 1, half), F32),
            pltpu.VMEM((TP, 1, feat), F32),
            pltpu.VMEM((feat, rows), F32),
            pltpu.VMEM((PHASES, 1, rows), F32),
            pltpu.VMEM((PHASES, rows, q_cols + 2 * kv_cols), F32),
            pltpu.VMEM((PHASES, rows, hd), F32),
            pltpu.VMEM((PHASES, rows, hd), F32),
            pltpu.VMEM((8, rows), jnp.int32),
            pltpu.VMEM((PHASES, 8, rows), jnp.int32),
            pltpu.VMEM((CTX, kv_heads, 2, rows, hd), BF16),
            pltpu.VMEM((kv_heads, 2 * rows, hd), BF16),
            pltpu.VMEM((PHASES, 2 * kv_heads, rows, 2 * hd), BF16),
            pltpu.VMEM((PHASES, TP, wide, rows), BF16),
            pltpu.VMEM((PHASES, TP, half, rows), BF16),
            pltpu.VMEM((PHASES, TP, half, rows), BF16),
            pltpu.VMEM((PHASES, half, rows), F32),
            pltpu.VMEM((PHASES, half, rows), BF16),
            pltpu.VMEM((HALVES, half, rows), BF16),
            pltpu.VMEM((PHASES, 8, rows), F32),
            pltpu.VMEM((TP * HALVES, 8, rows), F32),
            dma((TP * HALVES,)),
            dma((TP,)),
            dma,
            dma((PHASES, TP)),
            dma((PHASES, TP)),
            dma((PHASES, TP)),
            dma((PHASES, TP, HOPS)),
            dma,
            dma((PHASES,)),
            dma((PHASES,)),
            dma((CTX, kv_heads)),
            dma((PHASES,)),
            dma((PHASES,)),
            dma((PHASES, TP)),
            dma((PHASES, TP, RS_CHUNKS)),
            dma((PHASES, TP, RS_CHUNKS)),
            dma((PHASES,)),
            dma((HALVES, RS_CHUNKS)),
            dma((PHASES,)),
            dma,
        ],
        compiler_params=pltpu.CompilerParams(
            collective_id=0, has_side_effects=True, vmem_limit_bytes=60 * 1024 * 1024
        ),
    )(
        tokens.T,
        positions.reshape(1, rows),
        first_key.reshape(1, rows),
        input_gain,
        query_gain.reshape(1, hd),
        key_gain.reshape(1, hd),
        post_gain,
        query_weight,
        kv_weight,
        out_weight,
    ).T


def solution(mesh):
    fused = mesh.shape["tp"] == TP and mesh.shape["ctx"] == CTX
    return jax.shard_map(
        per_device_fused if fused else per_device,
        mesh=mesh,
        in_specs=(
            P(("group", "ctx"), "tp"),
            P(("group", "ctx")),
            P(("group", "ctx")),
            P(),
            P(None, "tp"),
            P(None, None, "tp"),
            P(),
            P(),
            P("tp", None),
            P(),
        ),
        out_specs=P(("group", "ctx"), "tp"),
        check_vma=False,
    )
```

```python
import math

import jax
import jax.numpy as jnp
from jax import lax
from jax.experimental import pallas as pl
from jax.experimental.pallas import tpu as pltpu
from jax.sharding import PartitionSpec as P

D = 5376
H = 32
WINDOW = 1024


EPSILON = 1e-06


def from_partner(array, axis, distance):
    return lax.ppermute(array, axis, [(i, i ^ 1 << distance) for i in range(lax.axis_size(axis))])


def passed_along(block, axis, distance):
    devices = range(lax.axis_size(axis))
    route = [(i - distance, i) for i in devices if i - distance in devices]
    return lax.ppermute(block, axis, route)


def rms_norm(values, gain_vec):
    return (
        values * lax.rsqrt(jnp.mean(values * values, axis=-1, keepdims=True) + EPSILON) * gain_vec
    )


def rotate(values, positions_in):
    half_dim = values.shape[-1] // 2
    frequency = jnp.exp(
        jnp.arange(half_dim, dtype=jnp.float32) * (-2.0 * math.log(10000.0) / values.shape[-1])
    )
    angles = positions_in.astype(jnp.float32)[:, None] * frequency[None, :]
    cosines = jnp.cos(angles)[:, None, :]
    sine_part = jnp.sin(angles)[:, None, :]
    lower_half = values[..., :half_dim]
    upper_half = values[..., half_dim:]
    return jnp.concatenate(
        [
            lower_half * cosines - upper_half * sine_part,
            upper_half * cosines + lower_half * sine_part,
        ],
        axis=-1,
    )


def per_device(
    tokens,
    positions,
    first_key,
    input_gain,
    query_weight,
    kv_weight,
    query_gain,
    key_gain,
    out_weight,
    post_gain,
):
    tok_rows = tokens.shape[0]
    feat_dev = tokens.shape[1]
    head_dim = query_gain.shape[0]
    heads_dev = query_weight.shape[1] // head_dim
    tp_index = lax.axis_index("tp")
    ctx_index = lax.axis_index("ctx")
    ctx_count = lax.axis_size("ctx")
    local_x = tokens.astype(jnp.float32)
    kv_full = kv_weight
    if heads_dev == 1:
        partner = from_partner(kv_weight, "tp", 0)
        is_even = tp_index % 2 == 0
        kv_full = jnp.where(
            is_even,
            jnp.concatenate([kv_weight, partner], axis=2),
            jnp.concatenate([partner, kv_weight], axis=2),
        )
    gathered = lax.all_gather(tokens, "tp", axis=1, tiled=True).astype(jnp.float32)
    normed = rms_norm(gathered, input_gain).astype(jnp.bfloat16)
    query_raw = jnp.dot(normed, query_weight, preferred_element_type=jnp.float32)
    key_raw = jnp.dot(normed, kv_full[0], preferred_element_type=jnp.float32)
    value_raw = jnp.dot(normed, kv_full[1], preferred_element_type=jnp.float32)
    kv_heads = key_raw.shape[1] // head_dim
    group_size = heads_dev // kv_heads
    queries = (
        rotate(rms_norm(query_raw.reshape(tok_rows, heads_dev, head_dim), query_gain), positions)
        * (D // H) ** (-0.5)
    ).astype(jnp.bfloat16)
    keys = rotate(
        rms_norm(key_raw.reshape(tok_rows, kv_heads, head_dim), key_gain), positions
    ).astype(jnp.bfloat16)
    values_b = value_raw.reshape(tok_rows, kv_heads, head_dim).astype(jnp.bfloat16)
    kv_block = jnp.stack([keys, values_b])
    reach_blocks = min(ctx_count - 1, (WINDOW + tok_rows - 2) // tok_rows)
    received = []
    moving = kv_block
    for offset in range(reach_blocks):
        moving = passed_along(moving, "ctx", 1)
        received.append(moving)
    blocks = received[::-1] + [kv_block]
    keys_all = jnp.concatenate(blocks, axis=1)
    key_count = keys_all.shape[1]
    key_index = (ctx_index - reach_blocks) * tok_rows + jnp.arange(key_count, dtype=jnp.int32)
    query_index = ctx_index * tok_rows + jnp.arange(tok_rows, dtype=jnp.int32)
    visible = (key_index[None, :] >= first_key[:, None]) & (
        key_index[None, :] <= query_index[:, None]
    )
    grouped = queries.reshape(tok_rows, kv_heads, group_size, head_dim)
    scores = jnp.einsum("qkgd,tkd->kgqt", grouped, keys_all[0], preferred_element_type=jnp.float32)
    scores = jnp.where(visible[None, None], scores, -1e30)
    row_max = jnp.max(scores, axis=-1, keepdims=True)
    weights = jnp.exp(scores - row_max)
    denominator = jnp.sum(weights, axis=-1)
    mixed_out = jnp.einsum(
        "kgqt,tkd->qkgd",
        weights.astype(jnp.bfloat16),
        keys_all[1],
        preferred_element_type=jnp.float32,
    )
    mixed_out = mixed_out / jnp.transpose(denominator, (2, 0, 1))[..., None]
    attn = mixed_out.astype(jnp.bfloat16).reshape(tok_rows, heads_dev * head_dim)
    partial_value = jnp.dot(attn, out_weight, preferred_element_type=jnp.float32)
    summed = lax.psum(partial_value.astype(jnp.bfloat16), "tp").astype(jnp.float32)
    post_normed = rms_norm(summed, post_gain)
    own_cols = lax.dynamic_slice_in_dim(post_normed, tp_index * feat_dev, feat_dev, 1)
    return (local_x + own_cols).astype(jnp.bfloat16)


MESH = pl.DeviceIdType.MESH
F32 = jnp.float32
BF16 = jnp.bfloat16
TP = 4
CTX = 4
PHASES = 2
HALVES = 2
HOPS = 4
RS_CHUNKS = 2
PRESCALE = 2.0**-10


def fused_kernel(
    tok_ref, pos_ref, fk_ref, ig_ref, qg_ref, kg_ref, pg_ref, qw_hbm, kvw_hbm, ow_hbm, out_ref,
    xbuf, xg_ref, w_ref, wo_ref, gain_in, gain_post, gain_out, ssq_ref, acc_ref, cos_ref, sin_ref,
    meta_mine, meta_ref, kvbuf, q_ref, attn_ref, part, rup, rdn, own, fin_mine, fin_ref, sq_mine, sq_all,
    w_sem, wo_sem, x_send, ag_up, ag_dn, ag_pt, ag_recv, meta_send, meta_recv, kv_send, kv_recv,
    at_send, at_recv, rs_send, rs_up_recv, rs_dn_recv, fin_send, fin_recv, sq_send, sq_recv,
):
    feat, rows = tok_ref.shape
    half = feat // HALVES
    hop = feat // HOPS
    per_half = HOPS // HALVES
    chunk = half // RS_CHUNKS
    hd = qg_ref.shape[1]
    kv_heads = kvbuf.shape[1]
    kv_cols = kv_heads * hd
    q_cols = w_ref.shape[1] - 2 * kv_cols
    q_heads = q_cols // hd
    model = feat * TP
    z = lax.axis_index("tp")
    c = lax.axis_index("ctx")
    side = c // 2
    core = c % 2
    carrier = side == core
    partner = c + 1 - 2 * core
    far = lax.rem(c + 2, CTX)
    edge = (z == 0) | (z == TP - 1)
    up = {"tp": lax.rem(z + 1, TP)}
    down = {"tp": lax.rem(z + TP - 1, TP)}

    barrier = pltpu.get_barrier_semaphore()

    @pl.when(z < TP - 1)
    def _():
        pl.semaphore_signal(barrier, inc=1, device_id=up, device_id_type=MESH)

    @pl.when(z > 0)
    def _():
        pl.semaphore_signal(barrier, inc=1, device_id=down, device_id_type=MESH)

    for other in (far, partner, CTX - 1 - c):
        pl.semaphore_signal(barrier, inc=1, device_id={"ctx": other}, device_id_type=MESH)

    def half_span(spot):
        return pl.ds(pl.multiple_of(spot * half, 32), half)

    def weight_copies(spot):
        span = half_span(spot)
        kv_from = pl.ds(pl.multiple_of(core * kv_cols, 128), kv_cols)
        q_from = pl.ds(pl.multiple_of(core * q_cols, 128), q_cols)
        return (
            pltpu.make_async_copy(
                kvw_hbm.at[0, span, kv_from], w_ref.at[span, 0:kv_cols], w_sem.at[spot]
            ),
            pltpu.make_async_copy(
                kvw_hbm.at[1, span, kv_from], w_ref.at[span, kv_cols : 2 * kv_cols], w_sem.at[spot]
            ),
            pltpu.make_async_copy(
                qw_hbm.at[span, q_from], w_ref.at[span, 2 * kv_cols :], w_sem.at[spot]
            ),
        )

    def source(i):
        second = jnp.where(z % 2 == 0, 1, 2)
        third = jnp.where(z == 0, 2, jnp.where(z == 1, 0, jnp.where(z == 2, 3, 1)))
        fourth = jnp.where(z < TP // 2, TP - 1, 0)
        return jnp.where(i == 0, z, jnp.where(i == 1, second, jnp.where(i == 2, third, fourth)))

    extra = half % 128
    turns = 128 // extra
    wide = half + 128 - extra

    def turn_of(dest):
        return (dest * HALVES + core) % turns

    def wo_copy(dest):
        start = pl.multiple_of((dest * HALVES + core) * half - turn_of(dest) * extra, 128)
        return pltpu.make_async_copy(ow_hbm.at[:, pl.ds(start, wide)], wo_ref.at[dest], wo_sem.at[dest])

    def out_order(i):
        outer = TP - 1 - i
        inner = jnp.where(i == 0, 3, jnp.where(i == 1, 0, jnp.where(i == 2, 2, 1)))
        dest = jnp.where(edge, outer, inner)
        return jnp.where(z < TP // 2, dest, TP - 1 - dest)

    def begin_weights(i, carry):
        for g in range(HALVES):
            for copy in weight_copies(source(i) * HALVES + g):
                copy.start()
        return carry

    lax.fori_loop(0, TP, begin_weights, 0)

    def begin_wo(i, carry):
        wo_copy(out_order(i)).start()
        return carry

    lax.fori_loop(0, TP, begin_wo, 0)

    meta_mine[0:1] = pos_ref[...]
    meta_mine[1:2] = fk_ref[...]

    @pl.when(carrier)
    def _():
        xbuf[side, z] = tok_ref[...]
        meta_ref[side] = meta_mine[...]

    pl.semaphore_wait(barrier, jnp.where(edge, 4, 5))

    def hop_span(ch):
        return pl.ds(pl.multiple_of(ch * hop, 16), hop)

    def x_copy(ch):
        return pltpu.make_async_remote_copy(
            src_ref=tok_ref.at[hop_span(ch)],
            dst_ref=xbuf.at[side, z, hop_span(ch)],
            send_sem=x_send,
            recv_sem=ag_recv.at[side, z, ch],
            device_id={"ctx": far},
            device_id_type=MESH,
        )

    def ag_copy(p, src, ch, send, target):
        here = xbuf.at[p, src, hop_span(ch)]
        return pltpu.make_async_remote_copy(
            src_ref=here,
            dst_ref=here,
            send_sem=send.at[p, src],
            recv_sem=ag_recv.at[p, src, ch],
            device_id=target,
            device_id_type=MESH,
        )

    def meta_copy(target):
        return pltpu.make_async_remote_copy(
            src_ref=meta_mine,
            dst_ref=meta_ref.at[side],
            send_sem=meta_send,
            recv_sem=meta_recv.at[side],
            device_id={"ctx": target},
            device_id_type=MESH,
        )

    def forward(p, src, ch):
        @pl.when(carrier & (src <= z) & (z < TP - 1))
        def _():
            ag_copy(p, src, ch, ag_up, up).start()

        @pl.when(carrier & (src >= z) & (z > 0))
        def _():
            ag_copy(p, src, ch, ag_dn, down).start()

        @pl.when(carrier)
        def _():
            ag_copy(p, src, ch, ag_pt, {"ctx": partner}).start()

    @pl.when(jnp.logical_not(carrier))
    def _():
        for ch in range(HOPS):
            x_copy(ch).start()
        meta_copy(far).start()
        meta_copy(CTX - 1 - c).start()

    @pl.when(carrier)
    def _():
        meta_copy(partner).start()

    ssq_ref[...] = jnp.zeros_like(ssq_ref)
    acc_ref[...] = jnp.zeros_like(acc_ref)
    r_iota = lax.broadcasted_iota(jnp.int32, (rows, rows), 0)
    c_iota = lax.broadcasted_iota(jnp.int32, (rows, rows), 1)
    diagonal = r_iota == c_iota

    def as_column(row):
        return jnp.sum(jnp.where(diagonal, row, 0.0), axis=1, keepdims=True)

    def prepare_gains():
        gains = ig_ref[...].reshape(1, model) * PRESCALE
        for i in range(TP * HALVES):
            gain_in[i] = gains[:, i * half : (i + 1) * half]

    def prepare_trig(p):
        @pl.when(jnp.logical_not(carrier & (side == p)))
        def _():
            pltpu.make_async_copy(meta_mine, meta_ref.at[p], meta_recv.at[p]).wait()

        lane = lax.broadcasted_iota(jnp.int32, (rows, hd), 1)
        place = jnp.where(lane < hd // 2, lane, lane - hd // 2).astype(F32)
        angles = as_column(meta_ref[p, 0:1].astype(F32)) * jnp.exp(
            place * (-2.0 * math.log(10000.0) / hd)
        )
        cos_ref[p] = jnp.cos(angles)
        sines = jnp.sin(angles)
        sin_ref[p] = jnp.where(lane < hd // 2, -sines, sines)

    def arrive(p, i, g):
        src = source(i)
        for j in range(per_half):
            ch = g * per_half + j
            local = carrier & (i == 0) & ((side == p) if p == 0 else True)

            @pl.when(jnp.logical_not(local))
            def _():
                ag_copy(p, src, ch, ag_pt, {"ctx": partner}).wait_recv()

            @pl.when((p == 0) | (i > 0))
            def _():
                forward(p, src, ch)

    def begin_second():
        for ch in range(HOPS):
            @pl.when(carrier & (side == 0))
            def _():
                ag_copy(1, z, ch, ag_pt, {"ctx": partner}).wait_recv()

            forward(1, z, ch)

    kv_width = 2 * kv_cols

    def project(p, i, g):
        src = source(i)
        spot = src * HALVES + g
        x_t = xbuf[p, src, pl.ds(pl.multiple_of(g * half, 32), half)].astype(F32)
        ssq_ref[p] += jnp.sum(x_t * x_t, axis=0, keepdims=True)
        xg_ref[...] = (x_t.T * gain_in[spot]).astype(BF16)
        last = (i == TP - 1) & (g == HALVES - 1)
        if p == 0:
            loaded = w_ref.at[half_span(spot)]
            pltpu.make_async_copy(loaded, loaded, w_sem.at[spot]).wait()

        @pl.when(jnp.logical_not(last))
        def _():
            acc_ref[p] += jnp.dot(xg_ref[...], w_ref[half_span(spot)], preferred_element_type=F32)

        @pl.when(last)
        def _():
            acc_ref[p, :, 0:kv_width] += jnp.dot(
                xg_ref[...], w_ref[half_span(spot), 0:kv_width], preferred_element_type=F32
            )

    middle = jnp.logical_not(edge)
    lag = jnp.where(carrier & middle, 1, 0)

    def first_gather(step, carry):
        i = step // HALVES
        g = step % HALVES

        @pl.when(i < TP)
        def _():
            arrive(0, i, g)

        @pl.when((g == HALVES - 1) & (i == jnp.where(edge, 1, TP - 1)))
        def _():
            begin_second()

        @pl.when(step == 0)
        def _():
            prepare_gains()

        @pl.when((g == 0) & (i == jnp.where(lag == 0, 1, TP)))
        def _():
            prepare_trig(0)

        @pl.when((i >= lag) & (i < TP + lag))
        def _():
            project(0, i - lag, g)

        return carry

    lax.fori_loop(0, (TP + lag) * HALVES, first_gather, 0)

    def kv_copy(p, h):
        here = kvbuf.at[2 * p + side, h]
        return pltpu.make_async_remote_copy(
            src_ref=here,
            dst_ref=here,
            send_sem=kv_send.at[p],
            recv_sem=kv_recv.at[2 * p + side, h],
            device_id={"ctx": far},
            device_id_type=MESH,
        )

    def kv_arrived(block, h):
        there = kvbuf.at[block, h]
        pltpu.make_async_copy(there, there, kv_recv.at[block, h]).wait()

    def attn_copy(p, h):
        here = attn_ref.at[p, kv_heads * core + h]
        return pltpu.make_async_remote_copy(
            src_ref=here,
            dst_ref=here,
            send_sem=at_send.at[p],
            recv_sem=at_recv.at[p],
            device_id={"ctx": partner},
            device_id_type=MESH,
        )

    def attn_wait(p, owner, sem):
        both = attn_ref.at[p, pl.ds(kv_heads * owner, kv_heads)]
        pltpu.make_async_copy(both, both, sem.at[p]).wait()

    def attend(p, ready, late):
        own_block = ready[0]
        first = as_column(meta_ref[p, 1:2].astype(F32)).astype(jnp.int32)

        def hidden(block):
            visible = block * rows + c_iota >= first
            if block == own_block:
                visible = visible & (c_iota <= r_iota)
            bias = jnp.where(visible, 0.0, -1e30)
            return jnp.concatenate([bias, bias], axis=0)

        def score(h, block, bias):
            return bias + lax.dot_general(
                q_ref[h], kvbuf[block, h, 0], (((1,), (1,)), ((), ())), preferred_element_type=F32
            )

        def mix(h, weights, blocks):
            weights = weights.astype(BF16)
            return sum(
                jnp.dot(
                    weights[:, j * rows : (j + 1) * rows], kvbuf[block, h, 1],
                    preferred_element_type=F32,
                )
                for j, block in enumerate(blocks)
            )

        biases = [hidden(block) for block in ready]
        states = []
        for h in range(kv_heads):
            s = jnp.concatenate([score(h, b, bias) for b, bias in zip(ready, biases)], axis=1)
            top = jnp.max(s, axis=1, keepdims=True)
            weights = jnp.exp(s - top)
            states.append((top, jnp.sum(weights, axis=1, keepdims=True), mix(h, weights, ready)))
        late_bias = None if late is None else hidden(late)
        for h in range(kv_heads):
            top, total, mixed = states[h]
            if late is not None:
                kv_arrived(late, h)
                s = score(h, late, late_bias)
                higher = jnp.maximum(top, jnp.max(s, axis=1, keepdims=True))
                fade = jnp.exp(top - higher)
                weights = jnp.exp(s - higher)
                total = total * fade + jnp.sum(weights, axis=1, keepdims=True)
                mixed = mixed * fade + mix(h, weights, [late])
            mixed = (mixed / total).astype(BF16)
            attn_ref[p, kv_heads * core + h] = jnp.concatenate([mixed[:rows], mixed[rows:]], axis=1)
            attn_copy(p, h).start()

    def attention(p):
        inv = lax.rsqrt(as_column(ssq_ref[p]) * (1.0 / model) + EPSILON) * (1.0 / PRESCALE)

        def normed_rotated(raw, gain_vec):
            raw = raw * inv
            scaled = raw * lax.rsqrt(jnp.mean(raw * raw, axis=1, keepdims=True) + EPSILON) * gain_vec
            return scaled * cos_ref[p] + pltpu.roll(scaled, hd // 2, 1) * sin_ref[p]

        block = 2 * p + side
        for h in range(kv_heads):
            k_cols = slice(h * hd, (h + 1) * hd)
            v_cols = slice(kv_cols + h * hd, kv_cols + (h + 1) * hd)
            kvbuf[block, h, 0] = normed_rotated(acc_ref[p, :, k_cols], kg_ref[...]).astype(BF16)
            kvbuf[block, h, 1] = (acc_ref[p, :, v_cols] * inv).astype(BF16)

            @pl.when((p == 0) | (side == 0))
            def _():
                kv_copy(p, h).start()

        spot = source(TP - 1) * HALVES + HALVES - 1
        acc_ref[p, :, kv_width:] += jnp.dot(
            xg_ref[...], w_ref[half_span(spot), kv_width:], preferred_element_type=F32
        )
        for h in range(q_heads):
            cols = slice(kv_width + h * hd, kv_width + (h + 1) * hd)
            q_ref[h // 2, (h % 2) * rows : (h % 2 + 1) * rows] = (
                normed_rotated(acc_ref[p, :, cols], qg_ref[...]) * (D // H) ** (-0.5)
            ).astype(BF16)

        if p == 0:
            @pl.when(middle)
            def _():
                for g in range(HALVES):
                    arrive(1, 1, g)

        @pl.when(side == 0)
        def _():
            if p == 1:
                for h in range(kv_heads):
                    kv_arrived(1, h)
            attend(p, [2 * p, *range(2 * p)], None)

        @pl.when(side == 1)
        def _():
            attend(p, [2 * p + 1, *range(2 * p)], 2 * p)

    def rs_copy(p, dest, ch, buf, recv, target):
        start = pl.multiple_of(turn_of(dest) * extra + ch * chunk, 16)
        return pltpu.make_async_remote_copy(
            src_ref=part.at[p, dest, pl.ds(start, chunk)],
            dst_ref=buf.at[p, dest, pl.ds(pl.multiple_of(ch * chunk, 16), chunk)],
            send_sem=rs_send.at[p, dest],
            recv_sem=recv.at[p, dest, ch],
            device_id=target,
            device_id_type=MESH,
        )

    def rs_up(p, dest, ch):
        return rs_copy(p, dest, ch, rup, rs_up_recv, up)

    def rs_dn(p, dest, ch):
        return rs_copy(p, dest, ch, rdn, rs_dn_recv, down)

    def output_terms(p):
        attn_wait(p, 1 - core, at_recv)

        def out_step(i, carry):
            dest = out_order(i)
            if p == 0:
                wo_copy(dest).wait()
            mixed = jnp.concatenate([attn_ref[p, j] for j in range(2 * kv_heads)], axis=1)
            part[p, dest] = jnp.dot(mixed, wo_ref[dest], preferred_element_type=F32).T.astype(BF16)

            for ch in range(RS_CHUNKS):
                @pl.when((z == 0) & (dest > 0))
                def _():
                    rs_up(p, dest, ch).start()

                @pl.when((z == TP - 1) & (dest < TP - 1))
                def _():
                    rs_dn(p, dest, ch).start()

            return carry

        lax.fori_loop(0, TP, out_step, 0)
        own[p] = part[p, z, pl.ds(pl.multiple_of(turn_of(z) * extra, 16), half)].astype(F32)

    def fin_copy(p, ch):
        span = pl.ds(pl.multiple_of(ch * chunk, 16), chunk)
        return pltpu.make_async_remote_copy(
            src_ref=fin_mine.at[p, span],
            dst_ref=fin_ref.at[core, span],
            send_sem=fin_send.at[p],
            recv_sem=fin_recv.at[core, ch],
            device_id={"ctx": 2 * p + side},
            device_id_type=MESH,
        )

    def sq_copy(p, d):
        return pltpu.make_async_remote_copy(
            src_ref=sq_mine.at[p],
            dst_ref=sq_all.at[HALVES * z + core],
            send_sem=sq_send.at[p],
            recv_sem=sq_recv,
            device_id={"ctx": 2 * p + side, "tp": lax.rem(z + d, TP)},
            device_id_type=MESH,
        )

    def sum_terms(p, begin, end):
        mine = c == 2 * p + side

        def sum_step(k, carry):
            from_low = z + TP - 1 - k
            from_high = z + k - (TP - 1)
            for ch in range(RS_CHUNKS):
                span = slice(ch * chunk, (ch + 1) * chunk)
                for dest, has, buf, copy in (
                    (from_low, (z > 0) & (from_low < TP), rup, rs_up),
                    (from_high, (z < TP - 1) & (from_high >= 0), rdn, rs_dn),
                ):
                    @pl.when(has)
                    def _():
                        copy(p, dest, ch).wait_recv()

                        @pl.when(dest != z)
                        def _():
                            start = pl.multiple_of(turn_of(dest) * extra + ch * chunk, 16)
                            there = pl.ds(start, chunk)
                            part[p, dest, there] = (
                                part[p, dest, there].astype(F32) + buf[p, dest, span].astype(F32)
                            ).astype(BF16)
                            copy(p, dest, ch).start()

                        @pl.when(dest == z)
                        def _():
                            own[p, span] += buf[p, dest, span].astype(F32)

                @pl.when(k == TP - 1)
                def _():
                    rounded = own[p, span].astype(BF16)

                    @pl.when(mine)
                    def _():
                        fin_ref[core, span] = rounded

                    @pl.when(jnp.logical_not(mine))
                    def _():
                        fin_mine[p, span] = rounded
                        fin_copy(p, ch).start()

            return carry

        lax.fori_loop(begin, end, sum_step, 0)

    def send_squares(p):
        mine = c == 2 * p + side
        as_row = jnp.sum(own[p] * own[p], axis=0, keepdims=True)
        sq_mine[p] = jnp.broadcast_to(as_row, sq_mine.shape[1:])

        @pl.when(mine)
        def _():
            sq_all[HALVES * z + core] = sq_mine[p]

        @pl.when(jnp.logical_not(mine))
        def _():
            sq_copy(p, 0).start()

        for d in range(1, TP):
            sq_copy(p, d).start()

    attention(0)

    def early_arrive(step, carry):
        arrive(1, 2 + step // HALVES, step % HALVES)
        return carry

    @pl.when(middle)
    def _():
        lax.fori_loop(0, HALVES, early_arrive, 0)

    output_terms(0)

    @pl.when(middle)
    def _():
        lax.fori_loop(HALVES, 2 * HALVES, early_arrive, 0)

    prepare_trig(1)

    def second_gather(step, carry):
        i = step // HALVES
        g = step % HALVES

        @pl.when(edge | (i == 0))
        def _():
            arrive(1, i, g)

        project(1, i, g)
        return carry

    lax.fori_loop(0, TP * HALVES, second_gather, 0)
    sum_terms(0, 1, 2)
    attention(1)
    sum_terms(0, 2, TP - 1)
    output_terms(1)
    sum_terms(0, TP - 1, TP)
    send_squares(0)
    post_gains = pg_ref[...].reshape(1, model)
    for i in range(TP):
        gain_post[i] = post_gains[:, i * feat : (i + 1) * feat]
    gain_out[...] = jnp.broadcast_to(gain_post[z], (rows, feat)).T
    sum_terms(1, 1, TP - 1)

    def landed(whole, sem):
        pltpu.make_async_copy(whole, whole, sem).wait()

    @pl.when(jnp.logical_not(carrier))
    def _():
        landed(tok_ref, x_send)
        landed(meta_ref, meta_send)

    @pl.when(carrier)
    def _():
        landed(meta_mine, meta_send)

    for p in range(PHASES):
        @pl.when(carrier)
        def _():
            def settle(i, carry):
                @pl.when((z < TP - 1) & (i <= z))
                def _():
                    landed(xbuf.at[p, i], ag_up.at[p, i])

                @pl.when((z > 0) & (i >= z))
                def _():
                    landed(xbuf.at[p, i], ag_dn.at[p, i])

                landed(xbuf.at[p, i], ag_pt.at[p, i])
                return carry

            lax.fori_loop(0, TP, settle, 0)

        @pl.when((p == 0) | (side == 0))
        def _():
            landed(kvbuf.at[2 * p + side], kv_send.at[p])

        attn_wait(p, core, at_send)

    sum_terms(1, TP - 1, TP)
    send_squares(1)

    source_side = c % 2
    count = TP * HALVES - 1

    @pl.when(carrier)
    def _():
        landed(sq_all.at[0:count], sq_recv)

    @pl.when(jnp.logical_not(carrier))
    def _():
        landed(sq_all, sq_recv)

    total = jnp.sum(sq_all[...], axis=0)[0:1]
    inv_post = lax.rsqrt(total * (1.0 / model) + EPSILON)
    for kk in range(HALVES):
        for ch in range(RS_CHUNKS):
            @pl.when(2 * source_side + kk != c)
            def _():
                landed(fin_ref.at[kk, slice(ch * chunk, (ch + 1) * chunk)], fin_recv.at[kk, ch])

            span = slice(kk * half + ch * chunk, kk * half + (ch + 1) * chunk)
            summed = fin_ref[kk, ch * chunk : (ch + 1) * chunk].astype(F32)
            out_ref[span] = (
                tok_ref[span].astype(F32) + summed * inv_post * gain_out[span]
            ).astype(BF16)

    for p in range(PHASES):
        def settle(i, carry):
            @pl.when(i != z)
            def _():
                landed(rup.at[p, i], rs_send.at[p, i])

            return carry

        lax.fori_loop(0, TP, settle, 0)

        @pl.when(c != 2 * p + side)
        def _():
            landed(fin_mine.at[p], fin_send.at[p])
            landed(sq_all.at[0:TP], sq_send.at[p])

        @pl.when(c == 2 * p + side)
        def _():
            landed(sq_all.at[0 : TP - 1], sq_send.at[p])


def per_device_fused(
    tokens, positions, first_key, input_gain, query_weight, kv_weight, query_gain, key_gain,
    out_weight, post_gain,
):
    feat, rows = tokens.shape[1], tokens.shape[0]
    half = feat // HALVES
    hd = query_gain.shape[0]
    model = query_weight.shape[0]
    q_cols = query_weight.shape[1] // 2
    kv_cols = kv_weight.shape[2] // 2
    kv_heads = kv_cols // hd
    wide = half + 128 - half % 128
    vmem = pl.BlockSpec(memory_space=pltpu.VMEM)
    anywhere = pl.BlockSpec(memory_space=pl.ANY)
    dma = pltpu.SemaphoreType.DMA
    return pl.pallas_call(
        fused_kernel,
        out_shape=jax.ShapeDtypeStruct((feat, rows), BF16),
        in_specs=[vmem] * 7 + [anywhere] * 3,
        out_specs=vmem,
        scratch_shapes=[
            pltpu.VMEM((PHASES, TP, feat, rows), BF16),
            pltpu.VMEM((rows, half), BF16),
            pltpu.VMEM((model, q_cols + 2 * kv_cols), BF16),
            pltpu.VMEM((TP, 2 * q_cols, wide), BF16),
            pltpu.VMEM((TP * HALVES, 1, half), F32),
            pltpu.VMEM((TP, 1, feat), F32),
            pltpu.VMEM((feat, rows), F32),
            pltpu.VMEM((PHASES, 1, rows), F32),
            pltpu.VMEM((PHASES, rows, q_cols + 2 * kv_cols), F32),
            pltpu.VMEM((PHASES, rows, hd), F32),
            pltpu.VMEM((PHASES, rows, hd), F32),
            pltpu.VMEM((8, rows), jnp.int32),
            pltpu.VMEM((PHASES, 8, rows), jnp.int32),
            pltpu.VMEM((CTX, kv_heads, 2, rows, hd), BF16),
            pltpu.VMEM((kv_heads, 2 * rows, hd), BF16),
            pltpu.VMEM((PHASES, 2 * kv_heads, rows, 2 * hd), BF16),
            pltpu.VMEM((PHASES, TP, wide, rows), BF16),
            pltpu.VMEM((PHASES, TP, half, rows), BF16),
            pltpu.VMEM((PHASES, TP, half, rows), BF16),
            pltpu.VMEM((PHASES, half, rows), F32),
            pltpu.VMEM((PHASES, half, rows), BF16),
            pltpu.VMEM((HALVES, half, rows), BF16),
            pltpu.VMEM((PHASES, 8, rows), F32),
            pltpu.VMEM((TP * HALVES, 8, rows), F32),
            dma((TP * HALVES,)),
            dma((TP,)),
            dma,
            dma((PHASES, TP)),
            dma((PHASES, TP)),
            dma((PHASES, TP)),
            dma((PHASES, TP, HOPS)),
            dma,
            dma((PHASES,)),
            dma((PHASES,)),
            dma((CTX, kv_heads)),
            dma((PHASES,)),
            dma((PHASES,)),
            dma((PHASES, TP)),
            dma((PHASES, TP, RS_CHUNKS)),
            dma((PHASES, TP, RS_CHUNKS)),
            dma((PHASES,)),
            dma((HALVES, RS_CHUNKS)),
            dma((PHASES,)),
            dma,
        ],
        compiler_params=pltpu.CompilerParams(
            collective_id=0, has_side_effects=True, vmem_limit_bytes=60 * 1024 * 1024
        ),
    )(
        tokens.T,
        positions.reshape(1, rows),
        first_key.reshape(1, rows),
        input_gain,
        query_gain.reshape(1, hd),
        key_gain.reshape(1, hd),
        post_gain,
        query_weight,
        kv_weight,
        out_weight,
    ).T


def solution(mesh):
    fused = mesh.shape["tp"] == TP and mesh.shape["ctx"] == CTX
    return jax.shard_map(
        per_device_fused if fused else per_device,
        mesh=mesh,
        in_specs=(
            P(("group", "ctx"), "tp"),
            P(("group", "ctx")),
            P(("group", "ctx")),
            P(),
            P(None, "tp"),
            P(None, None, "tp"),
            P(),
            P(),
            P("tp", None),
            P(),
        ),
        out_specs=P(("group", "ctx"), "tp"),
        check_vma=False,
    )
```

```python
import math

import jax
import jax.numpy as jnp
from jax import lax
from jax.experimental import pallas as pl
from jax.experimental.pallas import tpu as pltpu
from jax.sharding import PartitionSpec as P

D = 5376
H = 32
WINDOW = 1024


EPSILON = 1e-06


def from_partner(array, axis, distance):
    return lax.ppermute(array, axis, [(i, i ^ 1 << distance) for i in range(lax.axis_size(axis))])


def passed_along(block, axis, distance):
    devices = range(lax.axis_size(axis))
    route = [(i - distance, i) for i in devices if i - distance in devices]
    return lax.ppermute(block, axis, route)


def rms_norm(values, gain_vec):
    return (
        values * lax.rsqrt(jnp.mean(values * values, axis=-1, keepdims=True) + EPSILON) * gain_vec
    )


def rotate(values, positions_in):
    half_dim = values.shape[-1] // 2
    frequency = jnp.exp(
        jnp.arange(half_dim, dtype=jnp.float32) * (-2.0 * math.log(10000.0) / values.shape[-1])
    )
    angles = positions_in.astype(jnp.float32)[:, None] * frequency[None, :]
    cosines = jnp.cos(angles)[:, None, :]
    sine_part = jnp.sin(angles)[:, None, :]
    lower_half = values[..., :half_dim]
    upper_half = values[..., half_dim:]
    return jnp.concatenate(
        [
            lower_half * cosines - upper_half * sine_part,
            upper_half * cosines + lower_half * sine_part,
        ],
        axis=-1,
    )


def per_device(
    tokens,
    positions,
    first_key,
    input_gain,
    query_weight,
    kv_weight,
    query_gain,
    key_gain,
    out_weight,
    post_gain,
):
    tok_rows = tokens.shape[0]
    feat_dev = tokens.shape[1]
    head_dim = query_gain.shape[0]
    heads_dev = query_weight.shape[1] // head_dim
    tp_index = lax.axis_index("tp")
    ctx_index = lax.axis_index("ctx")
    ctx_count = lax.axis_size("ctx")
    local_x = tokens.astype(jnp.float32)
    kv_full = kv_weight
    if heads_dev == 1:
        partner = from_partner(kv_weight, "tp", 0)
        is_even = tp_index % 2 == 0
        kv_full = jnp.where(
            is_even,
            jnp.concatenate([kv_weight, partner], axis=2),
            jnp.concatenate([partner, kv_weight], axis=2),
        )
    gathered = lax.all_gather(tokens, "tp", axis=1, tiled=True).astype(jnp.float32)
    normed = rms_norm(gathered, input_gain).astype(jnp.bfloat16)
    query_raw = jnp.dot(normed, query_weight, preferred_element_type=jnp.float32)
    key_raw = jnp.dot(normed, kv_full[0], preferred_element_type=jnp.float32)
    value_raw = jnp.dot(normed, kv_full[1], preferred_element_type=jnp.float32)
    kv_heads = key_raw.shape[1] // head_dim
    group_size = heads_dev // kv_heads
    queries = (
        rotate(rms_norm(query_raw.reshape(tok_rows, heads_dev, head_dim), query_gain), positions)
        * (D // H) ** (-0.5)
    ).astype(jnp.bfloat16)
    keys = rotate(
        rms_norm(key_raw.reshape(tok_rows, kv_heads, head_dim), key_gain), positions
    ).astype(jnp.bfloat16)
    values_b = value_raw.reshape(tok_rows, kv_heads, head_dim).astype(jnp.bfloat16)
    kv_block = jnp.stack([keys, values_b])
    reach_blocks = min(ctx_count - 1, (WINDOW + tok_rows - 2) // tok_rows)
    received = []
    moving = kv_block
    for offset in range(reach_blocks):
        moving = passed_along(moving, "ctx", 1)
        received.append(moving)
    blocks = received[::-1] + [kv_block]
    keys_all = jnp.concatenate(blocks, axis=1)
    key_count = keys_all.shape[1]
    key_index = (ctx_index - reach_blocks) * tok_rows + jnp.arange(key_count, dtype=jnp.int32)
    query_index = ctx_index * tok_rows + jnp.arange(tok_rows, dtype=jnp.int32)
    visible = (key_index[None, :] >= first_key[:, None]) & (
        key_index[None, :] <= query_index[:, None]
    )
    grouped = queries.reshape(tok_rows, kv_heads, group_size, head_dim)
    scores = jnp.einsum("qkgd,tkd->kgqt", grouped, keys_all[0], preferred_element_type=jnp.float32)
    scores = jnp.where(visible[None, None], scores, -1e30)
    row_max = jnp.max(scores, axis=-1, keepdims=True)
    weights = jnp.exp(scores - row_max)
    denominator = jnp.sum(weights, axis=-1)
    mixed_out = jnp.einsum(
        "kgqt,tkd->qkgd",
        weights.astype(jnp.bfloat16),
        keys_all[1],
        preferred_element_type=jnp.float32,
    )
    mixed_out = mixed_out / jnp.transpose(denominator, (2, 0, 1))[..., None]
    attn = mixed_out.astype(jnp.bfloat16).reshape(tok_rows, heads_dev * head_dim)
    partial_value = jnp.dot(attn, out_weight, preferred_element_type=jnp.float32)
    summed = lax.psum(partial_value.astype(jnp.bfloat16), "tp").astype(jnp.float32)
    post_normed = rms_norm(summed, post_gain)
    own_cols = lax.dynamic_slice_in_dim(post_normed, tp_index * feat_dev, feat_dev, 1)
    return (local_x + own_cols).astype(jnp.bfloat16)


MESH = pl.DeviceIdType.MESH
F32 = jnp.float32
BF16 = jnp.bfloat16
TP = 4
CTX = 4
PHASES = 2
HALVES = 2
HOPS = 4
RS_CHUNKS = 2
PRESCALE = 2.0**-10


def fused_kernel(
    tok_ref, pos_ref, fk_ref, ig_ref, qg_ref, kg_ref, pg_ref, qw_hbm, kvw_hbm, ow_hbm, out_ref,
    xbuf, xg_ref, w_ref, wo_ref, gain_in, gain_post, gain_out, ssq_ref, acc_ref, cos_ref, sin_ref,
    meta_mine, meta_ref, kvbuf, q_ref, attn_ref, part, rup, rdn, own, fin_mine, fin_ref, sq_mine, sq_all,
    w_sem, wo_sem, x_send, ag_up, ag_dn, ag_pt, ag_recv, meta_send, meta_recv, kv_send, kv_recv,
    at_send, at_recv, rs_send, rs_up_recv, rs_dn_recv, fin_send, fin_recv, sq_send, sq_recv,
):
    feat, rows = tok_ref.shape
    half = feat // HALVES
    hop = feat // HOPS
    per_half = HOPS // HALVES
    chunk = half // RS_CHUNKS
    hd = qg_ref.shape[1]
    kv_heads = kvbuf.shape[1]
    kv_cols = kv_heads * hd
    q_cols = w_ref.shape[1] - 2 * kv_cols
    q_heads = q_cols // hd
    model = feat * TP
    z = lax.axis_index("tp")
    c = lax.axis_index("ctx")
    side = c // 2
    core = c % 2
    carrier = side == core
    partner = c + 1 - 2 * core
    far = lax.rem(c + 2, CTX)
    edge = (z == 0) | (z == TP - 1)
    up = {"tp": lax.rem(z + 1, TP)}
    down = {"tp": lax.rem(z + TP - 1, TP)}

    barrier = pltpu.get_barrier_semaphore()

    @pl.when(z < TP - 1)
    def _():
        pl.semaphore_signal(barrier, inc=1, device_id=up, device_id_type=MESH)

    @pl.when(z > 0)
    def _():
        pl.semaphore_signal(barrier, inc=1, device_id=down, device_id_type=MESH)

    for other in (far, partner, CTX - 1 - c):
        pl.semaphore_signal(barrier, inc=1, device_id={"ctx": other}, device_id_type=MESH)

    def half_span(spot):
        return pl.ds(pl.multiple_of(spot * half, 32), half)

    def weight_copies(spot):
        span = half_span(spot)
        kv_from = pl.ds(pl.multiple_of(core * kv_cols, 128), kv_cols)
        q_from = pl.ds(pl.multiple_of(core * q_cols, 128), q_cols)
        return (
            pltpu.make_async_copy(
                kvw_hbm.at[0, span, kv_from], w_ref.at[span, 0:kv_cols], w_sem.at[spot]
            ),
            pltpu.make_async_copy(
                kvw_hbm.at[1, span, kv_from], w_ref.at[span, kv_cols : 2 * kv_cols], w_sem.at[spot]
            ),
            pltpu.make_async_copy(
                qw_hbm.at[span, q_from], w_ref.at[span, 2 * kv_cols :], w_sem.at[spot]
            ),
        )

    def source(i):
        second = jnp.where(z % 2 == 0, 1, 2)
        third = jnp.where(z == 0, 2, jnp.where(z == 1, 0, jnp.where(z == 2, 3, 1)))
        fourth = jnp.where(z < TP // 2, TP - 1, 0)
        return jnp.where(i == 0, z, jnp.where(i == 1, second, jnp.where(i == 2, third, fourth)))

    extra = half % 128
    turns = 128 // extra
    wide = half + 128 - extra

    def turn_of(dest):
        return (dest * HALVES + core) % turns

    def wo_copy(dest):
        start = pl.multiple_of((dest * HALVES + core) * half - turn_of(dest) * extra, 128)
        return pltpu.make_async_copy(ow_hbm.at[:, pl.ds(start, wide)], wo_ref.at[dest], wo_sem.at[dest])

    def out_order(i):
        outer = TP - 1 - i
        inner = jnp.where(i == 0, 3, jnp.where(i == 1, 0, jnp.where(i == 2, 2, 1)))
        dest = jnp.where(edge, outer, inner)
        return jnp.where(z < TP // 2, dest, TP - 1 - dest)

    def begin_weights(i, carry):
        for g in range(HALVES):
            for copy in weight_copies(source(i) * HALVES + g):
                copy.start()
        return carry

    lax.fori_loop(0, TP, begin_weights, 0)

    def begin_wo(i, carry):
        wo_copy(out_order(i)).start()
        return carry

    lax.fori_loop(0, TP, begin_wo, 0)

    meta_mine[0:1] = pos_ref[...]
    meta_mine[1:2] = fk_ref[...]

    @pl.when(carrier)
    def _():
        xbuf[side, z] = tok_ref[...]
        meta_ref[side] = meta_mine[...]

    pl.semaphore_wait(barrier, jnp.where(edge, 4, 5))

    def hop_span(ch):
        return pl.ds(pl.multiple_of(ch * hop, 16), hop)

    def x_copy(ch):
        return pltpu.make_async_remote_copy(
            src_ref=tok_ref.at[hop_span(ch)],
            dst_ref=xbuf.at[side, z, hop_span(ch)],
            send_sem=x_send,
            recv_sem=ag_recv.at[side, z, ch],
            device_id={"ctx": far},
            device_id_type=MESH,
        )

    def ag_copy(p, src, ch, send, target):
        here = xbuf.at[p, src, hop_span(ch)]
        return pltpu.make_async_remote_copy(
            src_ref=here,
            dst_ref=here,
            send_sem=send.at[p, src],
            recv_sem=ag_recv.at[p, src, ch],
            device_id=target,
            device_id_type=MESH,
        )

    def meta_copy(target):
        return pltpu.make_async_remote_copy(
            src_ref=meta_mine,
            dst_ref=meta_ref.at[side],
            send_sem=meta_send,
            recv_sem=meta_recv.at[side],
            device_id={"ctx": target},
            device_id_type=MESH,
        )

    def forward(p, src, ch):
        @pl.when(carrier & (src <= z) & (z < TP - 1))
        def _():
            ag_copy(p, src, ch, ag_up, up).start()

        @pl.when(carrier & (src >= z) & (z > 0))
        def _():
            ag_copy(p, src, ch, ag_dn, down).start()

        @pl.when(carrier)
        def _():
            ag_copy(p, src, ch, ag_pt, {"ctx": partner}).start()

    @pl.when(jnp.logical_not(carrier))
    def _():
        for ch in range(HOPS):
            x_copy(ch).start()
        meta_copy(far).start()
        meta_copy(CTX - 1 - c).start()

    @pl.when(carrier)
    def _():
        meta_copy(partner).start()

    ssq_ref[...] = jnp.zeros_like(ssq_ref)
    acc_ref[...] = jnp.zeros_like(acc_ref)
    r_iota = lax.broadcasted_iota(jnp.int32, (rows, rows), 0)
    c_iota = lax.broadcasted_iota(jnp.int32, (rows, rows), 1)
    diagonal = r_iota == c_iota

    def as_column(row):
        return jnp.sum(jnp.where(diagonal, row, 0.0), axis=1, keepdims=True)

    def prepare_gains():
        gains = ig_ref[...].reshape(1, model) * PRESCALE
        for i in range(TP * HALVES):
            gain_in[i] = gains[:, i * half : (i + 1) * half]

    def prepare_trig(p):
        @pl.when(jnp.logical_not(carrier & (side == p)))
        def _():
            pltpu.make_async_copy(meta_mine, meta_ref.at[p], meta_recv.at[p]).wait()

        lane = lax.broadcasted_iota(jnp.int32, (rows, hd), 1)
        place = jnp.where(lane < hd // 2, lane, lane - hd // 2).astype(F32)
        angles = as_column(meta_ref[p, 0:1].astype(F32)) * jnp.exp(
            place * (-2.0 * math.log(10000.0) / hd)
        )
        cos_ref[p] = jnp.cos(angles)
        sines = jnp.sin(angles)
        sin_ref[p] = jnp.where(lane < hd // 2, -sines, sines)

    def arrive_hop(p, i, ch):
        src = source(i)
        local = carrier & (i == 0) & ((side == p) if p == 0 else True)

        @pl.when(jnp.logical_not(local))
        def _():
            ag_copy(p, src, ch, ag_pt, {"ctx": partner}).wait_recv()

        @pl.when((p == 0) | (i > 0))
        def _():
            forward(p, src, ch)

    def arrive(p, i, g):
        for j in range(per_half):
            arrive_hop(p, i, g * per_half + j)

    def arrive_both(p, ch):
        arrive_hop(p, 1, ch)
        arrive_hop(p, 2, ch)

    def begin_second():
        for ch in range(HOPS):
            @pl.when(carrier & (side == 0))
            def _():
                ag_copy(1, z, ch, ag_pt, {"ctx": partner}).wait_recv()

            forward(1, z, ch)

    kv_width = 2 * kv_cols

    def project(p, i, g):
        src = source(i)
        spot = src * HALVES + g
        x_t = xbuf[p, src, pl.ds(pl.multiple_of(g * half, 32), half)].astype(F32)
        ssq_ref[p] += jnp.sum(x_t * x_t, axis=0, keepdims=True)
        xg_ref[...] = (x_t.T * gain_in[spot]).astype(BF16)
        last = (i == TP - 1) & (g == HALVES - 1)
        if p == 0:
            loaded = w_ref.at[half_span(spot)]
            pltpu.make_async_copy(loaded, loaded, w_sem.at[spot]).wait()

        @pl.when(jnp.logical_not(last))
        def _():
            acc_ref[p] += jnp.dot(xg_ref[...], w_ref[half_span(spot)], preferred_element_type=F32)

        @pl.when(last)
        def _():
            acc_ref[p, :, 0:kv_width] += jnp.dot(
                xg_ref[...], w_ref[half_span(spot), 0:kv_width], preferred_element_type=F32
            )

    middle = jnp.logical_not(edge)
    lag = jnp.where(middle, 1, 0)

    def first_gather(step, carry):
        i = step // HALVES
        g = step % HALVES

        @pl.when((edge & (i < TP)) | (middle & (i != 1) & (i < TP - 1)))
        def _():
            arrive(0, jnp.where(middle & (i == 2), TP - 1, i), g)

        @pl.when(middle & (i == 1))
        def _():
            for j in range(per_half):
                arrive_both(0, g * per_half + j)

        @pl.when((g == HALVES - 1) & (i == jnp.where(edge, 1, 2)))
        def _():
            begin_second()

        @pl.when(step == 0)
        def _():
            prepare_gains()

        @pl.when((g == 0) & (i == jnp.where(edge, 1, TP)))
        def _():
            prepare_trig(0)

        @pl.when((i >= lag) & (i < TP + lag))
        def _():
            project(0, i - lag, g)

        return carry

    lax.fori_loop(0, (TP + lag) * HALVES, first_gather, 0)

    def kv_copy(p, h):
        here = kvbuf.at[2 * p + side, h]
        return pltpu.make_async_remote_copy(
            src_ref=here,
            dst_ref=here,
            send_sem=kv_send.at[p],
            recv_sem=kv_recv.at[2 * p + side, h],
            device_id={"ctx": far},
            device_id_type=MESH,
        )

    def kv_arrived(block, h):
        there = kvbuf.at[block, h]
        pltpu.make_async_copy(there, there, kv_recv.at[block, h]).wait()

    def attn_copy(p, h):
        here = attn_ref.at[p, kv_heads * core + h]
        return pltpu.make_async_remote_copy(
            src_ref=here,
            dst_ref=here,
            send_sem=at_send.at[p],
            recv_sem=at_recv.at[p],
            device_id={"ctx": partner},
            device_id_type=MESH,
        )

    def attn_wait(p, owner, sem):
        both = attn_ref.at[p, pl.ds(kv_heads * owner, kv_heads)]
        pltpu.make_async_copy(both, both, sem.at[p]).wait()

    def attend(p, ready, late):
        own_block = ready[0]
        first = as_column(meta_ref[p, 1:2].astype(F32)).astype(jnp.int32)

        def hidden(block):
            visible = block * rows + c_iota >= first
            if block == own_block:
                visible = visible & (c_iota <= r_iota)
            bias = jnp.where(visible, 0.0, -1e30)
            return jnp.concatenate([bias, bias], axis=0)

        def score(h, block, bias):
            return bias + lax.dot_general(
                q_ref[h], kvbuf[block, h, 0], (((1,), (1,)), ((), ())), preferred_element_type=F32
            )

        def mix(h, weights, blocks):
            weights = weights.astype(BF16)
            return sum(
                jnp.dot(
                    weights[:, j * rows : (j + 1) * rows], kvbuf[block, h, 1],
                    preferred_element_type=F32,
                )
                for j, block in enumerate(blocks)
            )

        biases = [hidden(block) for block in ready]
        states = []
        for h in range(kv_heads):
            s = jnp.concatenate([score(h, b, bias) for b, bias in zip(ready, biases)], axis=1)
            top = jnp.max(s, axis=1, keepdims=True)
            weights = jnp.exp(s - top)
            states.append((top, jnp.sum(weights, axis=1, keepdims=True), mix(h, weights, ready)))
        late_bias = None if late is None else hidden(late)
        for h in range(kv_heads):
            top, total, mixed = states[h]
            if late is not None:
                kv_arrived(late, h)
                s = score(h, late, late_bias)
                higher = jnp.maximum(top, jnp.max(s, axis=1, keepdims=True))
                fade = jnp.exp(top - higher)
                weights = jnp.exp(s - higher)
                total = total * fade + jnp.sum(weights, axis=1, keepdims=True)
                mixed = mixed * fade + mix(h, weights, [late])
            mixed = (mixed / total).astype(BF16)
            attn_ref[p, kv_heads * core + h] = jnp.concatenate([mixed[:rows], mixed[rows:]], axis=1)
            attn_copy(p, h).start()

    def attention(p):
        inv = lax.rsqrt(as_column(ssq_ref[p]) * (1.0 / model) + EPSILON) * (1.0 / PRESCALE)

        def normed_rotated(raw, gain_vec):
            raw = raw * inv
            scaled = raw * lax.rsqrt(jnp.mean(raw * raw, axis=1, keepdims=True) + EPSILON) * gain_vec
            return scaled * cos_ref[p] + pltpu.roll(scaled, hd // 2, 1) * sin_ref[p]

        block = 2 * p + side
        for h in range(kv_heads):
            k_cols = slice(h * hd, (h + 1) * hd)
            v_cols = slice(kv_cols + h * hd, kv_cols + (h + 1) * hd)
            kvbuf[block, h, 0] = normed_rotated(acc_ref[p, :, k_cols], kg_ref[...]).astype(BF16)
            kvbuf[block, h, 1] = (acc_ref[p, :, v_cols] * inv).astype(BF16)

            @pl.when((p == 0) | (side == 0))
            def _():
                kv_copy(p, h).start()

        spot = source(TP - 1) * HALVES + HALVES - 1
        acc_ref[p, :, kv_width:] += jnp.dot(
            xg_ref[...], w_ref[half_span(spot), kv_width:], preferred_element_type=F32
        )
        for h in range(q_heads):
            cols = slice(kv_width + h * hd, kv_width + (h + 1) * hd)
            q_ref[h // 2, (h % 2) * rows : (h % 2 + 1) * rows] = (
                normed_rotated(acc_ref[p, :, cols], qg_ref[...]) * (D // H) ** (-0.5)
            ).astype(BF16)

        if p == 0:
            @pl.when(middle)
            def _():
                for ch in range(HOPS):
                    arrive_both(1, ch)

        @pl.when(side == 0)
        def _():
            if p == 1:
                for h in range(kv_heads):
                    kv_arrived(1, h)
            attend(p, [2 * p, *range(2 * p)], None)

        @pl.when(side == 1)
        def _():
            attend(p, [2 * p + 1, *range(2 * p)], 2 * p)

    def rs_copy(p, dest, ch, buf, recv, target):
        start = pl.multiple_of(turn_of(dest) * extra + ch * chunk, 16)
        return pltpu.make_async_remote_copy(
            src_ref=part.at[p, dest, pl.ds(start, chunk)],
            dst_ref=buf.at[p, dest, pl.ds(pl.multiple_of(ch * chunk, 16), chunk)],
            send_sem=rs_send.at[p, dest],
            recv_sem=recv.at[p, dest, ch],
            device_id=target,
            device_id_type=MESH,
        )

    def rs_up(p, dest, ch):
        return rs_copy(p, dest, ch, rup, rs_up_recv, up)

    def rs_dn(p, dest, ch):
        return rs_copy(p, dest, ch, rdn, rs_dn_recv, down)

    def output_terms(p):
        attn_wait(p, 1 - core, at_recv)

        def out_step(i, carry):
            dest = out_order(i)
            if p == 0:
                wo_copy(dest).wait()
            mixed = jnp.concatenate([attn_ref[p, j] for j in range(2 * kv_heads)], axis=1)
            part[p, dest] = jnp.dot(mixed, wo_ref[dest], preferred_element_type=F32).T.astype(BF16)

            for ch in range(RS_CHUNKS):
                @pl.when((z == 0) & (dest > 0))
                def _():
                    rs_up(p, dest, ch).start()

                @pl.when((z == TP - 1) & (dest < TP - 1))
                def _():
                    rs_dn(p, dest, ch).start()

            return carry

        lax.fori_loop(0, TP, out_step, 0)
        own[p] = part[p, z, pl.ds(pl.multiple_of(turn_of(z) * extra, 16), half)].astype(F32)

    def fin_copy(p, ch):
        span = pl.ds(pl.multiple_of(ch * chunk, 16), chunk)
        return pltpu.make_async_remote_copy(
            src_ref=fin_mine.at[p, span],
            dst_ref=fin_ref.at[core, span],
            send_sem=fin_send.at[p],
            recv_sem=fin_recv.at[core, ch],
            device_id={"ctx": 2 * p + side},
            device_id_type=MESH,
        )

    def sq_copy(p, d):
        return pltpu.make_async_remote_copy(
            src_ref=sq_mine.at[p],
            dst_ref=sq_all.at[HALVES * z + core],
            send_sem=sq_send.at[p],
            recv_sem=sq_recv,
            device_id={"ctx": 2 * p + side, "tp": lax.rem(z + d, TP)},
            device_id_type=MESH,
        )

    def sum_terms(p, begin, end):
        mine = c == 2 * p + side

        def sum_step(k, carry):
            from_low = z + TP - 1 - k
            from_high = z + k - (TP - 1)
            for ch in range(RS_CHUNKS):
                span = slice(ch * chunk, (ch + 1) * chunk)
                low = (z > 0) & (from_low < TP)
                high = (z < TP - 1) & (from_high >= 0)
                for dest, has, buf, copy in (
                    (from_high, high & (z == 1), rdn, rs_dn),
                    (from_low, low, rup, rs_up),
                    (from_high, high & (z != 1), rdn, rs_dn),
                ):
                    @pl.when(has)
                    def _():
                        copy(p, dest, ch).wait_recv()

                        @pl.when(dest != z)
                        def _():
                            start = pl.multiple_of(turn_of(dest) * extra + ch * chunk, 16)
                            there = pl.ds(start, chunk)
                            part[p, dest, there] = (
                                part[p, dest, there].astype(F32) + buf[p, dest, span].astype(F32)
                            ).astype(BF16)
                            copy(p, dest, ch).start()

                        @pl.when(dest == z)
                        def _():
                            own[p, span] += buf[p, dest, span].astype(F32)

                @pl.when(k == TP - 1)
                def _():
                    rounded = own[p, span].astype(BF16)

                    @pl.when(mine)
                    def _():
                        fin_ref[core, span] = rounded

                    @pl.when(jnp.logical_not(mine))
                    def _():
                        fin_mine[p, span] = rounded
                        fin_copy(p, ch).start()

            return carry

        lax.fori_loop(begin, end, sum_step, 0)

    def send_squares(p):
        mine = c == 2 * p + side
        as_row = jnp.sum(own[p] * own[p], axis=0, keepdims=True)
        sq_mine[p] = jnp.broadcast_to(as_row, sq_mine.shape[1:])

        @pl.when(mine)
        def _():
            sq_all[HALVES * z + core] = sq_mine[p]

        @pl.when(jnp.logical_not(mine))
        def _():
            sq_copy(p, 0).start()

        for d in range(1, TP):
            sq_copy(p, d).start()

    attention(0)

    output_terms(0)

    @pl.when(middle)
    def _():
        for g in range(HALVES):
            arrive(1, TP - 1, g)

    prepare_trig(1)

    def second_gather(step, carry):
        i = step // HALVES
        g = step % HALVES

        @pl.when(edge | (i == 0))
        def _():
            arrive(1, i, g)

        project(1, i, g)
        return carry

    lax.fori_loop(0, TP * HALVES, second_gather, 0)
    sum_terms(0, 1, 2)
    attention(1)
    sum_terms(0, 2, TP - 1)
    output_terms(1)
    sum_terms(0, TP - 1, TP)
    send_squares(0)
    post_gains = pg_ref[...].reshape(1, model)
    for i in range(TP):
        gain_post[i] = post_gains[:, i * feat : (i + 1) * feat]
    gain_out[...] = jnp.broadcast_to(gain_post[z], (rows, feat)).T
    sum_terms(1, 1, TP - 1)

    def landed(whole, sem):
        pltpu.make_async_copy(whole, whole, sem).wait()

    @pl.when(jnp.logical_not(carrier))
    def _():
        landed(tok_ref, x_send)
        landed(meta_ref, meta_send)

    @pl.when(carrier)
    def _():
        landed(meta_mine, meta_send)

    for p in range(PHASES):
        @pl.when(carrier)
        def _():
            def settle(i, carry):
                @pl.when((z < TP - 1) & (i <= z))
                def _():
                    landed(xbuf.at[p, i], ag_up.at[p, i])

                @pl.when((z > 0) & (i >= z))
                def _():
                    landed(xbuf.at[p, i], ag_dn.at[p, i])

                landed(xbuf.at[p, i], ag_pt.at[p, i])
                return carry

            lax.fori_loop(0, TP, settle, 0)

        @pl.when((p == 0) | (side == 0))
        def _():
            landed(kvbuf.at[2 * p + side], kv_send.at[p])

        attn_wait(p, core, at_send)

    sum_terms(1, TP - 1, TP)
    send_squares(1)

    source_side = c % 2
    count = TP * HALVES - 1

    @pl.when(carrier)
    def _():
        landed(sq_all.at[0:count], sq_recv)

    @pl.when(jnp.logical_not(carrier))
    def _():
        landed(sq_all, sq_recv)

    total = jnp.sum(sq_all[...], axis=0)[0:1]
    inv_post = lax.rsqrt(total * (1.0 / model) + EPSILON)
    for kk in range(HALVES):
        for ch in range(RS_CHUNKS):
            @pl.when(2 * source_side + kk != c)
            def _():
                landed(fin_ref.at[kk, slice(ch * chunk, (ch + 1) * chunk)], fin_recv.at[kk, ch])

            span = slice(kk * half + ch * chunk, kk * half + (ch + 1) * chunk)
            summed = fin_ref[kk, ch * chunk : (ch + 1) * chunk].astype(F32)
            out_ref[span] = (
                tok_ref[span].astype(F32) + summed * inv_post * gain_out[span]
            ).astype(BF16)

    for p in range(PHASES):
        def settle(i, carry):
            @pl.when(i != z)
            def _():
                landed(rup.at[p, i], rs_send.at[p, i])

            return carry

        lax.fori_loop(0, TP, settle, 0)

        @pl.when(c != 2 * p + side)
        def _():
            landed(fin_mine.at[p], fin_send.at[p])
            landed(sq_all.at[0:TP], sq_send.at[p])

        @pl.when(c == 2 * p + side)
        def _():
            landed(sq_all.at[0 : TP - 1], sq_send.at[p])


def per_device_fused(
    tokens, positions, first_key, input_gain, query_weight, kv_weight, query_gain, key_gain,
    out_weight, post_gain,
):
    feat, rows = tokens.shape[1], tokens.shape[0]
    half = feat // HALVES
    hd = query_gain.shape[0]
    model = query_weight.shape[0]
    q_cols = query_weight.shape[1] // 2
    kv_cols = kv_weight.shape[2] // 2
    kv_heads = kv_cols // hd
    wide = half + 128 - half % 128
    vmem = pl.BlockSpec(memory_space=pltpu.VMEM)
    anywhere = pl.BlockSpec(memory_space=pl.ANY)
    dma = pltpu.SemaphoreType.DMA
    return pl.pallas_call(
        fused_kernel,
        out_shape=jax.ShapeDtypeStruct((feat, rows), BF16),
        in_specs=[vmem] * 7 + [anywhere] * 3,
        out_specs=vmem,
        scratch_shapes=[
            pltpu.VMEM((PHASES, TP, feat, rows), BF16),
            pltpu.VMEM((rows, half), BF16),
            pltpu.VMEM((model, q_cols + 2 * kv_cols), BF16),
            pltpu.VMEM((TP, 2 * q_cols, wide), BF16),
            pltpu.VMEM((TP * HALVES, 1, half), F32),
            pltpu.VMEM((TP, 1, feat), F32),
            pltpu.VMEM((feat, rows), F32),
            pltpu.VMEM((PHASES, 1, rows), F32),
            pltpu.VMEM((PHASES, rows, q_cols + 2 * kv_cols), F32),
            pltpu.VMEM((PHASES, rows, hd), F32),
            pltpu.VMEM((PHASES, rows, hd), F32),
            pltpu.VMEM((8, rows), jnp.int32),
            pltpu.VMEM((PHASES, 8, rows), jnp.int32),
            pltpu.VMEM((CTX, kv_heads, 2, rows, hd), BF16),
            pltpu.VMEM((kv_heads, 2 * rows, hd), BF16),
            pltpu.VMEM((PHASES, 2 * kv_heads, rows, 2 * hd), BF16),
            pltpu.VMEM((PHASES, TP, wide, rows), BF16),
            pltpu.VMEM((PHASES, TP, half, rows), BF16),
            pltpu.VMEM((PHASES, TP, half, rows), BF16),
            pltpu.VMEM((PHASES, half, rows), F32),
            pltpu.VMEM((PHASES, half, rows), BF16),
            pltpu.VMEM((HALVES, half, rows), BF16),
            pltpu.VMEM((PHASES, 8, rows), F32),
            pltpu.VMEM((TP * HALVES, 8, rows), F32),
            dma((TP * HALVES,)),
            dma((TP,)),
            dma,
            dma((PHASES, TP)),
            dma((PHASES, TP)),
            dma((PHASES, TP)),
            dma((PHASES, TP, HOPS)),
            dma,
            dma((PHASES,)),
            dma((PHASES,)),
            dma((CTX, kv_heads)),
            dma((PHASES,)),
            dma((PHASES,)),
            dma((PHASES, TP)),
            dma((PHASES, TP, RS_CHUNKS)),
            dma((PHASES, TP, RS_CHUNKS)),
            dma((PHASES,)),
            dma((HALVES, RS_CHUNKS)),
            dma((PHASES,)),
            dma,
        ],
        compiler_params=pltpu.CompilerParams(
            collective_id=0, has_side_effects=True, vmem_limit_bytes=60 * 1024 * 1024
        ),
    )(
        tokens.T,
        positions.reshape(1, rows),
        first_key.reshape(1, rows),
        input_gain,
        query_gain.reshape(1, hd),
        key_gain.reshape(1, hd),
        post_gain,
        query_weight,
        kv_weight,
        out_weight,
    ).T


def solution(mesh):
    fused = mesh.shape["tp"] == TP and mesh.shape["ctx"] == CTX
    return jax.shard_map(
        per_device_fused if fused else per_device,
        mesh=mesh,
        in_specs=(
            P(("group", "ctx"), "tp"),
            P(("group", "ctx")),
            P(("group", "ctx")),
            P(),
            P(None, "tp"),
            P(None, None, "tp"),
            P(),
            P(),
            P("tp", None),
            P(),
        ),
        out_specs=P(("group", "ctx"), "tp"),
        check_vma=False,
    )
```

```python
import math

import jax
import jax.numpy as jnp
from jax import lax
from jax.experimental import pallas as pl
from jax.experimental.pallas import tpu as pltpu
from jax.sharding import PartitionSpec as P

D = 5376
H = 32
WINDOW = 1024


EPSILON = 1e-06


def from_partner(array, axis, distance):
    return lax.ppermute(array, axis, [(i, i ^ 1 << distance) for i in range(lax.axis_size(axis))])


def passed_along(block, axis, distance):
    devices = range(lax.axis_size(axis))
    route = [(i - distance, i) for i in devices if i - distance in devices]
    return lax.ppermute(block, axis, route)


def rms_norm(values, gain_vec):
    return (
        values * lax.rsqrt(jnp.mean(values * values, axis=-1, keepdims=True) + EPSILON) * gain_vec
    )


def rotate(values, positions_in):
    half_dim = values.shape[-1] // 2
    frequency = jnp.exp(
        jnp.arange(half_dim, dtype=jnp.float32) * (-2.0 * math.log(10000.0) / values.shape[-1])
    )
    angles = positions_in.astype(jnp.float32)[:, None] * frequency[None, :]
    cosines = jnp.cos(angles)[:, None, :]
    sine_part = jnp.sin(angles)[:, None, :]
    lower_half = values[..., :half_dim]
    upper_half = values[..., half_dim:]
    return jnp.concatenate(
        [
            lower_half * cosines - upper_half * sine_part,
            upper_half * cosines + lower_half * sine_part,
        ],
        axis=-1,
    )


def per_device(
    tokens,
    positions,
    first_key,
    input_gain,
    query_weight,
    kv_weight,
    query_gain,
    key_gain,
    out_weight,
    post_gain,
):
    tok_rows = tokens.shape[0]
    feat_dev = tokens.shape[1]
    head_dim = query_gain.shape[0]
    heads_dev = query_weight.shape[1] // head_dim
    tp_index = lax.axis_index("tp")
    ctx_index = lax.axis_index("ctx")
    ctx_count = lax.axis_size("ctx")
    local_x = tokens.astype(jnp.float32)
    kv_full = kv_weight
    if heads_dev == 1:
        partner = from_partner(kv_weight, "tp", 0)
        is_even = tp_index % 2 == 0
        kv_full = jnp.where(
            is_even,
            jnp.concatenate([kv_weight, partner], axis=2),
            jnp.concatenate([partner, kv_weight], axis=2),
        )
    gathered = lax.all_gather(tokens, "tp", axis=1, tiled=True).astype(jnp.float32)
    normed = rms_norm(gathered, input_gain).astype(jnp.bfloat16)
    query_raw = jnp.dot(normed, query_weight, preferred_element_type=jnp.float32)
    key_raw = jnp.dot(normed, kv_full[0], preferred_element_type=jnp.float32)
    value_raw = jnp.dot(normed, kv_full[1], preferred_element_type=jnp.float32)
    kv_heads = key_raw.shape[1] // head_dim
    group_size = heads_dev // kv_heads
    queries = (
        rotate(rms_norm(query_raw.reshape(tok_rows, heads_dev, head_dim), query_gain), positions)
        * (D // H) ** (-0.5)
    ).astype(jnp.bfloat16)
    keys = rotate(
        rms_norm(key_raw.reshape(tok_rows, kv_heads, head_dim), key_gain), positions
    ).astype(jnp.bfloat16)
    values_b = value_raw.reshape(tok_rows, kv_heads, head_dim).astype(jnp.bfloat16)
    kv_block = jnp.stack([keys, values_b])
    reach_blocks = min(ctx_count - 1, (WINDOW + tok_rows - 2) // tok_rows)
    received = []
    moving = kv_block
    for offset in range(reach_blocks):
        moving = passed_along(moving, "ctx", 1)
        received.append(moving)
    blocks = received[::-1] + [kv_block]
    keys_all = jnp.concatenate(blocks, axis=1)
    key_count = keys_all.shape[1]
    key_index = (ctx_index - reach_blocks) * tok_rows + jnp.arange(key_count, dtype=jnp.int32)
    query_index = ctx_index * tok_rows + jnp.arange(tok_rows, dtype=jnp.int32)
    visible = (key_index[None, :] >= first_key[:, None]) & (
        key_index[None, :] <= query_index[:, None]
    )
    grouped = queries.reshape(tok_rows, kv_heads, group_size, head_dim)
    scores = jnp.einsum("qkgd,tkd->kgqt", grouped, keys_all[0], preferred_element_type=jnp.float32)
    scores = jnp.where(visible[None, None], scores, -1e30)
    row_max = jnp.max(scores, axis=-1, keepdims=True)
    weights = jnp.exp(scores - row_max)
    denominator = jnp.sum(weights, axis=-1)
    mixed_out = jnp.einsum(
        "kgqt,tkd->qkgd",
        weights.astype(jnp.bfloat16),
        keys_all[1],
        preferred_element_type=jnp.float32,
    )
    mixed_out = mixed_out / jnp.transpose(denominator, (2, 0, 1))[..., None]
    attn = mixed_out.astype(jnp.bfloat16).reshape(tok_rows, heads_dev * head_dim)
    partial_value = jnp.dot(attn, out_weight, preferred_element_type=jnp.float32)
    summed = lax.psum(partial_value.astype(jnp.bfloat16), "tp").astype(jnp.float32)
    post_normed = rms_norm(summed, post_gain)
    own_cols = lax.dynamic_slice_in_dim(post_normed, tp_index * feat_dev, feat_dev, 1)
    return (local_x + own_cols).astype(jnp.bfloat16)


MESH = pl.DeviceIdType.MESH
F32 = jnp.float32
BF16 = jnp.bfloat16
TP = 4
CTX = 4
PHASES = 2
HALVES = 2
HOPS = 4
BEFORE_0 = 1
BEFORE_1 = 2
RS_CHUNKS = 2
PRESCALE = 2.0**-10


def fused_kernel(
    pos_ref, fk_ref, ig_ref, qg_ref, kg_ref, pg_ref, tok_hbm, qw_hbm, kvw_hbm, ow_hbm, out_ref,
    tok_ref, xbuf, xg_ref, w_ref, wo_ref, gain_in, gain_post, gain_out, ssq_ref, acc_ref, cos_ref, sin_ref,
    meta_mine, meta_ref, kvbuf, q_ref, attn_ref, part, rup, rdn, own, fin_mine, fin_ref, sq_mine, sq_all,
    tok_sem, own_sem, w_sem, wo_sem, x_send, ag_up, ag_dn, ag_pt, ag_recv, meta_send, meta_recv, kv_send, kv_recv,
    at_send, at_recv, rs_send, rs_up_recv, rs_dn_recv, fin_send, fin_recv, sq_send, sq_recv,
):
    feat, rows = tok_ref.shape
    half = feat // HALVES
    hop = feat // HOPS
    per_half = HOPS // HALVES
    chunk = half // RS_CHUNKS
    hd = qg_ref.shape[1]
    kv_heads = kvbuf.shape[1]
    kv_cols = kv_heads * hd
    q_cols = w_ref.shape[1] - 2 * kv_cols
    q_heads = q_cols // hd
    model = feat * TP
    z = lax.axis_index("tp")
    c = lax.axis_index("ctx")
    side = c // 2
    core = c % 2
    carrier = side == core
    partner = c + 1 - 2 * core
    far = lax.rem(c + 2, CTX)
    edge = (z == 0) | (z == TP - 1)
    up = {"tp": lax.rem(z + 1, TP)}
    down = {"tp": lax.rem(z + TP - 1, TP)}

    barrier = pltpu.get_barrier_semaphore()

    @pl.when(z < TP - 1)
    def _():
        pl.semaphore_signal(barrier, inc=1, device_id=up, device_id_type=MESH)

    @pl.when(z > 0)
    def _():
        pl.semaphore_signal(barrier, inc=1, device_id=down, device_id_type=MESH)

    for other in (far, partner, CTX - 1 - c):
        pl.semaphore_signal(barrier, inc=1, device_id={"ctx": other}, device_id_type=MESH)

    def half_span(spot):
        return pl.ds(pl.multiple_of(spot * half, 32), half)

    def weight_copies(src):
        span = pl.ds(pl.multiple_of(src * feat, 64), feat)
        kv_from = pl.ds(pl.multiple_of(core * kv_cols, 128), kv_cols)
        q_from = pl.ds(pl.multiple_of(core * q_cols, 128), q_cols)
        return (
            pltpu.make_async_copy(
                kvw_hbm.at[0, span, kv_from], w_ref.at[span, 0:kv_cols], w_sem.at[src]
            ),
            pltpu.make_async_copy(
                kvw_hbm.at[1, span, kv_from], w_ref.at[span, kv_cols : 2 * kv_cols], w_sem.at[src]
            ),
            pltpu.make_async_copy(
                qw_hbm.at[span, q_from], w_ref.at[span, 2 * kv_cols :], w_sem.at[src]
            ),
        )

    def source(i):
        second = jnp.where(z % 2 == 0, 1, 2)
        third = jnp.where(z == 0, 2, jnp.where(z == 1, 0, jnp.where(z == 2, 3, 1)))
        fourth = jnp.where(z < TP // 2, TP - 1, 0)
        return jnp.where(i == 0, z, jnp.where(i == 1, second, jnp.where(i == 2, third, fourth)))

    extra = half % 128
    turns = 128 // extra
    wide = half + 128 - extra

    def turn_of(dest):
        return (dest * HALVES + core) % turns

    def wo_copy(dest):
        start = pl.multiple_of((dest * HALVES + core) * half - turn_of(dest) * extra, 128)
        return pltpu.make_async_copy(ow_hbm.at[:, pl.ds(start, wide)], wo_ref.at[dest], wo_sem.at[dest])

    def out_order(i):
        outer = TP - 1 - i
        inner = jnp.where(i == 0, 3, jnp.where(i == 1, 0, jnp.where(i == 2, 2, 1)))
        dest = jnp.where(edge, outer, inner)
        return jnp.where(z < TP // 2, dest, TP - 1 - dest)

    def begin_weights(i, carry):
        for copy in weight_copies(source(i)):
            copy.start()
        return carry

    def begin_wo(i, carry):
        wo_copy(out_order(i)).start()
        return carry

    meta_mine[0:1] = pos_ref[...]
    meta_mine[1:2] = fk_ref[...]

    tok_copy = pltpu.make_async_copy(tok_hbm, tok_ref, tok_sem)
    own_copy = pltpu.make_async_copy(tok_hbm, xbuf.at[side, z], own_sem)

    @pl.when(carrier)
    def _():
        own_copy.start()
        meta_ref[side] = meta_mine[...]

    pl.semaphore_wait(barrier, jnp.where(edge, 4, 5))

    def hop_span(ch):
        return pl.ds(pl.multiple_of(ch * hop, 16), hop)

    def x_copy(ch):
        return pltpu.make_async_remote_copy(
            src_ref=tok_hbm.at[hop_span(ch)],
            dst_ref=xbuf.at[side, z, hop_span(ch)],
            send_sem=x_send,
            recv_sem=ag_recv.at[side, z, ch],
            device_id={"ctx": far},
            device_id_type=MESH,
        )

    def ag_copy(p, src, ch, send, target, block=None):
        here = xbuf.at[p, src, hop_span(ch)]
        return pltpu.make_async_remote_copy(
            src_ref=here if block is None else block.at[hop_span(ch)],
            dst_ref=here,
            send_sem=send.at[p, src],
            recv_sem=ag_recv.at[p, src, ch],
            device_id=target,
            device_id_type=MESH,
        )

    def meta_copy(target):
        return pltpu.make_async_remote_copy(
            src_ref=meta_mine,
            dst_ref=meta_ref.at[side],
            send_sem=meta_send,
            recv_sem=meta_recv.at[side],
            device_id={"ctx": target},
            device_id_type=MESH,
        )

    def forward_up(p, src, ch):
        @pl.when(carrier & (src <= z) & (z < TP - 1))
        def _():
            ag_copy(p, src, ch, ag_up, up).start()

    def forward_down(p, src, ch):
        @pl.when(carrier & (src >= z) & (z > 0))
        def _():
            ag_copy(p, src, ch, ag_dn, down).start()

    def forward_partner(p, src, ch):
        @pl.when(carrier)
        def _():
            ag_copy(p, src, ch, ag_pt, {"ctx": partner}).start()

    def forward(p, src, ch):
        forward_up(p, src, ch)
        forward_down(p, src, ch)
        forward_partner(p, src, ch)

    @pl.when(jnp.logical_not(carrier))
    def _():
        for ch in range(HOPS):
            x_copy(ch).start()
        meta_copy(far).start()
        meta_copy(CTX - 1 - c).start()

    @pl.when(carrier & (side == 0))
    def _():
        for ch in range(HOPS):
            @pl.when(z < TP - 1)
            def _():
                ag_copy(0, z, ch, ag_up, up, tok_hbm).start()

            @pl.when(z > 0)
            def _():
                ag_copy(0, z, ch, ag_dn, down, tok_hbm).start()

            ag_copy(0, z, ch, ag_pt, {"ctx": partner}, tok_hbm).start()

    @pl.when(carrier)
    def _():
        meta_copy(partner).start()

    lax.fori_loop(0, TP, begin_weights, 0)
    lax.fori_loop(0, TP, begin_wo, 0)
    tok_copy.start()
    ssq_ref[...] = jnp.zeros_like(ssq_ref)
    acc_ref[...] = jnp.zeros_like(acc_ref)
    r_iota = lax.broadcasted_iota(jnp.int32, (rows, rows), 0)
    c_iota = lax.broadcasted_iota(jnp.int32, (rows, rows), 1)
    diagonal = r_iota == c_iota

    def as_column(row):
        return jnp.sum(jnp.where(diagonal, row, 0.0), axis=1, keepdims=True)

    def prepare_gains():
        gains = ig_ref[...].reshape(1, model) * PRESCALE
        for i in range(TP * HALVES):
            gain_in[i] = gains[:, i * half : (i + 1) * half]

    def prepare_trig(p):
        @pl.when(jnp.logical_not(carrier & (side == p)))
        def _():
            pltpu.make_async_copy(meta_mine, meta_ref.at[p], meta_recv.at[p]).wait()

        lane = lax.broadcasted_iota(jnp.int32, (rows, hd), 1)
        place = jnp.where(lane < hd // 2, lane, lane - hd // 2).astype(F32)
        angles = as_column(meta_ref[p, 0:1].astype(F32)) * jnp.exp(
            place * (-2.0 * math.log(10000.0) / hd)
        )
        cos_ref[p] = jnp.cos(angles)
        sines = jnp.sin(angles)
        sin_ref[p] = jnp.where(lane < hd // 2, -sines, sines)

    def arrive_hop(p, i, ch):
        src = source(i)
        local = carrier & (i == 0) & ((side == p) if p == 0 else True)

        @pl.when(jnp.logical_not(local))
        def _():
            ag_copy(p, src, ch, ag_pt, {"ctx": partner}).wait_recv()

        @pl.when(jnp.logical_not(local) if p == 0 else i > 0)
        def _():
            forward(p, src, ch)

    def arrive(p, i, g):
        for j in range(per_half):
            arrive_hop(p, i, g * per_half + j)

    def arrive_both(p, ch):
        arrive_hop(p, 1, ch)
        arrive_hop(p, 2, ch)

    def begin_second(inner, outer):
        for ch in range(HOPS):
            @pl.when(carrier & (side == 0) & inner)
            def _():
                ag_copy(1, z, ch, ag_pt, {"ctx": partner}).wait_recv()

            @pl.when(jnp.where(z < TP // 2, inner, outer))
            def _():
                forward_up(1, z, ch)

            @pl.when(jnp.where(z < TP // 2, outer, inner))
            def _():
                forward_down(1, z, ch)

            @pl.when(outer)
            def _():
                forward_partner(1, z, ch)

    kv_width = 2 * kv_cols

    def project(p, i, g):
        src = source(i)
        spot = src * HALVES + g
        x_t = xbuf[p, src, pl.ds(pl.multiple_of(g * half, 32), half)].astype(F32)
        ssq_ref[p] += jnp.sum(x_t * x_t, axis=0, keepdims=True)
        xg_ref[...] = (x_t.T * gain_in[spot]).astype(BF16)
        last = (i == TP - 1) & (g == HALVES - 1)
        if p == 0:
            @pl.when(g == 0)
            def _():
                loaded = w_ref.at[pl.ds(pl.multiple_of(src * feat, 64), feat)]
                pltpu.make_async_copy(loaded, loaded, w_sem.at[src]).wait()


        @pl.when(jnp.logical_not(last))
        def _():
            acc_ref[p] += jnp.dot(xg_ref[...], w_ref[half_span(spot)], preferred_element_type=F32)

        @pl.when(last)
        def _():
            acc_ref[p, :, 0:kv_width] += jnp.dot(
                xg_ref[...], w_ref[half_span(spot), 0:kv_width], preferred_element_type=F32
            )

    middle = jnp.logical_not(edge)
    lag = jnp.where(middle, 1, 0)

    def first_gather(step, carry):
        i = step // HALVES
        g = step % HALVES

        @pl.when((edge & (i < TP)) | (middle & (i != 1) & (i < TP - 1)))
        def _():
            arrive(0, jnp.where(middle & (i == 2), TP - 1, i), g)

        @pl.when(middle & (i == 1))
        def _():
            for j in range(per_half):
                arrive_both(0, g * per_half + j)

        @pl.when((g == HALVES - 1) & ((i == 1) | (middle & (i == 2))))
        def _():
            begin_second(i == 1, edge | (i == 2))

        @pl.when(step == 0)
        def _():
            @pl.when(carrier)
            def _():
                own_copy.wait()

            prepare_gains()

        @pl.when((g == 0) & (i == jnp.where(edge, 1, TP)))
        def _():
            prepare_trig(0)

        @pl.when((i >= lag) & (i < TP + lag))
        def _():
            project(0, i - lag, g)

        return carry

    lax.fori_loop(0, (TP + lag) * HALVES, first_gather, 0)

    def kv_copy(p, h):
        here = kvbuf.at[2 * p + side, h]
        return pltpu.make_async_remote_copy(
            src_ref=here,
            dst_ref=here,
            send_sem=kv_send.at[p],
            recv_sem=kv_recv.at[2 * p + side, h],
            device_id={"ctx": far},
            device_id_type=MESH,
        )

    def kv_arrived(block, h):
        there = kvbuf.at[block, h]
        pltpu.make_async_copy(there, there, kv_recv.at[block, h]).wait()

    def attn_copy(p, h):
        here = attn_ref.at[p, kv_heads * core + h]
        return pltpu.make_async_remote_copy(
            src_ref=here,
            dst_ref=here,
            send_sem=at_send.at[p],
            recv_sem=at_recv.at[p],
            device_id={"ctx": partner},
            device_id_type=MESH,
        )

    def attn_wait(p, owner, sem):
        both = attn_ref.at[p, pl.ds(kv_heads * owner, kv_heads)]
        pltpu.make_async_copy(both, both, sem.at[p]).wait()

    def attend(p, ready, late):
        own_block = ready[0]
        first = as_column(meta_ref[p, 1:2].astype(F32)).astype(jnp.int32)

        def hidden(block):
            visible = block * rows + c_iota >= first
            if block == own_block:
                visible = visible & (c_iota <= r_iota)
            bias = jnp.where(visible, 0.0, -1e30)
            return jnp.concatenate([bias, bias], axis=0)

        def score(h, block, bias):
            return bias + lax.dot_general(
                q_ref[h], kvbuf[block, h, 0], (((1,), (1,)), ((), ())), preferred_element_type=F32
            )

        def mix(h, weights, blocks):
            weights = weights.astype(BF16)
            return sum(
                jnp.dot(
                    weights[:, j * rows : (j + 1) * rows], kvbuf[block, h, 1],
                    preferred_element_type=F32,
                )
                for j, block in enumerate(blocks)
            )

        biases = [hidden(block) for block in ready]
        states = []
        for h in range(kv_heads):
            s = jnp.concatenate([score(h, b, bias) for b, bias in zip(ready, biases)], axis=1)
            top = jnp.max(s, axis=1, keepdims=True)
            weights = jnp.exp(s - top)
            states.append((top, jnp.sum(weights, axis=1, keepdims=True), mix(h, weights, ready)))
        late_bias = None if late is None else hidden(late)
        for h in range(kv_heads):
            top, total, mixed = states[h]
            if late is not None:
                kv_arrived(late, h)
                s = score(h, late, late_bias)
                higher = jnp.maximum(top, jnp.max(s, axis=1, keepdims=True))
                fade = jnp.exp(top - higher)
                weights = jnp.exp(s - higher)
                total = total * fade + jnp.sum(weights, axis=1, keepdims=True)
                mixed = mixed * fade + mix(h, weights, [late])
            mixed = (mixed / total).astype(BF16)
            attn_ref[p, kv_heads * core + h] = jnp.concatenate([mixed[:rows], mixed[rows:]], axis=1)
            attn_copy(p, h).start()

    def attention(p):
        inv = lax.rsqrt(as_column(ssq_ref[p]) * (1.0 / model) + EPSILON) * (1.0 / PRESCALE)

        def normed_rotated(raw, gain_vec):
            raw = raw * inv
            scaled = raw * lax.rsqrt(jnp.mean(raw * raw, axis=1, keepdims=True) + EPSILON) * gain_vec
            return scaled * cos_ref[p] + pltpu.roll(scaled, hd // 2, 1) * sin_ref[p]

        block = 2 * p + side
        for h in range(kv_heads):
            k_cols = slice(h * hd, (h + 1) * hd)
            v_cols = slice(kv_cols + h * hd, kv_cols + (h + 1) * hd)
            kvbuf[block, h, 0] = normed_rotated(acc_ref[p, :, k_cols], kg_ref[...]).astype(BF16)
            kvbuf[block, h, 1] = (acc_ref[p, :, v_cols] * inv).astype(BF16)

            @pl.when((p == 0) | (side == 0))
            def _():
                kv_copy(p, h).start()

        spot = source(TP - 1) * HALVES + HALVES - 1
        acc_ref[p, :, kv_width:] += jnp.dot(
            xg_ref[...], w_ref[half_span(spot), kv_width:], preferred_element_type=F32
        )
        for h in range(q_heads):
            cols = slice(kv_width + h * hd, kv_width + (h + 1) * hd)
            q_ref[h // 2, (h % 2) * rows : (h % 2 + 1) * rows] = (
                normed_rotated(acc_ref[p, :, cols], qg_ref[...]) * (D // H) ** (-0.5)
            ).astype(BF16)

        if p == 0:
            @pl.when(middle)
            def _():
                for ch in range(HOPS):
                    arrive_both(1, ch)
        else:
            sum_terms(0, 2, TP - 1)

        @pl.when(side == 0)
        def _():
            if p == 1:
                for h in range(kv_heads):
                    kv_arrived(1, h)
            attend(p, [2 * p, *range(2 * p)], None)

        @pl.when(side == 1)
        def _():
            attend(p, [2 * p + 1, *range(2 * p)], 2 * p)

    def rs_copy(p, dest, ch, buf, recv, target):
        start = pl.multiple_of(turn_of(dest) * extra + ch * chunk, 16)
        return pltpu.make_async_remote_copy(
            src_ref=part.at[p, dest, pl.ds(start, chunk)],
            dst_ref=buf.at[p, dest, pl.ds(pl.multiple_of(ch * chunk, 16), chunk)],
            send_sem=rs_send.at[p, dest],
            recv_sem=recv.at[p, dest, ch],
            device_id=target,
            device_id_type=MESH,
        )

    def rs_up(p, dest, ch):
        return rs_copy(p, dest, ch, rup, rs_up_recv, up)

    def rs_dn(p, dest, ch):
        return rs_copy(p, dest, ch, rdn, rs_dn_recv, down)

    def output_terms(p):
        attn_wait(p, 1 - core, at_recv)

        def out_step(i, carry):
            dest = out_order(i)
            if p == 0:
                wo_copy(dest).wait()
            mixed = jnp.concatenate([attn_ref[p, j] for j in range(2 * kv_heads)], axis=1)
            part[p, dest] = jnp.dot(mixed, wo_ref[dest], preferred_element_type=F32).T.astype(BF16)

            for ch in range(RS_CHUNKS):
                @pl.when((z == 0) & (dest > 0))
                def _():
                    rs_up(p, dest, ch).start()

                @pl.when((z == TP - 1) & (dest < TP - 1))
                def _():
                    rs_dn(p, dest, ch).start()

            return carry

        lax.fori_loop(0, TP, out_step, 0)
        own[p] = part[p, z, pl.ds(pl.multiple_of(turn_of(z) * extra, 16), half)].astype(F32)

    def fin_copy(p, ch):
        span = pl.ds(pl.multiple_of(ch * chunk, 16), chunk)
        return pltpu.make_async_remote_copy(
            src_ref=fin_mine.at[p, span],
            dst_ref=fin_ref.at[core, span],
            send_sem=fin_send.at[p],
            recv_sem=fin_recv.at[core, ch],
            device_id={"ctx": 2 * p + side},
            device_id_type=MESH,
        )

    def sq_copy(p, d):
        return pltpu.make_async_remote_copy(
            src_ref=sq_mine.at[p],
            dst_ref=sq_all.at[HALVES * z + core],
            send_sem=sq_send.at[p],
            recv_sem=sq_recv,
            device_id={"ctx": 2 * p + side, "tp": lax.rem(z + d, TP)},
            device_id_type=MESH,
        )

    def sum_terms(p, begin, end):
        mine = c == 2 * p + side

        def sum_step(k, carry):
            from_low = z + TP - 1 - k
            from_high = z + k - (TP - 1)
            for ch in range(RS_CHUNKS):
                span = slice(ch * chunk, (ch + 1) * chunk)
                low = (z > 0) & (from_low < TP)
                high = (z < TP - 1) & (from_high >= 0)
                for dest, has, buf, copy in (
                    (from_high, high & (z == 1), rdn, rs_dn),
                    (from_low, low, rup, rs_up),
                    (from_high, high & (z != 1), rdn, rs_dn),
                ):
                    @pl.when(has)
                    def _():
                        copy(p, dest, ch).wait_recv()

                        @pl.when(dest != z)
                        def _():
                            start = pl.multiple_of(turn_of(dest) * extra + ch * chunk, 16)
                            there = pl.ds(start, chunk)
                            part[p, dest, there] = (
                                part[p, dest, there].astype(F32) + buf[p, dest, span].astype(F32)
                            ).astype(BF16)
                            copy(p, dest, ch).start()

                        @pl.when(dest == z)
                        def _():
                            own[p, span] += buf[p, dest, span].astype(F32)

                @pl.when(k == TP - 1)
                def _():
                    rounded = own[p, span].astype(BF16)

                    @pl.when(mine)
                    def _():
                        fin_ref[core, span] = rounded

                    @pl.when(jnp.logical_not(mine))
                    def _():
                        fin_mine[p, span] = rounded
                        fin_copy(p, ch).start()

            return carry

        lax.fori_loop(begin, end, sum_step, 0)

    def send_squares(p):
        mine = c == 2 * p + side
        as_row = jnp.sum(own[p] * own[p], axis=0, keepdims=True)
        sq_mine[p] = jnp.broadcast_to(as_row, sq_mine.shape[1:])

        @pl.when(mine)
        def _():
            sq_all[HALVES * z + core] = sq_mine[p]

        @pl.when(jnp.logical_not(mine))
        def _():
            sq_copy(p, 0).start()

        for d in range(1, TP):
            sq_copy(p, d).start()

    attention(0)

    @pl.when(middle)
    def _():
        for g in range(HALVES):
            arrive(1, TP - 1, g)

    output_terms(0)
    prepare_trig(1)
    before_sums = HALVES * jnp.where(side == 0, BEFORE_0, BEFORE_1)

    def second_gather(step, carry):
        i = step // HALVES
        g = step % HALVES

        @pl.when(step == before_sums)
        def _():
            sum_terms(0, 1, 2)

        @pl.when(edge | (i == 0))
        def _():
            arrive(1, i, g)

        project(1, i, g)
        return carry

    lax.fori_loop(0, TP * HALVES, second_gather, 0)
    attention(1)
    output_terms(1)
    sum_terms(0, TP - 1, TP)
    send_squares(0)
    post_gains = pg_ref[...].reshape(1, model)
    for i in range(TP):
        gain_post[i] = post_gains[:, i * feat : (i + 1) * feat]
    gain_out[...] = jnp.broadcast_to(gain_post[z], (rows, feat)).T
    sum_terms(1, 1, TP - 1)

    def landed(whole, sem):
        pltpu.make_async_copy(whole, whole, sem).wait()

    tok_copy.wait()

    @pl.when(jnp.logical_not(carrier))
    def _():
        landed(tok_ref, x_send)
        landed(meta_ref, meta_send)

    @pl.when(carrier)
    def _():
        landed(meta_mine, meta_send)

    for p in range(PHASES):
        @pl.when(carrier)
        def _():
            def settle(i, carry):
                @pl.when((z < TP - 1) & (i <= z))
                def _():
                    landed(xbuf.at[p, i], ag_up.at[p, i])

                @pl.when((z > 0) & (i >= z))
                def _():
                    landed(xbuf.at[p, i], ag_dn.at[p, i])

                landed(xbuf.at[p, i], ag_pt.at[p, i])
                return carry

            lax.fori_loop(0, TP, settle, 0)

        @pl.when((p == 0) | (side == 0))
        def _():
            landed(kvbuf.at[2 * p + side], kv_send.at[p])

        attn_wait(p, core, at_send)

    sum_terms(1, TP - 1, TP)
    send_squares(1)

    source_side = c % 2
    count = TP * HALVES - 1

    @pl.when(carrier)
    def _():
        landed(sq_all.at[0:count], sq_recv)

    @pl.when(jnp.logical_not(carrier))
    def _():
        landed(sq_all, sq_recv)

    total = jnp.sum(sq_all[...], axis=0)[0:1]
    inv_post = lax.rsqrt(total * (1.0 / model) + EPSILON)
    for kk in range(HALVES):
        for ch in range(RS_CHUNKS):
            @pl.when(2 * source_side + kk != c)
            def _():
                landed(fin_ref.at[kk, slice(ch * chunk, (ch + 1) * chunk)], fin_recv.at[kk, ch])

            span = slice(kk * half + ch * chunk, kk * half + (ch + 1) * chunk)
            summed = fin_ref[kk, ch * chunk : (ch + 1) * chunk].astype(F32)
            out_ref[span] = (
                tok_ref[span].astype(F32) + summed * inv_post * gain_out[span]
            ).astype(BF16)

    for p in range(PHASES):
        def settle(i, carry):
            @pl.when(i != z)
            def _():
                landed(rup.at[p, i], rs_send.at[p, i])

            return carry

        lax.fori_loop(0, TP, settle, 0)

        @pl.when(c != 2 * p + side)
        def _():
            landed(fin_mine.at[p], fin_send.at[p])
            landed(sq_all.at[0:TP], sq_send.at[p])

        @pl.when(c == 2 * p + side)
        def _():
            landed(sq_all.at[0 : TP - 1], sq_send.at[p])


def per_device_fused(
    tokens, positions, first_key, input_gain, query_weight, kv_weight, query_gain, key_gain,
    out_weight, post_gain,
):
    feat, rows = tokens.shape[1], tokens.shape[0]
    half = feat // HALVES
    hd = query_gain.shape[0]
    model = query_weight.shape[0]
    q_cols = query_weight.shape[1] // 2
    kv_cols = kv_weight.shape[2] // 2
    kv_heads = kv_cols // hd
    wide = half + 128 - half % 128
    vmem = pl.BlockSpec(memory_space=pltpu.VMEM)
    anywhere = pl.BlockSpec(memory_space=pl.ANY)
    dma = pltpu.SemaphoreType.DMA
    return pl.pallas_call(
        fused_kernel,
        out_shape=jax.ShapeDtypeStruct((feat, rows), BF16),
        in_specs=[vmem] * 6 + [anywhere] * 4,
        out_specs=vmem,
        scratch_shapes=[
            pltpu.VMEM((feat, rows), BF16),
            pltpu.VMEM((PHASES, TP, feat, rows), BF16),
            pltpu.VMEM((rows, half), BF16),
            pltpu.VMEM((model, q_cols + 2 * kv_cols), BF16),
            pltpu.VMEM((TP, 2 * q_cols, wide), BF16),
            pltpu.VMEM((TP * HALVES, 1, half), F32),
            pltpu.VMEM((TP, 1, feat), F32),
            pltpu.VMEM((feat, rows), F32),
            pltpu.VMEM((PHASES, 1, rows), F32),
            pltpu.VMEM((PHASES, rows, q_cols + 2 * kv_cols), F32),
            pltpu.VMEM((PHASES, rows, hd), F32),
            pltpu.VMEM((PHASES, rows, hd), F32),
            pltpu.VMEM((8, rows), jnp.int32),
            pltpu.VMEM((PHASES, 8, rows), jnp.int32),
            pltpu.VMEM((CTX, kv_heads, 2, rows, hd), BF16),
            pltpu.VMEM((kv_heads, 2 * rows, hd), BF16),
            pltpu.VMEM((PHASES, 2 * kv_heads, rows, 2 * hd), BF16),
            pltpu.VMEM((PHASES, TP, wide, rows), BF16),
            pltpu.VMEM((PHASES, TP, half, rows), BF16),
            pltpu.VMEM((PHASES, TP, half, rows), BF16),
            pltpu.VMEM((PHASES, half, rows), F32),
            pltpu.VMEM((PHASES, half, rows), BF16),
            pltpu.VMEM((HALVES, half, rows), BF16),
            pltpu.VMEM((PHASES, 8, rows), F32),
            pltpu.VMEM((TP * HALVES, 8, rows), F32),
            dma,
            dma,
            dma((TP,)),
            dma((TP,)),
            dma,
            dma((PHASES, TP)),
            dma((PHASES, TP)),
            dma((PHASES, TP)),
            dma((PHASES, TP, HOPS)),
            dma,
            dma((PHASES,)),
            dma((PHASES,)),
            dma((CTX, kv_heads)),
            dma((PHASES,)),
            dma((PHASES,)),
            dma((PHASES, TP)),
            dma((PHASES, TP, RS_CHUNKS)),
            dma((PHASES, TP, RS_CHUNKS)),
            dma((PHASES,)),
            dma((HALVES, RS_CHUNKS)),
            dma((PHASES,)),
            dma,
        ],
        compiler_params=pltpu.CompilerParams(
            collective_id=0, has_side_effects=True, vmem_limit_bytes=60 * 1024 * 1024
        ),
    )(
        positions.reshape(1, rows),
        first_key.reshape(1, rows),
        input_gain,
        query_gain.reshape(1, hd),
        key_gain.reshape(1, hd),
        post_gain,
        tokens.T,
        query_weight,
        kv_weight,
        out_weight,
    ).T


def solution(mesh):
    fused = mesh.shape["tp"] == TP and mesh.shape["ctx"] == CTX
    return jax.shard_map(
        per_device_fused if fused else per_device,
        mesh=mesh,
        in_specs=(
            P(("group", "ctx"), "tp"),
            P(("group", "ctx")),
            P(("group", "ctx")),
            P(),
            P(None, "tp"),
            P(None, None, "tp"),
            P(),
            P(),
            P("tp", None),
            P(),
        ),
        out_specs=P(("group", "ctx"), "tp"),
        check_vma=False,
    )
```

```python
import math

import jax
import jax.numpy as jnp
from jax import lax
from jax.experimental import pallas as pl
from jax.experimental.pallas import tpu as pltpu
from jax.sharding import PartitionSpec as P

D = 5376
H = 32
WINDOW = 1024


EPSILON = 1e-06


def from_partner(array, axis, distance):
    return lax.ppermute(array, axis, [(i, i ^ 1 << distance) for i in range(lax.axis_size(axis))])


def passed_along(block, axis, distance):
    devices = range(lax.axis_size(axis))
    route = [(i - distance, i) for i in devices if i - distance in devices]
    return lax.ppermute(block, axis, route)


def rms_norm(values, gain_vec):
    return (
        values * lax.rsqrt(jnp.mean(values * values, axis=-1, keepdims=True) + EPSILON) * gain_vec
    )


def rotate(values, positions_in):
    half_dim = values.shape[-1] // 2
    frequency = jnp.exp(
        jnp.arange(half_dim, dtype=jnp.float32) * (-2.0 * math.log(10000.0) / values.shape[-1])
    )
    angles = positions_in.astype(jnp.float32)[:, None] * frequency[None, :]
    cosines = jnp.cos(angles)[:, None, :]
    sine_part = jnp.sin(angles)[:, None, :]
    lower_half = values[..., :half_dim]
    upper_half = values[..., half_dim:]
    return jnp.concatenate(
        [
            lower_half * cosines - upper_half * sine_part,
            upper_half * cosines + lower_half * sine_part,
        ],
        axis=-1,
    )


def per_device(
    tokens,
    positions,
    first_key,
    input_gain,
    query_weight,
    kv_weight,
    query_gain,
    key_gain,
    out_weight,
    post_gain,
):
    tok_rows = tokens.shape[0]
    feat_dev = tokens.shape[1]
    head_dim = query_gain.shape[0]
    heads_dev = query_weight.shape[1] // head_dim
    tp_index = lax.axis_index("tp")
    ctx_index = lax.axis_index("ctx")
    ctx_count = lax.axis_size("ctx")
    local_x = tokens.astype(jnp.float32)
    kv_full = kv_weight
    if heads_dev == 1:
        partner = from_partner(kv_weight, "tp", 0)
        is_even = tp_index % 2 == 0
        kv_full = jnp.where(
            is_even,
            jnp.concatenate([kv_weight, partner], axis=2),
            jnp.concatenate([partner, kv_weight], axis=2),
        )
    gathered = lax.all_gather(tokens, "tp", axis=1, tiled=True).astype(jnp.float32)
    normed = rms_norm(gathered, input_gain).astype(jnp.bfloat16)
    query_raw = jnp.dot(normed, query_weight, preferred_element_type=jnp.float32)
    key_raw = jnp.dot(normed, kv_full[0], preferred_element_type=jnp.float32)
    value_raw = jnp.dot(normed, kv_full[1], preferred_element_type=jnp.float32)
    kv_heads = key_raw.shape[1] // head_dim
    group_size = heads_dev // kv_heads
    queries = (
        rotate(rms_norm(query_raw.reshape(tok_rows, heads_dev, head_dim), query_gain), positions)
        * (D // H) ** (-0.5)
    ).astype(jnp.bfloat16)
    keys = rotate(
        rms_norm(key_raw.reshape(tok_rows, kv_heads, head_dim), key_gain), positions
    ).astype(jnp.bfloat16)
    values_b = value_raw.reshape(tok_rows, kv_heads, head_dim).astype(jnp.bfloat16)
    kv_block = jnp.stack([keys, values_b])
    reach_blocks = min(ctx_count - 1, (WINDOW + tok_rows - 2) // tok_rows)
    received = []
    moving = kv_block
    for offset in range(reach_blocks):
        moving = passed_along(moving, "ctx", 1)
        received.append(moving)
    blocks = received[::-1] + [kv_block]
    keys_all = jnp.concatenate(blocks, axis=1)
    key_count = keys_all.shape[1]
    key_index = (ctx_index - reach_blocks) * tok_rows + jnp.arange(key_count, dtype=jnp.int32)
    query_index = ctx_index * tok_rows + jnp.arange(tok_rows, dtype=jnp.int32)
    visible = (key_index[None, :] >= first_key[:, None]) & (
        key_index[None, :] <= query_index[:, None]
    )
    grouped = queries.reshape(tok_rows, kv_heads, group_size, head_dim)
    scores = jnp.einsum("qkgd,tkd->kgqt", grouped, keys_all[0], preferred_element_type=jnp.float32)
    scores = jnp.where(visible[None, None], scores, -1e30)
    row_max = jnp.max(scores, axis=-1, keepdims=True)
    weights = jnp.exp(scores - row_max)
    denominator = jnp.sum(weights, axis=-1)
    mixed_out = jnp.einsum(
        "kgqt,tkd->qkgd",
        weights.astype(jnp.bfloat16),
        keys_all[1],
        preferred_element_type=jnp.float32,
    )
    mixed_out = mixed_out / jnp.transpose(denominator, (2, 0, 1))[..., None]
    attn = mixed_out.astype(jnp.bfloat16).reshape(tok_rows, heads_dev * head_dim)
    partial_value = jnp.dot(attn, out_weight, preferred_element_type=jnp.float32)
    summed = lax.psum(partial_value.astype(jnp.bfloat16), "tp").astype(jnp.float32)
    post_normed = rms_norm(summed, post_gain)
    own_cols = lax.dynamic_slice_in_dim(post_normed, tp_index * feat_dev, feat_dev, 1)
    return (local_x + own_cols).astype(jnp.bfloat16)


MESH = pl.DeviceIdType.MESH
F32 = jnp.float32
BF16 = jnp.bfloat16
TP = 4
CTX = 4
PHASES = 2
HALVES = 2
HOPS = 4
BEFORE_0 = 1
BEFORE_1 = 2
RS_CHUNKS = 2
PRESCALE = 2.0**-10


def fused_kernel(
    pos_ref, fk_ref, ig_ref, qg_ref, kg_ref, pg_ref, tok_hbm, qw_hbm, kvw_hbm, ow_hbm, out_ref,
    tok_ref, xbuf, xg_ref, w_ref, wo_ref, gain_in, gain_post, gain_out, ssq_ref, acc_ref, cos_ref, sin_ref,
    meta_mine, meta_ref, kvbuf, q_ref, attn_ref, part, rup, rdn, own, fin_mine, fin_ref, sq_mine, sq_all,
    sq_pair, sq_sum,
    tok_sem, own_sem, w_sem, wo_sem, x_send, ag_up, ag_dn, ag_pt, ag_recv, meta_send, meta_recv, kv_send, kv_recv,
    at_send, at_recv, rs_send, rs_up_recv, rs_dn_recv, fin_send, fin_recv, sq_send, sq_recv,
    pair_recv, share_send,
):
    feat, rows = tok_ref.shape
    half = feat // HALVES
    hop = feat // HOPS
    per_half = HOPS // HALVES
    chunk = half // RS_CHUNKS
    hd = qg_ref.shape[1]
    kv_heads = kvbuf.shape[2]
    kv_cols = kv_heads * hd
    q_cols = w_ref.shape[1] - 2 * kv_cols
    q_heads = q_cols // hd
    model = feat * TP
    z = lax.axis_index("tp")
    c = lax.axis_index("ctx")
    side = c // 2
    core = c % 2
    carrier = side == core
    partner = c + 1 - 2 * core
    far = lax.rem(c + 2, CTX)
    edge = (z == 0) | (z == TP - 1)
    up = {"tp": lax.rem(z + 1, TP)}
    down = {"tp": lax.rem(z + TP - 1, TP)}

    barrier = pltpu.get_barrier_semaphore()

    @pl.when(z < TP - 1)
    def _():
        pl.semaphore_signal(barrier, inc=1, device_id=up, device_id_type=MESH)

    @pl.when(z > 0)
    def _():
        pl.semaphore_signal(barrier, inc=1, device_id=down, device_id_type=MESH)

    for other in (far, partner, CTX - 1 - c):
        pl.semaphore_signal(barrier, inc=1, device_id={"ctx": other}, device_id_type=MESH)

    def half_span(spot):
        return pl.ds(pl.multiple_of(spot * half, 32), half)

    def weight_copies(src):
        span = pl.ds(pl.multiple_of(src * feat, 64), feat)
        kv_from = pl.ds(pl.multiple_of(core * kv_cols, 128), kv_cols)
        q_from = pl.ds(pl.multiple_of(core * q_cols, 128), q_cols)
        return (
            pltpu.make_async_copy(
                kvw_hbm.at[0, span, kv_from], w_ref.at[span, 0:kv_cols], w_sem.at[src]
            ),
            pltpu.make_async_copy(
                kvw_hbm.at[1, span, kv_from], w_ref.at[span, kv_cols : 2 * kv_cols], w_sem.at[src]
            ),
            pltpu.make_async_copy(
                qw_hbm.at[span, q_from], w_ref.at[span, 2 * kv_cols :], w_sem.at[src]
            ),
        )

    def source(i):
        second = jnp.where(z % 2 == 0, 1, 2)
        third = jnp.where(z == 0, 2, jnp.where(z == 1, 0, jnp.where(z == 2, 3, 1)))
        fourth = jnp.where(z < TP // 2, TP - 1, 0)
        return jnp.where(i == 0, z, jnp.where(i == 1, second, jnp.where(i == 2, third, fourth)))

    extra = half % 128
    turns = 128 // extra
    wide = half + 128 - extra

    def turn_of(dest):
        return (dest * HALVES + core) % turns

    def wo_copy(dest):
        start = pl.multiple_of((dest * HALVES + core) * half - turn_of(dest) * extra, 128)
        return pltpu.make_async_copy(ow_hbm.at[:, pl.ds(start, wide)], wo_ref.at[dest], wo_sem.at[dest])

    def out_order(i):
        outer = TP - 1 - i
        inner = jnp.where(i == 0, 3, jnp.where(i == 1, 0, jnp.where(i == 2, 2, 1)))
        dest = jnp.where(edge, outer, inner)
        return jnp.where(z < TP // 2, dest, TP - 1 - dest)

    def begin_weights(i, carry):
        for copy in weight_copies(source(i)):
            copy.start()
        return carry

    def begin_wo(i, carry):
        wo_copy(out_order(i)).start()
        return carry

    meta_mine[0:1] = pos_ref[...]
    meta_mine[1:2] = fk_ref[...]

    tok_copy = pltpu.make_async_copy(tok_hbm, tok_ref, tok_sem)
    own_copy = pltpu.make_async_copy(tok_hbm, xbuf.at[side, z], own_sem)

    @pl.when(carrier)
    def _():
        own_copy.start()
        meta_ref[side] = meta_mine[...]

    pl.semaphore_wait(barrier, jnp.where(edge, 4, 5))

    def hop_span(ch):
        return pl.ds(pl.multiple_of(ch * hop, 16), hop)

    def x_copy(ch):
        return pltpu.make_async_remote_copy(
            src_ref=tok_hbm.at[hop_span(ch)],
            dst_ref=xbuf.at[side, z, hop_span(ch)],
            send_sem=x_send,
            recv_sem=ag_recv.at[side, z, ch],
            device_id={"ctx": far},
            device_id_type=MESH,
        )

    def ag_copy(p, src, ch, send, target, block=None):
        here = xbuf.at[p, src, hop_span(ch)]
        return pltpu.make_async_remote_copy(
            src_ref=here if block is None else block.at[hop_span(ch)],
            dst_ref=here,
            send_sem=send.at[p],
            recv_sem=ag_recv.at[p, src, ch],
            device_id=target,
            device_id_type=MESH,
        )

    def meta_copy(target):
        return pltpu.make_async_remote_copy(
            src_ref=meta_mine,
            dst_ref=meta_ref.at[side],
            send_sem=meta_send,
            recv_sem=meta_recv.at[side],
            device_id={"ctx": target},
            device_id_type=MESH,
        )

    def forward_up(p, src, ch):
        @pl.when(carrier & (src <= z) & (z < TP - 1))
        def _():
            ag_copy(p, src, ch, ag_up, up).start()

    def forward_down(p, src, ch):
        @pl.when(carrier & (src >= z) & (z > 0))
        def _():
            ag_copy(p, src, ch, ag_dn, down).start()

    def forward_partner(p, src, ch):
        @pl.when(carrier)
        def _():
            ag_copy(p, src, ch, ag_pt, {"ctx": partner}).start()

    def forward(p, src, ch):
        forward_up(p, src, ch)
        forward_down(p, src, ch)
        forward_partner(p, src, ch)

    @pl.when(jnp.logical_not(carrier))
    def _():
        for ch in range(HOPS):
            x_copy(ch).start()
        meta_copy(far).start()
        meta_copy(CTX - 1 - c).start()

    @pl.when(carrier & (side == 0))
    def _():
        for ch in range(HOPS):
            @pl.when(z < TP - 1)
            def _():
                ag_copy(0, z, ch, ag_up, up, tok_hbm).start()

            @pl.when(z > 0)
            def _():
                ag_copy(0, z, ch, ag_dn, down, tok_hbm).start()

            ag_copy(0, z, ch, ag_pt, {"ctx": partner}, tok_hbm).start()

    @pl.when(carrier)
    def _():
        meta_copy(partner).start()

    lax.fori_loop(0, TP, begin_weights, 0)
    lax.fori_loop(0, TP, begin_wo, 0)
    tok_copy.start()
    ssq_ref[...] = jnp.zeros_like(ssq_ref)
    acc_ref[...] = jnp.zeros_like(acc_ref)
    r_iota = lax.broadcasted_iota(jnp.int32, (rows, rows), 0)
    c_iota = lax.broadcasted_iota(jnp.int32, (rows, rows), 1)
    diagonal = r_iota == c_iota

    def as_column(row):
        return jnp.sum(jnp.where(diagonal, row, 0.0), axis=1, keepdims=True)

    def prepare_gains():
        gains = ig_ref[...].reshape(1, model) * PRESCALE
        for i in range(TP * HALVES):
            gain_in[i] = gains[:, i * half : (i + 1) * half]

    def prepare_trig(p):
        @pl.when(jnp.logical_not(carrier & (side == p)))
        def _():
            pltpu.make_async_copy(meta_mine, meta_ref.at[p], meta_recv.at[p]).wait()

        lane = lax.broadcasted_iota(jnp.int32, (rows, hd), 1)
        place = jnp.where(lane < hd // 2, lane, lane - hd // 2).astype(F32)
        angles = as_column(meta_ref[p, 0:1].astype(F32)) * jnp.exp(
            place * (-2.0 * math.log(10000.0) / hd)
        )
        cos_ref[p] = jnp.cos(angles)
        sines = jnp.sin(angles)
        sin_ref[p] = jnp.where(lane < hd // 2, -sines, sines)

    def arrive_hop(p, i, ch):
        src = source(i)
        local = carrier & (i == 0) & ((side == p) if p == 0 else True)

        @pl.when(jnp.logical_not(local))
        def _():
            ag_copy(p, src, ch, ag_pt, {"ctx": partner}).wait_recv()

        @pl.when(jnp.logical_not(local) if p == 0 else i > 0)
        def _():
            forward(p, src, ch)

    def arrive(p, i, g):
        for j in range(per_half):
            arrive_hop(p, i, g * per_half + j)

    def arrive_both(p, ch):
        arrive_hop(p, 1, ch)
        arrive_hop(p, 2, ch)

    def begin_second(inner, outer):
        for ch in range(HOPS):
            @pl.when(carrier & (side == 0) & inner)
            def _():
                ag_copy(1, z, ch, ag_pt, {"ctx": partner}).wait_recv()

            @pl.when(jnp.where(z < TP // 2, inner, outer))
            def _():
                forward_up(1, z, ch)

            @pl.when(jnp.where(z < TP // 2, outer, inner))
            def _():
                forward_down(1, z, ch)

            @pl.when(outer)
            def _():
                forward_partner(1, z, ch)

    kv_width = 2 * kv_cols

    def project(p, i, g):
        src = source(i)
        spot = src * HALVES + g
        x_t = xbuf[p, src, pl.ds(pl.multiple_of(g * half, 32), half)].astype(F32)
        ssq_ref[p] += jnp.sum(x_t * x_t, axis=0, keepdims=True)
        xg_ref[...] = (x_t.T * gain_in[spot]).astype(BF16)
        last = (i == TP - 1) & (g == HALVES - 1)
        if p == 0:
            @pl.when(g == 0)
            def _():
                loaded = w_ref.at[pl.ds(pl.multiple_of(src * feat, 64), feat)]
                pltpu.make_async_copy(loaded, loaded, w_sem.at[src]).wait()


        @pl.when(jnp.logical_not(last))
        def _():
            acc_ref[p] += jnp.dot(xg_ref[...], w_ref[half_span(spot)], preferred_element_type=F32)

        @pl.when(last)
        def _():
            acc_ref[p, :, 0:kv_width] += jnp.dot(
                xg_ref[...], w_ref[half_span(spot), 0:kv_width], preferred_element_type=F32
            )

    middle = jnp.logical_not(edge)
    lag = jnp.where(middle, 1, 0)

    def first_gather(step, carry):
        i = step // HALVES
        g = step % HALVES

        @pl.when((edge & (i < TP)) | (middle & (i != 1) & (i < TP - 1)))
        def _():
            arrive(0, jnp.where(middle & (i == 2), TP - 1, i), g)

        @pl.when(middle & (i == 1))
        def _():
            for j in range(per_half):
                arrive_both(0, g * per_half + j)

        @pl.when((g == HALVES - 1) & ((i == 1) | (middle & (i == 2))))
        def _():
            begin_second(i == 1, edge | (i == 2))

        @pl.when(step == 0)
        def _():
            @pl.when(carrier)
            def _():
                own_copy.wait()

            prepare_gains()

        @pl.when((g == 0) & (i == jnp.where(edge, 1, TP)))
        def _():
            prepare_trig(0)

        @pl.when((i >= lag) & (i < TP + lag))
        def _():
            project(0, i - lag, g)

        return carry

    lax.fori_loop(0, (TP + lag) * HALVES, first_gather, 0)

    def kv_copy(p, j):
        here = kvbuf.at[2 * p + side, j]
        return pltpu.make_async_remote_copy(
            src_ref=here,
            dst_ref=here,
            send_sem=kv_send.at[p],
            recv_sem=kv_recv.at[2 * p + side, j],
            device_id={"ctx": far},
            device_id_type=MESH,
        )

    def kv_arrived(block, j):
        there = kvbuf.at[block, j]
        pltpu.make_async_copy(there, there, kv_recv.at[block, j]).wait()

    def attn_copy(p, h):
        here = attn_ref.at[p, kv_heads * core + h]
        return pltpu.make_async_remote_copy(
            src_ref=here,
            dst_ref=here,
            send_sem=at_send.at[p],
            recv_sem=at_recv.at[p],
            device_id={"ctx": partner},
            device_id_type=MESH,
        )

    def attn_wait(p, owner, sem):
        both = attn_ref.at[p, pl.ds(kv_heads * owner, kv_heads)]
        pltpu.make_async_copy(both, both, sem.at[p]).wait()

    def attend(p, ready, late):
        own_block = ready[0]
        first = as_column(meta_ref[p, 1:2].astype(F32)).astype(jnp.int32)

        def hidden(block):
            visible = block * rows + c_iota >= first
            if block == own_block:
                visible = visible & (c_iota <= r_iota)
            bias = jnp.where(visible, 0.0, -1e30)
            return jnp.concatenate([bias, bias], axis=0)

        def score(h, block, bias):
            return bias + lax.dot_general(
                q_ref[h], kvbuf[block, 0, h], (((1,), (1,)), ((), ())), preferred_element_type=F32
            )

        def mix(h, weights, blocks):
            weights = weights.astype(BF16)
            return sum(
                jnp.dot(
                    weights[:, j * rows : (j + 1) * rows], kvbuf[block, 1, h],
                    preferred_element_type=F32,
                )
                for j, block in enumerate(blocks)
            )

        biases = [hidden(block) for block in ready]
        states = []
        for h in range(kv_heads):
            s = jnp.concatenate([score(h, b, bias) for b, bias in zip(ready, biases)], axis=1)
            top = jnp.max(s, axis=1, keepdims=True)
            weights = jnp.exp(s - top)
            states.append((top, jnp.sum(weights, axis=1, keepdims=True), mix(h, weights, ready)))
        if late is not None:
            late_bias = hidden(late)
            kv_arrived(late, 0)
            late_weights = []
            for h in range(kv_heads):
                top, total, mixed = states[h]
                s = score(h, late, late_bias)
                higher = jnp.maximum(top, jnp.max(s, axis=1, keepdims=True))
                fade = jnp.exp(top - higher)
                weights = jnp.exp(s - higher)
                total = total * fade + jnp.sum(weights, axis=1, keepdims=True)
                states[h] = (higher, total, mixed * fade)
                late_weights.append(weights)
            kv_arrived(late, 1)
        for h in range(kv_heads):
            _, total, mixed = states[h]
            if late is not None:
                mixed = mixed + mix(h, late_weights[h], [late])
            mixed = (mixed / total).astype(BF16)
            attn_ref[p, kv_heads * core + h] = jnp.concatenate([mixed[:rows], mixed[rows:]], axis=1)
            attn_copy(p, h).start()

    def attention(p):
        inv = lax.rsqrt(as_column(ssq_ref[p]) * (1.0 / model) + EPSILON) * (1.0 / PRESCALE)

        def normed_rotated(raw, gain_vec):
            raw = raw * inv
            scaled = raw * lax.rsqrt(jnp.mean(raw * raw, axis=1, keepdims=True) + EPSILON) * gain_vec
            return scaled * cos_ref[p] + pltpu.roll(scaled, hd // 2, 1) * sin_ref[p]

        block = 2 * p + side
        for h in range(kv_heads):
            cols = slice(h * hd, (h + 1) * hd)
            kvbuf[block, 0, h] = normed_rotated(acc_ref[p, :, cols], kg_ref[...]).astype(BF16)

        @pl.when((p == 0) | (side == 0))
        def _():
            kv_copy(p, 0).start()

        for h in range(kv_heads):
            cols = slice(kv_cols + h * hd, kv_cols + (h + 1) * hd)
            kvbuf[block, 1, h] = (acc_ref[p, :, cols] * inv).astype(BF16)

        @pl.when((p == 0) | (side == 0))
        def _():
            kv_copy(p, 1).start()

        spot = source(TP - 1) * HALVES + HALVES - 1
        acc_ref[p, :, kv_width:] += jnp.dot(
            xg_ref[...], w_ref[half_span(spot), kv_width:], preferred_element_type=F32
        )
        for h in range(q_heads):
            cols = slice(kv_width + h * hd, kv_width + (h + 1) * hd)
            q_ref[h // 2, (h % 2) * rows : (h % 2 + 1) * rows] = (
                normed_rotated(acc_ref[p, :, cols], qg_ref[...]) * (D // H) ** (-0.5)
            ).astype(BF16)

        if p == 0:
            @pl.when(middle)
            def _():
                for ch in range(HOPS):
                    arrive_both(1, ch)

                def own_block(g, carry):
                    arrive(1, 0, g)
                    project(1, 0, g)
                    return carry

                lax.fori_loop(0, HALVES, own_block, 0)
        else:
            sum_terms(0, 2, TP - 1)

        @pl.when(side == 0)
        def _():
            if p == 1:
                for j in range(2):
                    kv_arrived(1, j)
            attend(p, [2 * p, *range(2 * p)], None)

        @pl.when(side == 1)
        def _():
            attend(p, [2 * p + 1, *range(2 * p)], 2 * p)

    def rs_copy(p, dest, ch, buf, recv, target):
        start = pl.multiple_of(turn_of(dest) * extra + ch * chunk, 16)
        return pltpu.make_async_remote_copy(
            src_ref=part.at[p, dest, pl.ds(start, chunk)],
            dst_ref=buf.at[p, dest, pl.ds(pl.multiple_of(ch * chunk, 16), chunk)],
            send_sem=rs_send.at[p],
            recv_sem=recv.at[p, dest, ch],
            device_id=target,
            device_id_type=MESH,
        )

    def rs_up(p, dest, ch):
        return rs_copy(p, dest, ch, rup, rs_up_recv, up)

    def rs_dn(p, dest, ch):
        return rs_copy(p, dest, ch, rdn, rs_dn_recv, down)

    def output_terms(p):
        def half_product(dest, owner):
            span = pl.ds(pl.multiple_of(owner * q_cols, 128), q_cols)
            mixed = jnp.concatenate(
                [attn_ref[p, kv_heads * owner + j] for j in range(kv_heads)], axis=1
            )
            return jnp.dot(mixed, wo_ref[dest, span], preferred_element_type=F32)

        def send_term(dest, term):
            part[p, dest] = term.T.astype(BF16)
            for ch in range(RS_CHUNKS):
                @pl.when((z == 0) & (dest > 0))
                def _():
                    rs_up(p, dest, ch).start()

                @pl.when((z == TP - 1) & (dest < TP - 1))
                def _():
                    rs_dn(p, dest, ch).start()

        first = out_order(0)
        if p == 0:
            wo_copy(first).wait()
        near = half_product(first, core)
        attn_wait(p, 1 - core, at_recv)
        send_term(first, near + half_product(first, 1 - core))

        def out_step(i, carry):
            dest = out_order(i)
            if p == 0:
                wo_copy(dest).wait()
            mixed = jnp.concatenate([attn_ref[p, j] for j in range(2 * kv_heads)], axis=1)
            send_term(dest, jnp.dot(mixed, wo_ref[dest], preferred_element_type=F32))
            return carry

        lax.fori_loop(1, TP, out_step, 0)
        own[p] = part[p, z, pl.ds(pl.multiple_of(turn_of(z) * extra, 16), half)].astype(F32)

    def fin_copy(p, ch):
        span = pl.ds(pl.multiple_of(ch * chunk, 16), chunk)
        return pltpu.make_async_remote_copy(
            src_ref=fin_mine.at[p, span],
            dst_ref=fin_ref.at[core, span],
            send_sem=fin_send.at[p],
            recv_sem=fin_recv.at[core, ch],
            device_id={"ctx": 2 * p + side},
            device_id_type=MESH,
        )

    def sq_copy(p, d):
        return pltpu.make_async_remote_copy(
            src_ref=sq_mine.at[p],
            dst_ref=sq_all.at[HALVES * z + core],
            send_sem=sq_send.at[p],
            recv_sem=sq_recv,
            device_id={"ctx": 2 * p + side, "tp": lax.rem(z + d, TP)},
            device_id_type=MESH,
        )

    def sum_terms(p, begin, end):
        mine = c == 2 * p + side

        def sum_step(k, carry):
            from_low = z + TP - 1 - k
            from_high = z + k - (TP - 1)
            for ch in range(RS_CHUNKS):
                span = slice(ch * chunk, (ch + 1) * chunk)
                low = (z > 0) & (from_low < TP)
                high = (z < TP - 1) & (from_high >= 0)
                for dest, has, buf, copy in (
                    (from_high, high & (z == 1), rdn, rs_dn),
                    (from_low, low, rup, rs_up),
                    (from_high, high & (z != 1), rdn, rs_dn),
                ):
                    @pl.when(has)
                    def _():
                        copy(p, dest, ch).wait_recv()

                        @pl.when(dest != z)
                        def _():
                            start = pl.multiple_of(turn_of(dest) * extra + ch * chunk, 16)
                            there = pl.ds(start, chunk)
                            part[p, dest, there] = (
                                part[p, dest, there].astype(F32) + buf[p, dest, span].astype(F32)
                            ).astype(BF16)
                            copy(p, dest, ch).start()

                        @pl.when(dest == z)
                        def _():
                            own[p, span] += buf[p, dest, span].astype(F32)

                @pl.when(k == TP - 1)
                def _():
                    rounded = own[p, span].astype(BF16)

                    @pl.when(mine)
                    def _():
                        fin_ref[core, span] = rounded

                    @pl.when(jnp.logical_not(mine))
                    def _():
                        fin_mine[p, span] = rounded
                        fin_copy(p, ch).start()

            return carry

        lax.fori_loop(begin, end, sum_step, 0)

    def pair_copy():
        return pltpu.make_async_remote_copy(
            src_ref=sq_mine.at[0],
            dst_ref=sq_pair.at[core],
            send_sem=sq_send.at[0],
            recv_sem=pair_recv,
            device_id={"ctx": 1},
            device_id_type=MESH,
        )

    def share_copy(d):
        return pltpu.make_async_remote_copy(
            src_ref=sq_sum,
            dst_ref=sq_all.at[z],
            send_sem=share_send,
            recv_sem=sq_recv,
            device_id={"tp": lax.rem(z + d, TP)},
            device_id_type=MESH,
        )

    def send_squares(p):
        mine = c == 2 * p + side
        as_row = jnp.sum(own[p] * own[p], axis=0, keepdims=True)
        sq_mine[p] = jnp.broadcast_to(as_row, sq_mine.shape[1:])

        @pl.when(mine)
        def _():
            sq_all[HALVES * z + core] = sq_mine[p]

        def send_direct():
            @pl.when(jnp.logical_not(mine))
            def _():
                sq_copy(p, 0).start()

            for d in range(1, TP):
                sq_copy(p, d).start()

        if p == 0:
            pl.when(side == 0)(send_direct)

            @pl.when(side == 1)
            def _():
                pair_copy().start()
        else:
            send_direct()

    attention(0)

    @pl.when(middle)
    def _():
        for g in range(HALVES):
            arrive(1, TP - 1, g)

    output_terms(0)
    prepare_trig(1)
    before_sums = HALVES * jnp.where(side == 0, BEFORE_0, BEFORE_1)

    def second_gather(step, carry):
        i = step // HALVES
        g = step % HALVES

        @pl.when(step == before_sums)
        def _():
            sum_terms(0, 1, 2)

        @pl.when(edge)
        def _():
            arrive(1, i, g)

        project(1, i, g)
        return carry

    lax.fori_loop(jnp.where(edge, 0, HALVES), TP * HALVES, second_gather, 0)
    attention(1)
    output_terms(1)
    sum_terms(0, TP - 1, TP)
    send_squares(0)
    post_gains = pg_ref[...].reshape(1, model)
    for i in range(TP):
        gain_post[i] = post_gains[:, i * feat : (i + 1) * feat]
    gain_out[...] = jnp.broadcast_to(gain_post[z], (rows, feat)).T
    sum_terms(1, 1, TP - 1)

    def landed(whole, sem):
        pltpu.make_async_copy(whole, whole, sem).wait()

    tok_copy.wait()

    @pl.when(jnp.logical_not(carrier))
    def _():
        landed(tok_ref, x_send)
        landed(meta_ref, meta_send)

    @pl.when(carrier)
    def _():
        landed(meta_mine, meta_send)

    for p in range(PHASES):
        @pl.when(carrier)
        def _():
            for n in range(1, TP):
                @pl.when(z == n - 1)
                def _():
                    landed(xbuf.at[p, 0:n], ag_up.at[p])

                @pl.when(z == TP - n)
                def _():
                    landed(xbuf.at[p, 0:n], ag_dn.at[p])

            landed(xbuf.at[p], ag_pt.at[p])

        @pl.when((p == 0) | (side == 0))
        def _():
            landed(kvbuf.at[2 * p + side], kv_send.at[p])

        attn_wait(p, core, at_send)

    sum_terms(1, TP - 1, TP)
    send_squares(1)

    for p in range(PHASES):
        landed(rup.at[p, 0 : TP - 1], rs_send.at[p])

    source_side = c % 2

    @pl.when(carrier)
    def _():
        landed(sq_all.at[0 : TP * HALVES - 1], sq_recv)

    @pl.when(c == 1)
    def _():
        landed(sq_pair, pair_recv)
        sq_sum[...] = sq_pair[0] + sq_pair[1]
        for d in range(1, TP):
            share_copy(d).start()
        sq_all[z] = sq_sum[...]
        sq_all[TP:] = jnp.zeros((TP * HALVES - TP, *sq_sum.shape), F32)
        landed(sq_all.at[0 : TP - 1], sq_recv)

    @pl.when(c == 2)
    def _():
        landed(sq_all, sq_recv)

    total = jnp.sum(sq_all[...], axis=0)[0:1]
    inv_post = lax.rsqrt(total * (1.0 / model) + EPSILON)
    for kk in range(HALVES):
        for ch in range(RS_CHUNKS):
            @pl.when(2 * source_side + kk != c)
            def _():
                landed(fin_ref.at[kk, slice(ch * chunk, (ch + 1) * chunk)], fin_recv.at[kk, ch])

            span = slice(kk * half + ch * chunk, kk * half + (ch + 1) * chunk)
            summed = fin_ref[kk, ch * chunk : (ch + 1) * chunk].astype(F32)
            out_ref[span] = (
                tok_ref[span].astype(F32) + summed * inv_post * gain_out[span]
            ).astype(BF16)

    for p in range(PHASES):
        paired = (side == 1) if p == 0 else False

        @pl.when(c != 2 * p + side)
        def _():
            landed(fin_mine.at[p], fin_send.at[p])

            @pl.when(jnp.logical_not(paired))
            def _():
                landed(sq_all.at[0:TP], sq_send.at[p])

        @pl.when(paired)
        def _():
            landed(sq_mine.at[0], sq_send.at[0])

        @pl.when(c == 2 * p + side)
        def _():
            landed(sq_all.at[0 : TP - 1], sq_send.at[p])

    @pl.when(c == 1)
    def _():
        landed(sq_all.at[0 : TP - 1], share_send)


def per_device_fused(
    tokens, positions, first_key, input_gain, query_weight, kv_weight, query_gain, key_gain,
    out_weight, post_gain,
):
    feat, rows = tokens.shape[1], tokens.shape[0]
    half = feat // HALVES
    hd = query_gain.shape[0]
    model = query_weight.shape[0]
    q_cols = query_weight.shape[1] // 2
    kv_cols = kv_weight.shape[2] // 2
    kv_heads = kv_cols // hd
    wide = half + 128 - half % 128
    vmem = pl.BlockSpec(memory_space=pltpu.VMEM)
    anywhere = pl.BlockSpec(memory_space=pl.ANY)
    dma = pltpu.SemaphoreType.DMA
    return pl.pallas_call(
        fused_kernel,
        out_shape=jax.ShapeDtypeStruct((feat, rows), BF16),
        in_specs=[vmem] * 6 + [anywhere] * 4,
        out_specs=vmem,
        scratch_shapes=[
            pltpu.VMEM((feat, rows), BF16),
            pltpu.VMEM((PHASES, TP, feat, rows), BF16),
            pltpu.VMEM((rows, half), BF16),
            pltpu.VMEM((model, q_cols + 2 * kv_cols), BF16),
            pltpu.VMEM((TP, 2 * q_cols, wide), BF16),
            pltpu.VMEM((TP * HALVES, 1, half), F32),
            pltpu.VMEM((TP, 1, feat), F32),
            pltpu.VMEM((feat, rows), F32),
            pltpu.VMEM((PHASES, 1, rows), F32),
            pltpu.VMEM((PHASES, rows, q_cols + 2 * kv_cols), F32),
            pltpu.VMEM((PHASES, rows, hd), F32),
            pltpu.VMEM((PHASES, rows, hd), F32),
            pltpu.VMEM((8, rows), jnp.int32),
            pltpu.VMEM((PHASES, 8, rows), jnp.int32),
            pltpu.VMEM((CTX, 2, kv_heads, rows, hd), BF16),
            pltpu.VMEM((kv_heads, 2 * rows, hd), BF16),
            pltpu.VMEM((PHASES, 2 * kv_heads, rows, 2 * hd), BF16),
            pltpu.VMEM((PHASES, TP, wide, rows), BF16),
            pltpu.VMEM((PHASES, TP, half, rows), BF16),
            pltpu.VMEM((PHASES, TP, half, rows), BF16),
            pltpu.VMEM((PHASES, half, rows), F32),
            pltpu.VMEM((PHASES, half, rows), BF16),
            pltpu.VMEM((HALVES, half, rows), BF16),
            pltpu.VMEM((PHASES, 8, rows), F32),
            pltpu.VMEM((TP * HALVES, 8, rows), F32),
            pltpu.VMEM((HALVES, 8, rows), F32),
            pltpu.VMEM((8, rows), F32),
            dma,
            dma,
            dma((TP,)),
            dma((TP,)),
            dma,
            dma((PHASES,)),
            dma((PHASES,)),
            dma((PHASES,)),
            dma((PHASES, TP, HOPS)),
            dma,
            dma((PHASES,)),
            dma((PHASES,)),
            dma((CTX, 2)),
            dma((PHASES,)),
            dma((PHASES,)),
            dma((PHASES,)),
            dma((PHASES, TP, RS_CHUNKS)),
            dma((PHASES, TP, RS_CHUNKS)),
            dma((PHASES,)),
            dma((HALVES, RS_CHUNKS)),
            dma((PHASES,)),
            dma,
            dma,
            dma,
        ],
        compiler_params=pltpu.CompilerParams(
            collective_id=0, has_side_effects=True, vmem_limit_bytes=60 * 1024 * 1024
        ),
    )(
        positions.reshape(1, rows),
        first_key.reshape(1, rows),
        input_gain,
        query_gain.reshape(1, hd),
        key_gain.reshape(1, hd),
        post_gain,
        tokens.T,
        query_weight,
        kv_weight,
        out_weight,
    ).T


def solution(mesh):
    fused = mesh.shape["tp"] == TP and mesh.shape["ctx"] == CTX
    return jax.shard_map(
        per_device_fused if fused else per_device,
        mesh=mesh,
        in_specs=(
            P(("group", "ctx"), "tp"),
            P(("group", "ctx")),
            P(("group", "ctx")),
            P(),
            P(None, "tp"),
            P(None, None, "tp"),
            P(),
            P(),
            P("tp", None),
            P(),
        ),
        out_specs=P(("group", "ctx"), "tp"),
        check_vma=False,
    )
```

```python
import math

import jax
import jax.numpy as jnp
from jax import lax
from jax.experimental import pallas as pl
from jax.experimental.pallas import tpu as pltpu
from jax.sharding import PartitionSpec as P

D = 5376
H = 32
WINDOW = 1024


EPSILON = 1e-06


def from_partner(array, axis, distance):
    return lax.ppermute(array, axis, [(i, i ^ 1 << distance) for i in range(lax.axis_size(axis))])


def passed_along(block, axis, distance):
    devices = range(lax.axis_size(axis))
    route = [(i - distance, i) for i in devices if i - distance in devices]
    return lax.ppermute(block, axis, route)


def rms_norm(values, gain_vec):
    return (
        values * lax.rsqrt(jnp.mean(values * values, axis=-1, keepdims=True) + EPSILON) * gain_vec
    )


def rotate(values, positions_in):
    half_dim = values.shape[-1] // 2
    frequency = jnp.exp(
        jnp.arange(half_dim, dtype=jnp.float32) * (-2.0 * math.log(10000.0) / values.shape[-1])
    )
    angles = positions_in.astype(jnp.float32)[:, None] * frequency[None, :]
    cosines = jnp.cos(angles)[:, None, :]
    sine_part = jnp.sin(angles)[:, None, :]
    lower_half = values[..., :half_dim]
    upper_half = values[..., half_dim:]
    return jnp.concatenate(
        [
            lower_half * cosines - upper_half * sine_part,
            upper_half * cosines + lower_half * sine_part,
        ],
        axis=-1,
    )


def per_device(
    tokens,
    positions,
    first_key,
    input_gain,
    query_weight,
    kv_weight,
    query_gain,
    key_gain,
    out_weight,
    post_gain,
):
    tok_rows = tokens.shape[0]
    feat_dev = tokens.shape[1]
    head_dim = query_gain.shape[0]
    heads_dev = query_weight.shape[1] // head_dim
    tp_index = lax.axis_index("tp")
    ctx_index = lax.axis_index("ctx")
    ctx_count = lax.axis_size("ctx")
    local_x = tokens.astype(jnp.float32)
    kv_full = kv_weight
    if heads_dev == 1:
        partner = from_partner(kv_weight, "tp", 0)
        is_even = tp_index % 2 == 0
        kv_full = jnp.where(
            is_even,
            jnp.concatenate([kv_weight, partner], axis=2),
            jnp.concatenate([partner, kv_weight], axis=2),
        )
    gathered = lax.all_gather(tokens, "tp", axis=1, tiled=True).astype(jnp.float32)
    normed = rms_norm(gathered, input_gain).astype(jnp.bfloat16)
    query_raw = jnp.dot(normed, query_weight, preferred_element_type=jnp.float32)
    key_raw = jnp.dot(normed, kv_full[0], preferred_element_type=jnp.float32)
    value_raw = jnp.dot(normed, kv_full[1], preferred_element_type=jnp.float32)
    kv_heads = key_raw.shape[1] // head_dim
    group_size = heads_dev // kv_heads
    queries = (
        rotate(rms_norm(query_raw.reshape(tok_rows, heads_dev, head_dim), query_gain), positions)
        * (D // H) ** (-0.5)
    ).astype(jnp.bfloat16)
    keys = rotate(
        rms_norm(key_raw.reshape(tok_rows, kv_heads, head_dim), key_gain), positions
    ).astype(jnp.bfloat16)
    values_b = value_raw.reshape(tok_rows, kv_heads, head_dim).astype(jnp.bfloat16)
    kv_block = jnp.stack([keys, values_b])
    reach_blocks = min(ctx_count - 1, (WINDOW + tok_rows - 2) // tok_rows)
    received = []
    moving = kv_block
    for offset in range(reach_blocks):
        moving = passed_along(moving, "ctx", 1)
        received.append(moving)
    blocks = received[::-1] + [kv_block]
    keys_all = jnp.concatenate(blocks, axis=1)
    key_count = keys_all.shape[1]
    key_index = (ctx_index - reach_blocks) * tok_rows + jnp.arange(key_count, dtype=jnp.int32)
    query_index = ctx_index * tok_rows + jnp.arange(tok_rows, dtype=jnp.int32)
    visible = (key_index[None, :] >= first_key[:, None]) & (
        key_index[None, :] <= query_index[:, None]
    )
    grouped = queries.reshape(tok_rows, kv_heads, group_size, head_dim)
    scores = jnp.einsum("qkgd,tkd->kgqt", grouped, keys_all[0], preferred_element_type=jnp.float32)
    scores = jnp.where(visible[None, None], scores, -1e30)
    row_max = jnp.max(scores, axis=-1, keepdims=True)
    weights = jnp.exp(scores - row_max)
    denominator = jnp.sum(weights, axis=-1)
    mixed_out = jnp.einsum(
        "kgqt,tkd->qkgd",
        weights.astype(jnp.bfloat16),
        keys_all[1],
        preferred_element_type=jnp.float32,
    )
    mixed_out = mixed_out / jnp.transpose(denominator, (2, 0, 1))[..., None]
    attn = mixed_out.astype(jnp.bfloat16).reshape(tok_rows, heads_dev * head_dim)
    partial_value = jnp.dot(attn, out_weight, preferred_element_type=jnp.float32)
    summed = lax.psum(partial_value.astype(jnp.bfloat16), "tp").astype(jnp.float32)
    post_normed = rms_norm(summed, post_gain)
    own_cols = lax.dynamic_slice_in_dim(post_normed, tp_index * feat_dev, feat_dev, 1)
    return (local_x + own_cols).astype(jnp.bfloat16)


MESH = pl.DeviceIdType.MESH
F32 = jnp.float32
BF16 = jnp.bfloat16
TP = 4
CTX = 4
PHASES = 2
HALVES = 2
HOPS = 4
BEFORE_0 = 1
BEFORE_1 = 2
RS_CHUNKS = 2
PRESCALE = 2.0**-10


def fused_kernel(
    pos_ref, fk_ref, ig_ref, qg_ref, kg_ref, pg_ref, tok_hbm, qw_hbm, kvw_hbm, ow_hbm, out_ref,
    tok_ref, xbuf, xg_ref, w_ref, wo_ref, gain_in, gain_post, gain_out, ssq_ref, acc_ref, cos_ref, sin_ref,
    meta_mine, meta_ref, kvbuf, q_ref, attn_ref, part, rup, rdn, own, fin_mine, fin_ref, sq_mine, sq_all,
    sq_pair, sq_sum,
    tok_sem, own_sem, w_sem, wo_sem, x_send, ag_up, ag_dn, ag_pt, ag_recv, meta_send, meta_recv, kv_send, kv_recv,
    at_send, at_recv, rs_send, rs_up_recv, rs_dn_recv, fin_send, fin_recv, sq_send, sq_recv,
    pair_recv, share_send,
):
    feat, rows = tok_ref.shape
    half = feat // HALVES
    hop = feat // HOPS
    per_half = HOPS // HALVES
    chunk = half // RS_CHUNKS
    hd = qg_ref.shape[1]
    kv_heads = kvbuf.shape[2]
    kv_cols = kv_heads * hd
    q_cols = w_ref.shape[1] - 2 * kv_cols
    q_heads = q_cols // hd
    model = feat * TP
    z = lax.axis_index("tp")
    c = lax.axis_index("ctx")
    side = c // 2
    core = c % 2
    carrier = side == core
    partner = c + 1 - 2 * core
    far = lax.rem(c + 2, CTX)
    edge = (z == 0) | (z == TP - 1)
    up = {"tp": lax.rem(z + 1, TP)}
    down = {"tp": lax.rem(z + TP - 1, TP)}

    barrier = pltpu.get_barrier_semaphore()

    @pl.when(z < TP - 1)
    def _():
        pl.semaphore_signal(barrier, inc=1, device_id=up, device_id_type=MESH)

    @pl.when(z > 0)
    def _():
        pl.semaphore_signal(barrier, inc=1, device_id=down, device_id_type=MESH)

    for other in (far, partner, CTX - 1 - c):
        pl.semaphore_signal(barrier, inc=1, device_id={"ctx": other}, device_id_type=MESH)

    def half_span(spot):
        return pl.ds(pl.multiple_of(spot * half, 32), half)

    def weight_copies(src):
        span = pl.ds(pl.multiple_of(src * feat, 64), feat)
        kv_from = pl.ds(pl.multiple_of(core * kv_cols, 128), kv_cols)
        q_from = pl.ds(pl.multiple_of(core * q_cols, 128), q_cols)
        return (
            pltpu.make_async_copy(
                kvw_hbm.at[0, span, kv_from], w_ref.at[span, 0:kv_cols], w_sem.at[src]
            ),
            pltpu.make_async_copy(
                kvw_hbm.at[1, span, kv_from], w_ref.at[span, kv_cols : 2 * kv_cols], w_sem.at[src]
            ),
            pltpu.make_async_copy(
                qw_hbm.at[span, q_from], w_ref.at[span, 2 * kv_cols :], w_sem.at[src]
            ),
        )

    def source(i):
        second = jnp.where(z % 2 == 0, 1, 2)
        third = jnp.where(z == 0, 2, jnp.where(z == 1, 0, jnp.where(z == 2, 3, 1)))
        fourth = jnp.where(z < TP // 2, TP - 1, 0)
        return jnp.where(i == 0, z, jnp.where(i == 1, second, jnp.where(i == 2, third, fourth)))

    extra = half % 128
    turns = 128 // extra
    wide = half + 128 - extra

    def turn_of(dest):
        return (dest * HALVES + core) % turns

    def wo_copy(dest):
        start = pl.multiple_of((dest * HALVES + core) * half - turn_of(dest) * extra, 128)
        return pltpu.make_async_copy(ow_hbm.at[:, pl.ds(start, wide)], wo_ref.at[dest], wo_sem.at[dest])

    def out_order(i):
        outer = TP - 1 - i
        inner = jnp.where(i == 0, 3, jnp.where(i == 1, 0, jnp.where(i == 2, 2, 1)))
        dest = jnp.where(edge, outer, inner)
        return jnp.where(z < TP // 2, dest, TP - 1 - dest)

    def begin_weights(i, carry):
        for copy in weight_copies(source(i)):
            copy.start()
        return carry

    def begin_wo(i, carry):
        wo_copy(out_order(i)).start()
        return carry

    meta_mine[0:1] = pos_ref[...]
    meta_mine[1:2] = fk_ref[...]

    tok_copy = pltpu.make_async_copy(tok_hbm, tok_ref, tok_sem)
    own_copy = pltpu.make_async_copy(tok_hbm, xbuf.at[side, z], own_sem)

    @pl.when(carrier)
    def _():
        own_copy.start()
        meta_ref[side] = meta_mine[...]

    pl.semaphore_wait(barrier, jnp.where(edge, 4, 5))

    def hop_span(ch):
        return pl.ds(pl.multiple_of(ch * hop, 16), hop)

    def x_copy(ch):
        return pltpu.make_async_remote_copy(
            src_ref=tok_hbm.at[hop_span(ch)],
            dst_ref=xbuf.at[side, z, hop_span(ch)],
            send_sem=x_send,
            recv_sem=ag_recv.at[side, z, ch],
            device_id={"ctx": far},
            device_id_type=MESH,
        )

    def ag_copy(p, src, ch, send, target, block=None):
        here = xbuf.at[p, src, hop_span(ch)]
        return pltpu.make_async_remote_copy(
            src_ref=here if block is None else block.at[hop_span(ch)],
            dst_ref=here,
            send_sem=send.at[p],
            recv_sem=ag_recv.at[p, src, ch],
            device_id=target,
            device_id_type=MESH,
        )

    def meta_copy(target):
        return pltpu.make_async_remote_copy(
            src_ref=meta_mine,
            dst_ref=meta_ref.at[side],
            send_sem=meta_send,
            recv_sem=meta_recv.at[side],
            device_id={"ctx": target},
            device_id_type=MESH,
        )

    def forward_up(p, src, ch):
        @pl.when(carrier & (src <= z) & (z < TP - 1))
        def _():
            ag_copy(p, src, ch, ag_up, up).start()

    def forward_down(p, src, ch):
        @pl.when(carrier & (src >= z) & (z > 0))
        def _():
            ag_copy(p, src, ch, ag_dn, down).start()

    def forward_partner(p, src, ch):
        @pl.when(carrier)
        def _():
            ag_copy(p, src, ch, ag_pt, {"ctx": partner}).start()

    def forward(p, src, ch):
        forward_up(p, src, ch)
        forward_down(p, src, ch)
        forward_partner(p, src, ch)

    @pl.when(jnp.logical_not(carrier))
    def _():
        for ch in range(HOPS):
            x_copy(ch).start()
        meta_copy(far).start()
        meta_copy(CTX - 1 - c).start()

    @pl.when(carrier & (side == 0))
    def _():
        for ch in range(HOPS):
            @pl.when(z < TP - 1)
            def _():
                ag_copy(0, z, ch, ag_up, up, tok_hbm).start()

            @pl.when(z > 0)
            def _():
                ag_copy(0, z, ch, ag_dn, down, tok_hbm).start()

            ag_copy(0, z, ch, ag_pt, {"ctx": partner}, tok_hbm).start()

    @pl.when(carrier)
    def _():
        meta_copy(partner).start()

    lax.fori_loop(0, TP, begin_weights, 0)
    lax.fori_loop(0, TP, begin_wo, 0)
    tok_copy.start()
    ssq_ref[...] = jnp.zeros_like(ssq_ref)
    acc_ref[...] = jnp.zeros_like(acc_ref)
    r_iota = lax.broadcasted_iota(jnp.int32, (rows, rows), 0)
    c_iota = lax.broadcasted_iota(jnp.int32, (rows, rows), 1)
    diagonal = r_iota == c_iota

    def as_column(row):
        return jnp.sum(jnp.where(diagonal, row, 0.0), axis=1, keepdims=True)

    def prepare_gains():
        gains = ig_ref[...].reshape(1, model) * PRESCALE
        for i in range(TP * HALVES):
            gain_in[i] = gains[:, i * half : (i + 1) * half]

    def prepare_trig(p):
        @pl.when(jnp.logical_not(carrier & (side == p)))
        def _():
            pltpu.make_async_copy(meta_mine, meta_ref.at[p], meta_recv.at[p]).wait()

        lane = lax.broadcasted_iota(jnp.int32, (rows, hd), 1)
        place = jnp.where(lane < hd // 2, lane, lane - hd // 2).astype(F32)
        angles = as_column(meta_ref[p, 0:1].astype(F32)) * jnp.exp(
            place * (-2.0 * math.log(10000.0) / hd)
        )
        cos_ref[p] = jnp.cos(angles)
        sines = jnp.sin(angles)
        sin_ref[p] = jnp.where(lane < hd // 2, -sines, sines)

    def arrive_hop(p, i, ch):
        src = source(i)
        local = carrier & (i == 0) & ((side == p) if p == 0 else True)

        @pl.when(jnp.logical_not(local))
        def _():
            ag_copy(p, src, ch, ag_pt, {"ctx": partner}).wait_recv()

        @pl.when(jnp.logical_not(local) if p == 0 else i > 0)
        def _():
            forward(p, src, ch)

    def arrive(p, i, g):
        for j in range(per_half):
            arrive_hop(p, i, g * per_half + j)

    def arrive_both(p, ch):
        arrive_hop(p, 1, ch)
        arrive_hop(p, 2, ch)

    def begin_second(inner, outer):
        for ch in range(HOPS):
            @pl.when(carrier & (side == 0) & inner)
            def _():
                ag_copy(1, z, ch, ag_pt, {"ctx": partner}).wait_recv()

            @pl.when(jnp.where(z < TP // 2, inner, outer))
            def _():
                forward_up(1, z, ch)

            @pl.when(jnp.where(z < TP // 2, outer, inner))
            def _():
                forward_down(1, z, ch)

            @pl.when(outer)
            def _():
                forward_partner(1, z, ch)

    kv_width = 2 * kv_cols

    def project(p, i, g):
        src = source(i)
        spot = src * HALVES + g
        x_t = xbuf[p, src, pl.ds(pl.multiple_of(g * half, 32), half)].astype(F32)
        ssq_ref[p] += jnp.sum(x_t * x_t, axis=0, keepdims=True)
        xg_ref[...] = (x_t.T * gain_in[spot]).astype(BF16)
        last = (i == TP - 1) & (g == HALVES - 1)
        if p == 0:
            @pl.when(g == 0)
            def _():
                loaded = w_ref.at[pl.ds(pl.multiple_of(src * feat, 64), feat)]
                pltpu.make_async_copy(loaded, loaded, w_sem.at[src]).wait()


        @pl.when(jnp.logical_not(last))
        def _():
            acc_ref[p] += jnp.dot(xg_ref[...], w_ref[half_span(spot)], preferred_element_type=F32)

        @pl.when(last)
        def _():
            acc_ref[p, :, 0:kv_width] += jnp.dot(
                xg_ref[...], w_ref[half_span(spot), 0:kv_width], preferred_element_type=F32
            )

    middle = jnp.logical_not(edge)
    lag = jnp.where(middle, 1, 0)

    def first_gather(step, carry):
        i = step // HALVES
        g = step % HALVES

        @pl.when((edge & (i < TP)) | (middle & (i != 1) & (i < TP - 1)))
        def _():
            arrive(0, jnp.where(middle & (i == 2), TP - 1, i), g)

        @pl.when(middle & (i == 1))
        def _():
            for j in range(per_half):
                arrive_both(0, g * per_half + j)

        @pl.when((g == HALVES - 1) & ((i == 1) | (middle & (i == 2))))
        def _():
            begin_second(i == 1, edge | (i == 2))

        @pl.when(step == 0)
        def _():
            @pl.when(carrier)
            def _():
                own_copy.wait()

            prepare_gains()

        @pl.when((g == 0) & (i == jnp.where(edge, 1, TP)))
        def _():
            prepare_trig(0)

        @pl.when((i >= lag) & (i < TP + lag))
        def _():
            project(0, i - lag, g)

        return carry

    lax.fori_loop(0, (TP + lag) * HALVES, first_gather, 0)

    def kv_copy(p, j):
        here = kvbuf.at[2 * p + side, j]
        return pltpu.make_async_remote_copy(
            src_ref=here,
            dst_ref=here,
            send_sem=kv_send.at[p],
            recv_sem=kv_recv.at[2 * p + side, j],
            device_id={"ctx": far},
            device_id_type=MESH,
        )

    def kv_arrived(block, j):
        there = kvbuf.at[block, j]
        pltpu.make_async_copy(there, there, kv_recv.at[block, j]).wait()

    def attn_copy(p, h):
        here = attn_ref.at[p, kv_heads * core + h]
        return pltpu.make_async_remote_copy(
            src_ref=here,
            dst_ref=here,
            send_sem=at_send.at[p],
            recv_sem=at_recv.at[p],
            device_id={"ctx": partner},
            device_id_type=MESH,
        )

    def attn_wait(p, owner, sem):
        both = attn_ref.at[p, pl.ds(kv_heads * owner, kv_heads)]
        pltpu.make_async_copy(both, both, sem.at[p]).wait()

    def attend(p, ready, late):
        own_block = ready[0]
        first = as_column(meta_ref[p, 1:2].astype(F32)).astype(jnp.int32)

        def hidden(block):
            visible = block * rows + c_iota >= first
            if block == own_block:
                visible = visible & (c_iota <= r_iota)
            bias = jnp.where(visible, 0.0, -1e30)
            return jnp.concatenate([bias, bias], axis=0)

        def score(h, block, bias):
            return bias + lax.dot_general(
                q_ref[h], kvbuf[block, 0, h], (((1,), (1,)), ((), ())), preferred_element_type=F32
            )

        def mix(h, weights, blocks):
            weights = weights.astype(BF16)
            return sum(
                jnp.dot(
                    weights[:, j * rows : (j + 1) * rows], kvbuf[block, 1, h],
                    preferred_element_type=F32,
                )
                for j, block in enumerate(blocks)
            )

        biases = [hidden(block) for block in ready]
        states = []
        for h in range(kv_heads):
            s = jnp.concatenate([score(h, b, bias) for b, bias in zip(ready, biases)], axis=1)
            top = jnp.max(s, axis=1, keepdims=True)
            weights = jnp.exp(s - top)
            states.append((top, jnp.sum(weights, axis=1, keepdims=True), mix(h, weights, ready)))
        if late is not None:
            late_bias = hidden(late)
            kv_arrived(late, 0)
            late_weights = []
            for h in range(kv_heads):
                top, total, mixed = states[h]
                s = score(h, late, late_bias)
                higher = jnp.maximum(top, jnp.max(s, axis=1, keepdims=True))
                fade = jnp.exp(top - higher)
                weights = jnp.exp(s - higher)
                total = total * fade + jnp.sum(weights, axis=1, keepdims=True)
                states[h] = (higher, total, mixed * fade)
                late_weights.append(weights)
            kv_arrived(late, 1)
        for h in range(kv_heads):
            _, total, mixed = states[h]
            if late is not None:
                mixed = mixed + mix(h, late_weights[h], [late])
            mixed = (mixed / total).astype(BF16)
            attn_ref[p, kv_heads * core + h] = jnp.concatenate([mixed[:rows], mixed[rows:]], axis=1)
            attn_copy(p, h).start()

    def attention(p):
        inv = lax.rsqrt(as_column(ssq_ref[p]) * (1.0 / model) + EPSILON) * (1.0 / PRESCALE)

        def normed_rotated(raw, gain_vec):
            raw = raw * inv
            scaled = raw * lax.rsqrt(jnp.mean(raw * raw, axis=1, keepdims=True) + EPSILON) * gain_vec
            return scaled * cos_ref[p] + pltpu.roll(scaled, hd // 2, 1) * sin_ref[p]

        block = 2 * p + side
        for h in range(kv_heads):
            cols = slice(h * hd, (h + 1) * hd)
            kvbuf[block, 0, h] = normed_rotated(acc_ref[p, :, cols], kg_ref[...]).astype(BF16)

        @pl.when((p == 0) | (side == 0))
        def _():
            kv_copy(p, 0).start()

        for h in range(kv_heads):
            cols = slice(kv_cols + h * hd, kv_cols + (h + 1) * hd)
            kvbuf[block, 1, h] = (acc_ref[p, :, cols] * inv).astype(BF16)

        @pl.when((p == 0) | (side == 0))
        def _():
            kv_copy(p, 1).start()

        spot = source(TP - 1) * HALVES + HALVES - 1
        acc_ref[p, :, kv_width:] += jnp.dot(
            xg_ref[...], w_ref[half_span(spot), kv_width:], preferred_element_type=F32
        )
        for h in range(q_heads):
            cols = slice(kv_width + h * hd, kv_width + (h + 1) * hd)
            q_ref[h // 2, (h % 2) * rows : (h % 2 + 1) * rows] = (
                normed_rotated(acc_ref[p, :, cols], qg_ref[...]) * (D // H) ** (-0.5)
            ).astype(BF16)

        if p == 0:
            @pl.when(middle)
            def _():
                for ch in range(HOPS):
                    arrive_both(1, ch)

                def own_block(g, carry):
                    arrive(1, 0, g)
                    project(1, 0, g)
                    return carry

                lax.fori_loop(0, HALVES, own_block, 0)
        else:
            sum_terms(0, 2, TP - 1)

        @pl.when(side == 0)
        def _():
            if p == 1:
                for j in range(2):
                    kv_arrived(1, j)
            attend(p, [2 * p, *range(2 * p)], None)

        @pl.when(side == 1)
        def _():
            attend(p, [2 * p + 1, *range(2 * p)], 2 * p)

    def rs_copy(p, dest, ch, buf, recv, target):
        start = pl.multiple_of(turn_of(dest) * extra + ch * chunk, 16)
        return pltpu.make_async_remote_copy(
            src_ref=part.at[p, dest, pl.ds(start, chunk)],
            dst_ref=buf.at[p, dest, pl.ds(pl.multiple_of(ch * chunk, 16), chunk)],
            send_sem=rs_send.at[p],
            recv_sem=recv.at[p, dest, ch],
            device_id=target,
            device_id_type=MESH,
        )

    def rs_up(p, dest, ch):
        return rs_copy(p, dest, ch, rup, rs_up_recv, up)

    def rs_dn(p, dest, ch):
        return rs_copy(p, dest, ch, rdn, rs_dn_recv, down)

    def output_terms(p):
        def half_product(dest, owner):
            span = pl.ds(pl.multiple_of(owner * q_cols, 128), q_cols)
            mixed = jnp.concatenate(
                [attn_ref[p, kv_heads * owner + j] for j in range(kv_heads)], axis=1
            )
            return jnp.dot(mixed, wo_ref[dest, span], preferred_element_type=F32)

        def send_term(dest, term):
            part[p, dest] = term.T.astype(BF16)
            for ch in range(RS_CHUNKS):
                @pl.when((z == 0) & (dest > 0))
                def _():
                    rs_up(p, dest, ch).start()

                @pl.when((z == TP - 1) & (dest < TP - 1))
                def _():
                    rs_dn(p, dest, ch).start()

        first = out_order(0)
        if p == 0:
            wo_copy(first).wait()
        near = half_product(first, core)
        attn_wait(p, 1 - core, at_recv)
        send_term(first, near + half_product(first, 1 - core))

        def out_step(i, carry):
            dest = out_order(i)
            if p == 0:
                wo_copy(dest).wait()
            mixed = jnp.concatenate([attn_ref[p, j] for j in range(2 * kv_heads)], axis=1)
            send_term(dest, jnp.dot(mixed, wo_ref[dest], preferred_element_type=F32))
            return carry

        lax.fori_loop(1, TP, out_step, 0)
        own[p] = part[p, z, pl.ds(pl.multiple_of(turn_of(z) * extra, 16), half)].astype(F32)

    def fin_copy(p, ch):
        span = pl.ds(pl.multiple_of(ch * chunk, 16), chunk)
        return pltpu.make_async_remote_copy(
            src_ref=fin_mine.at[p, span],
            dst_ref=fin_ref.at[core, span],
            send_sem=fin_send.at[p],
            recv_sem=fin_recv.at[core, ch],
            device_id={"ctx": 2 * p + side},
            device_id_type=MESH,
        )

    def sq_copy(p, d):
        return pltpu.make_async_remote_copy(
            src_ref=sq_mine.at[p],
            dst_ref=sq_all.at[HALVES * z + core],
            send_sem=sq_send.at[p],
            recv_sem=sq_recv,
            device_id={"ctx": 2 * p + side, "tp": lax.rem(z + d, TP)},
            device_id_type=MESH,
        )

    def sum_terms(p, begin, end):
        mine = c == 2 * p + side

        def sum_step(k, carry):
            from_low = z + TP - 1 - k
            from_high = z + k - (TP - 1)
            for ch in range(RS_CHUNKS):
                span = slice(ch * chunk, (ch + 1) * chunk)
                low = (z > 0) & (from_low < TP)
                high = (z < TP - 1) & (from_high >= 0)
                for dest, has, buf, copy in (
                    (from_high, high & (z == 1), rdn, rs_dn),
                    (from_low, low, rup, rs_up),
                    (from_high, high & (z != 1), rdn, rs_dn),
                ):
                    @pl.when(has)
                    def _():
                        copy(p, dest, ch).wait_recv()

                        @pl.when(dest != z)
                        def _():
                            start = pl.multiple_of(turn_of(dest) * extra + ch * chunk, 16)
                            there = pl.ds(start, chunk)
                            part[p, dest, there] = (
                                part[p, dest, there].astype(F32) + buf[p, dest, span].astype(F32)
                            ).astype(BF16)
                            copy(p, dest, ch).start()

                        @pl.when(dest == z)
                        def _():
                            own[p, span] += buf[p, dest, span].astype(F32)

                @pl.when(k == TP - 1)
                def _():
                    rounded = own[p, span].astype(BF16)

                    @pl.when(mine)
                    def _():
                        fin_ref[core, span] = rounded

                    @pl.when(jnp.logical_not(mine))
                    def _():
                        fin_mine[p, span] = rounded
                        fin_copy(p, ch).start()

            return carry

        lax.fori_loop(begin, end, sum_step, 0)

    def pair_copy():
        return pltpu.make_async_remote_copy(
            src_ref=sq_mine.at[0],
            dst_ref=sq_pair.at[core],
            send_sem=sq_send.at[0],
            recv_sem=pair_recv,
            device_id={"ctx": 1},
            device_id_type=MESH,
        )

    def share_copy(d):
        return pltpu.make_async_remote_copy(
            src_ref=sq_sum,
            dst_ref=sq_all.at[z],
            send_sem=share_send,
            recv_sem=sq_recv,
            device_id={"tp": lax.rem(z + d, TP)},
            device_id_type=MESH,
        )

    def send_squares(p):
        mine = c == 2 * p + side
        as_row = jnp.sum(own[p] * own[p], axis=0, keepdims=True)
        sq_mine[p] = jnp.broadcast_to(as_row, sq_mine.shape[1:])

        @pl.when(mine)
        def _():
            sq_all[HALVES * z + core] = sq_mine[p]

        def send_direct():
            @pl.when(jnp.logical_not(mine))
            def _():
                sq_copy(p, 0).start()

            for d in range(1, TP):
                sq_copy(p, d).start()

        if p == 0:
            pl.when(side == 0)(send_direct)

            @pl.when(side == 1)
            def _():
                pair_copy().start()
        else:
            send_direct()

    attention(0)

    @pl.when(middle)
    def _():
        for g in range(HALVES):
            arrive(1, TP - 1, g)

    output_terms(0)
    prepare_trig(1)
    before_sums = HALVES * jnp.where(side == 0, BEFORE_0, BEFORE_1)

    def second_gather(step, carry):
        i = step // HALVES
        g = step % HALVES

        @pl.when(step == before_sums)
        def _():
            sum_terms(0, 1, 2)

        @pl.when(edge)
        def _():
            arrive(1, i, g)

        project(1, i, g)
        return carry

    lax.fori_loop(jnp.where(edge, 0, HALVES), TP * HALVES, second_gather, 0)
    attention(1)
    output_terms(1)
    sum_terms(0, TP - 1, TP)
    send_squares(0)
    post_gains = pg_ref[...].reshape(1, model)
    for i in range(TP):
        gain_post[i] = post_gains[:, i * feat : (i + 1) * feat]
    gain_out[...] = jnp.broadcast_to(gain_post[z], (rows, feat)).T
    sum_terms(1, 1, TP - 1)

    def landed(whole, sem):
        pltpu.make_async_copy(whole, whole, sem).wait()

    tok_copy.wait()

    @pl.when(jnp.logical_not(carrier))
    def _():
        landed(tok_ref, x_send)
        landed(meta_ref, meta_send)

    @pl.when(carrier)
    def _():
        landed(meta_mine, meta_send)

    for p in range(PHASES):
        @pl.when(carrier)
        def _():
            for n in range(1, TP):
                @pl.when(z == n - 1)
                def _():
                    landed(xbuf.at[p, 0:n], ag_up.at[p])

                @pl.when(z == TP - n)
                def _():
                    landed(xbuf.at[p, 0:n], ag_dn.at[p])

            landed(xbuf.at[p], ag_pt.at[p])

        @pl.when((p == 0) | (side == 0))
        def _():
            landed(kvbuf.at[2 * p + side], kv_send.at[p])

        attn_wait(p, core, at_send)

    sum_terms(1, TP - 1, TP)
    send_squares(1)

    for p in range(PHASES):
        landed(rup.at[p, 0 : TP - 1], rs_send.at[p])

    source_side = c % 2

    @pl.when(c == 1)
    def _():
        landed(sq_pair, pair_recv)
        sq_sum[...] = sq_pair[0] + sq_pair[1]
        for d in range(1, TP):
            share_copy(d).start()
        sq_all[z] = sq_sum[...]
        sq_all[TP:] = jnp.zeros((TP * HALVES - TP, *sq_sum.shape), F32)

    for kk in range(HALVES):
        for ch in range(RS_CHUNKS):
            @pl.when(2 * source_side + kk != c)
            def _():
                landed(fin_ref.at[kk, slice(ch * chunk, (ch + 1) * chunk)], fin_recv.at[kk, ch])

            span = slice(kk * half + ch * chunk, kk * half + (ch + 1) * chunk)
            gain_out[span] = fin_ref[kk, ch * chunk : (ch + 1) * chunk].astype(F32) * gain_out[span]

    @pl.when(carrier)
    def _():
        landed(sq_all.at[0 : TP * HALVES - 1], sq_recv)

    @pl.when(c == 1)
    def _():
        landed(sq_all.at[0 : TP - 1], sq_recv)

    @pl.when(c == 2)
    def _():
        landed(sq_all, sq_recv)

    total = jnp.sum(sq_all[...], axis=0)[0:1]
    inv_post = lax.rsqrt(total * (1.0 / model) + EPSILON)
    out_ref[...] = (tok_ref[...].astype(F32) + gain_out[...] * inv_post).astype(BF16)

    for p in range(PHASES):
        paired = (side == 1) if p == 0 else False

        @pl.when(c != 2 * p + side)
        def _():
            landed(fin_mine.at[p], fin_send.at[p])

            @pl.when(jnp.logical_not(paired))
            def _():
                landed(sq_all.at[0:TP], sq_send.at[p])

        @pl.when(paired)
        def _():
            landed(sq_mine.at[0], sq_send.at[0])

        @pl.when(c == 2 * p + side)
        def _():
            landed(sq_all.at[0 : TP - 1], sq_send.at[p])

    @pl.when(c == 1)
    def _():
        landed(sq_all.at[0 : TP - 1], share_send)


def per_device_fused(
    tokens, positions, first_key, input_gain, query_weight, kv_weight, query_gain, key_gain,
    out_weight, post_gain,
):
    feat, rows = tokens.shape[1], tokens.shape[0]
    half = feat // HALVES
    hd = query_gain.shape[0]
    model = query_weight.shape[0]
    q_cols = query_weight.shape[1] // 2
    kv_cols = kv_weight.shape[2] // 2
    kv_heads = kv_cols // hd
    wide = half + 128 - half % 128
    vmem = pl.BlockSpec(memory_space=pltpu.VMEM)
    anywhere = pl.BlockSpec(memory_space=pl.ANY)
    dma = pltpu.SemaphoreType.DMA
    return pl.pallas_call(
        fused_kernel,
        out_shape=pltpu.VMEM((feat, rows), BF16),
        in_specs=[vmem] * 6 + [anywhere] * 4,
        out_specs=vmem,
        scratch_shapes=[
            pltpu.VMEM((feat, rows), BF16),
            pltpu.VMEM((PHASES, TP, feat, rows), BF16),
            pltpu.VMEM((rows, half), BF16),
            pltpu.VMEM((model, q_cols + 2 * kv_cols), BF16),
            pltpu.VMEM((TP, 2 * q_cols, wide), BF16),
            pltpu.VMEM((TP * HALVES, 1, half), F32),
            pltpu.VMEM((TP, 1, feat), F32),
            pltpu.VMEM((feat, rows), F32),
            pltpu.VMEM((PHASES, 1, rows), F32),
            pltpu.VMEM((PHASES, rows, q_cols + 2 * kv_cols), F32),
            pltpu.VMEM((PHASES, rows, hd), F32),
            pltpu.VMEM((PHASES, rows, hd), F32),
            pltpu.VMEM((8, rows), jnp.int32),
            pltpu.VMEM((PHASES, 8, rows), jnp.int32),
            pltpu.VMEM((CTX, 2, kv_heads, rows, hd), BF16),
            pltpu.VMEM((kv_heads, 2 * rows, hd), BF16),
            pltpu.VMEM((PHASES, 2 * kv_heads, rows, 2 * hd), BF16),
            pltpu.VMEM((PHASES, TP, wide, rows), BF16),
            pltpu.VMEM((PHASES, TP, half, rows), BF16),
            pltpu.VMEM((PHASES, TP, half, rows), BF16),
            pltpu.VMEM((PHASES, half, rows), F32),
            pltpu.VMEM((PHASES, half, rows), BF16),
            pltpu.VMEM((HALVES, half, rows), BF16),
            pltpu.VMEM((PHASES, 8, rows), F32),
            pltpu.VMEM((TP * HALVES, 8, rows), F32),
            pltpu.VMEM((HALVES, 8, rows), F32),
            pltpu.VMEM((8, rows), F32),
            dma,
            dma,
            dma((TP,)),
            dma((TP,)),
            dma,
            dma((PHASES,)),
            dma((PHASES,)),
            dma((PHASES,)),
            dma((PHASES, TP, HOPS)),
            dma,
            dma((PHASES,)),
            dma((PHASES,)),
            dma((CTX, 2)),
            dma((PHASES,)),
            dma((PHASES,)),
            dma((PHASES,)),
            dma((PHASES, TP, RS_CHUNKS)),
            dma((PHASES, TP, RS_CHUNKS)),
            dma((PHASES,)),
            dma((HALVES, RS_CHUNKS)),
            dma((PHASES,)),
            dma,
            dma,
            dma,
        ],
        compiler_params=pltpu.CompilerParams(
            collective_id=0, has_side_effects=True, vmem_limit_bytes=56 * 1024 * 1024
        ),
    )(
        positions.reshape(1, rows),
        first_key.reshape(1, rows),
        input_gain,
        query_gain.reshape(1, hd),
        key_gain.reshape(1, hd),
        post_gain,
        tokens.T,
        query_weight,
        kv_weight,
        out_weight,
    ).T


def solution(mesh):
    fused = mesh.shape["tp"] == TP and mesh.shape["ctx"] == CTX
    return jax.shard_map(
        per_device_fused if fused else per_device,
        mesh=mesh,
        in_specs=(
            P(("group", "ctx"), "tp"),
            P(("group", "ctx")),
            P(("group", "ctx")),
            P(),
            P(None, "tp"),
            P(None, None, "tp"),
            P(),
            P(),
            P("tp", None),
            P(),
        ),
        out_specs=P(("group", "ctx"), "tp"),
        check_vma=False,
    )
```

```python
import math

import jax
import jax.numpy as jnp
from jax import lax
from jax.experimental import pallas as pl
from jax.experimental.pallas import tpu as pltpu
from jax.sharding import PartitionSpec as P

D = 5376
H = 32
WINDOW = 1024


EPSILON = 1e-06


def from_partner(array, axis, distance):
    return lax.ppermute(array, axis, [(i, i ^ 1 << distance) for i in range(lax.axis_size(axis))])


def passed_along(block, axis, distance):
    devices = range(lax.axis_size(axis))
    route = [(i - distance, i) for i in devices if i - distance in devices]
    return lax.ppermute(block, axis, route)


def rms_norm(values, gain_vec):
    return (
        values * lax.rsqrt(jnp.mean(values * values, axis=-1, keepdims=True) + EPSILON) * gain_vec
    )


def rotate(values, positions_in):
    half_dim = values.shape[-1] // 2
    frequency = jnp.exp(
        jnp.arange(half_dim, dtype=jnp.float32) * (-2.0 * math.log(10000.0) / values.shape[-1])
    )
    angles = positions_in.astype(jnp.float32)[:, None] * frequency[None, :]
    cosines = jnp.cos(angles)[:, None, :]
    sine_part = jnp.sin(angles)[:, None, :]
    lower_half = values[..., :half_dim]
    upper_half = values[..., half_dim:]
    return jnp.concatenate(
        [
            lower_half * cosines - upper_half * sine_part,
            upper_half * cosines + lower_half * sine_part,
        ],
        axis=-1,
    )


def per_device(
    tokens,
    positions,
    first_key,
    input_gain,
    query_weight,
    kv_weight,
    query_gain,
    key_gain,
    out_weight,
    post_gain,
):
    tok_rows = tokens.shape[0]
    feat_dev = tokens.shape[1]
    head_dim = query_gain.shape[0]
    heads_dev = query_weight.shape[1] // head_dim
    tp_index = lax.axis_index("tp")
    ctx_index = lax.axis_index("ctx")
    ctx_count = lax.axis_size("ctx")
    local_x = tokens.astype(jnp.float32)
    kv_full = kv_weight
    if heads_dev == 1:
        partner = from_partner(kv_weight, "tp", 0)
        is_even = tp_index % 2 == 0
        kv_full = jnp.where(
            is_even,
            jnp.concatenate([kv_weight, partner], axis=2),
            jnp.concatenate([partner, kv_weight], axis=2),
        )
    gathered = lax.all_gather(tokens, "tp", axis=1, tiled=True).astype(jnp.float32)
    normed = rms_norm(gathered, input_gain).astype(jnp.bfloat16)
    query_raw = jnp.dot(normed, query_weight, preferred_element_type=jnp.float32)
    key_raw = jnp.dot(normed, kv_full[0], preferred_element_type=jnp.float32)
    value_raw = jnp.dot(normed, kv_full[1], preferred_element_type=jnp.float32)
    kv_heads = key_raw.shape[1] // head_dim
    group_size = heads_dev // kv_heads
    queries = (
        rotate(rms_norm(query_raw.reshape(tok_rows, heads_dev, head_dim), query_gain), positions)
        * (D // H) ** (-0.5)
    ).astype(jnp.bfloat16)
    keys = rotate(
        rms_norm(key_raw.reshape(tok_rows, kv_heads, head_dim), key_gain), positions
    ).astype(jnp.bfloat16)
    values_b = value_raw.reshape(tok_rows, kv_heads, head_dim).astype(jnp.bfloat16)
    kv_block = jnp.stack([keys, values_b])
    reach_blocks = min(ctx_count - 1, (WINDOW + tok_rows - 2) // tok_rows)
    received = []
    moving = kv_block
    for offset in range(reach_blocks):
        moving = passed_along(moving, "ctx", 1)
        received.append(moving)
    blocks = received[::-1] + [kv_block]
    keys_all = jnp.concatenate(blocks, axis=1)
    key_count = keys_all.shape[1]
    key_index = (ctx_index - reach_blocks) * tok_rows + jnp.arange(key_count, dtype=jnp.int32)
    query_index = ctx_index * tok_rows + jnp.arange(tok_rows, dtype=jnp.int32)
    visible = (key_index[None, :] >= first_key[:, None]) & (
        key_index[None, :] <= query_index[:, None]
    )
    grouped = queries.reshape(tok_rows, kv_heads, group_size, head_dim)
    scores = jnp.einsum("qkgd,tkd->kgqt", grouped, keys_all[0], preferred_element_type=jnp.float32)
    scores = jnp.where(visible[None, None], scores, -1e30)
    row_max = jnp.max(scores, axis=-1, keepdims=True)
    weights = jnp.exp(scores - row_max)
    denominator = jnp.sum(weights, axis=-1)
    mixed_out = jnp.einsum(
        "kgqt,tkd->qkgd",
        weights.astype(jnp.bfloat16),
        keys_all[1],
        preferred_element_type=jnp.float32,
    )
    mixed_out = mixed_out / jnp.transpose(denominator, (2, 0, 1))[..., None]
    attn = mixed_out.astype(jnp.bfloat16).reshape(tok_rows, heads_dev * head_dim)
    partial_value = jnp.dot(attn, out_weight, preferred_element_type=jnp.float32)
    summed = lax.psum(partial_value.astype(jnp.bfloat16), "tp").astype(jnp.float32)
    post_normed = rms_norm(summed, post_gain)
    own_cols = lax.dynamic_slice_in_dim(post_normed, tp_index * feat_dev, feat_dev, 1)
    return (local_x + own_cols).astype(jnp.bfloat16)


MESH = pl.DeviceIdType.MESH
F32 = jnp.float32
BF16 = jnp.bfloat16
TP = 4
CTX = 4
PHASES = 2
HALVES = 2
HOPS = 4
BEFORE_0 = 1
BEFORE_1 = 2
RS_CHUNKS = 2
PRESCALE = 2.0**-10


def fused_kernel(
    pos_hbm, fk_hbm, ig_hbm, qg_hbm, kg_hbm, pg_hbm, tok_hbm, qw_hbm, kvw_hbm, ow_hbm, out_ref,
    pos_ref, fk_ref, ig_ref, qg_ref, kg_ref, pg_ref, tok_ref, xbuf, xg_ref, w_ref, wo_ref, gain_in, gain_post, gain_out, ssq_ref, acc_ref, cos_ref, sin_ref,
    meta_mine, meta_ref, kvbuf, q_ref, attn_ref, part, rup, rdn, own, fin_mine, fin_ref, sq_mine, sq_all,
    sq_pair, sq_sum,
    in_sem, tok_sem, own_sem, w_sem, wo_sem, x_send, ag_up, ag_dn, ag_pt, ag_recv, meta_send, meta_recv, kv_send, kv_recv,
    at_send, at_recv, rs_send, rs_up_recv, rs_dn_recv, fin_send, fin_recv, sq_send, sq_recv,
    pair_recv, share_send,
):
    feat, rows = tok_ref.shape
    half = feat // HALVES
    hop = feat // HOPS
    per_half = HOPS // HALVES
    chunk = half // RS_CHUNKS
    hd = qg_ref.shape[1]
    kv_heads = kvbuf.shape[2]
    kv_cols = kv_heads * hd
    q_cols = w_ref.shape[1] - 2 * kv_cols
    q_heads = q_cols // hd
    model = feat * TP
    z = lax.axis_index("tp")
    c = lax.axis_index("ctx")
    side = c // 2
    core = c % 2
    carrier = side == core
    partner = c + 1 - 2 * core
    far = lax.rem(c + 2, CTX)
    edge = (z == 0) | (z == TP - 1)
    up = {"tp": lax.rem(z + 1, TP)}
    down = {"tp": lax.rem(z + TP - 1, TP)}

    barrier = pltpu.get_barrier_semaphore()

    @pl.when(z < TP - 1)
    def _():
        pl.semaphore_signal(barrier, inc=1, device_id=up, device_id_type=MESH)

    @pl.when(z > 0)
    def _():
        pl.semaphore_signal(barrier, inc=1, device_id=down, device_id_type=MESH)

    for other in (far, partner, CTX - 1 - c):
        pl.semaphore_signal(barrier, inc=1, device_id={"ctx": other}, device_id_type=MESH)

    pairs = (
        (pos_hbm, pos_ref), (fk_hbm, fk_ref), (ig_hbm, ig_ref),
        (qg_hbm, qg_ref), (kg_hbm, kg_ref), (pg_hbm, pg_ref),
    )
    small = [
        pltpu.make_async_copy(src, dst, in_sem.at[i]) for i, (src, dst) in enumerate(pairs)
    ]
    for copy in small:
        copy.start()

    def half_span(spot):
        return pl.ds(pl.multiple_of(spot * half, 32), half)

    def weight_copies(src):
        span = pl.ds(pl.multiple_of(src * feat, 64), feat)
        kv_from = pl.ds(pl.multiple_of(core * kv_cols, 128), kv_cols)
        q_from = pl.ds(pl.multiple_of(core * q_cols, 128), q_cols)
        return (
            pltpu.make_async_copy(
                kvw_hbm.at[0, span, kv_from], w_ref.at[span, 0:kv_cols], w_sem.at[src]
            ),
            pltpu.make_async_copy(
                kvw_hbm.at[1, span, kv_from], w_ref.at[span, kv_cols : 2 * kv_cols], w_sem.at[src]
            ),
            pltpu.make_async_copy(
                qw_hbm.at[span, q_from], w_ref.at[span, 2 * kv_cols :], w_sem.at[src]
            ),
        )

    def source(i):
        second = jnp.where(z % 2 == 0, 1, 2)
        third = jnp.where(z == 0, 2, jnp.where(z == 1, 0, jnp.where(z == 2, 3, 1)))
        fourth = jnp.where(z < TP // 2, TP - 1, 0)
        return jnp.where(i == 0, z, jnp.where(i == 1, second, jnp.where(i == 2, third, fourth)))

    extra = half % 128
    turns = 128 // extra
    wide = half + 128 - extra

    def turn_of(dest):
        return (dest * HALVES + core) % turns

    def wo_copy(dest):
        start = pl.multiple_of((dest * HALVES + core) * half - turn_of(dest) * extra, 128)
        return pltpu.make_async_copy(ow_hbm.at[:, pl.ds(start, wide)], wo_ref.at[dest], wo_sem.at[dest])

    def out_order(i):
        outer = TP - 1 - i
        inner = jnp.where(i == 0, 3, jnp.where(i == 1, 0, jnp.where(i == 2, 2, 1)))
        dest = jnp.where(edge, outer, inner)
        return jnp.where(z < TP // 2, dest, TP - 1 - dest)

    def begin_weights(i, carry):
        for copy in weight_copies(source(i)):
            copy.start()
        return carry

    def begin_wo(i, carry):
        wo_copy(out_order(i)).start()
        return carry

    small[0].wait()
    small[1].wait()
    meta_mine[0:1] = pos_ref[...]
    meta_mine[1:2] = fk_ref[...]

    tok_copy = pltpu.make_async_copy(tok_hbm, tok_ref, tok_sem)
    own_copy = pltpu.make_async_copy(tok_hbm, xbuf.at[side, z], own_sem)

    @pl.when(carrier)
    def _():
        own_copy.start()
        meta_ref[side] = meta_mine[...]

    pl.semaphore_wait(barrier, jnp.where(edge, 4, 5))

    def hop_span(ch):
        return pl.ds(pl.multiple_of(ch * hop, 16), hop)

    def x_copy(ch):
        return pltpu.make_async_remote_copy(
            src_ref=tok_hbm.at[hop_span(ch)],
            dst_ref=xbuf.at[side, z, hop_span(ch)],
            send_sem=x_send,
            recv_sem=ag_recv.at[side, z, ch],
            device_id={"ctx": far},
            device_id_type=MESH,
        )

    def ag_copy(p, src, ch, send, target, block=None):
        here = xbuf.at[p, src, hop_span(ch)]
        return pltpu.make_async_remote_copy(
            src_ref=here if block is None else block.at[hop_span(ch)],
            dst_ref=here,
            send_sem=send.at[p],
            recv_sem=ag_recv.at[p, src, ch],
            device_id=target,
            device_id_type=MESH,
        )

    def meta_copy(target):
        return pltpu.make_async_remote_copy(
            src_ref=meta_mine,
            dst_ref=meta_ref.at[side],
            send_sem=meta_send,
            recv_sem=meta_recv.at[side],
            device_id={"ctx": target},
            device_id_type=MESH,
        )

    def forward_up(p, src, ch):
        @pl.when(carrier & (src <= z) & (z < TP - 1))
        def _():
            ag_copy(p, src, ch, ag_up, up).start()

    def forward_down(p, src, ch):
        @pl.when(carrier & (src >= z) & (z > 0))
        def _():
            ag_copy(p, src, ch, ag_dn, down).start()

    def forward_partner(p, src, ch):
        @pl.when(carrier)
        def _():
            ag_copy(p, src, ch, ag_pt, {"ctx": partner}).start()

    def forward(p, src, ch):
        forward_up(p, src, ch)
        forward_down(p, src, ch)
        forward_partner(p, src, ch)

    @pl.when(jnp.logical_not(carrier))
    def _():
        for ch in range(HOPS):
            x_copy(ch).start()
        meta_copy(far).start()
        meta_copy(CTX - 1 - c).start()

    @pl.when(carrier & (side == 0))
    def _():
        for ch in range(HOPS):
            @pl.when(z < TP - 1)
            def _():
                ag_copy(0, z, ch, ag_up, up, tok_hbm).start()

            @pl.when(z > 0)
            def _():
                ag_copy(0, z, ch, ag_dn, down, tok_hbm).start()

            ag_copy(0, z, ch, ag_pt, {"ctx": partner}, tok_hbm).start()

    @pl.when(carrier)
    def _():
        meta_copy(partner).start()

    lax.fori_loop(0, TP, begin_weights, 0)
    lax.fori_loop(0, TP, begin_wo, 0)
    tok_copy.start()
    for copy in small[2:]:
        copy.wait()

    ssq_ref[...] = jnp.zeros_like(ssq_ref)
    acc_ref[...] = jnp.zeros_like(acc_ref)
    r_iota = lax.broadcasted_iota(jnp.int32, (rows, rows), 0)
    c_iota = lax.broadcasted_iota(jnp.int32, (rows, rows), 1)
    diagonal = r_iota == c_iota

    def as_column(row):
        return jnp.sum(jnp.where(diagonal, row, 0.0), axis=1, keepdims=True)

    def prepare_gains():
        gains = ig_ref[...].reshape(1, model) * PRESCALE
        for i in range(TP * HALVES):
            gain_in[i] = gains[:, i * half : (i + 1) * half]

    def prepare_trig(p):
        @pl.when(jnp.logical_not(carrier & (side == p)))
        def _():
            pltpu.make_async_copy(meta_mine, meta_ref.at[p], meta_recv.at[p]).wait()

        lane = lax.broadcasted_iota(jnp.int32, (rows, hd), 1)
        place = jnp.where(lane < hd // 2, lane, lane - hd // 2).astype(F32)
        angles = as_column(meta_ref[p, 0:1].astype(F32)) * jnp.exp(
            place * (-2.0 * math.log(10000.0) / hd)
        )
        cos_ref[p] = jnp.cos(angles)
        sines = jnp.sin(angles)
        sin_ref[p] = jnp.where(lane < hd // 2, -sines, sines)

    def arrive_hop(p, i, ch):
        src = source(i)
        local = carrier & (i == 0) & ((side == p) if p == 0 else True)

        @pl.when(jnp.logical_not(local))
        def _():
            ag_copy(p, src, ch, ag_pt, {"ctx": partner}).wait_recv()

        @pl.when(jnp.logical_not(local) if p == 0 else i > 0)
        def _():
            forward(p, src, ch)

    def arrive(p, i, g):
        for j in range(per_half):
            arrive_hop(p, i, g * per_half + j)

    def arrive_both(p, ch):
        arrive_hop(p, 1, ch)
        arrive_hop(p, 2, ch)

    def begin_second(inner, outer):
        for ch in range(HOPS):
            @pl.when(carrier & (side == 0) & inner)
            def _():
                ag_copy(1, z, ch, ag_pt, {"ctx": partner}).wait_recv()

            @pl.when(jnp.where(z < TP // 2, inner, outer))
            def _():
                forward_up(1, z, ch)

            @pl.when(jnp.where(z < TP // 2, outer, inner))
            def _():
                forward_down(1, z, ch)

            @pl.when(outer)
            def _():
                forward_partner(1, z, ch)

    kv_width = 2 * kv_cols

    def project(p, i, g):
        src = source(i)
        spot = src * HALVES + g
        x_t = xbuf[p, src, pl.ds(pl.multiple_of(g * half, 32), half)].astype(F32)
        ssq_ref[p] += jnp.sum(x_t * x_t, axis=0, keepdims=True)
        xg_ref[...] = (x_t.T * gain_in[spot]).astype(BF16)
        last = (i == TP - 1) & (g == HALVES - 1)
        if p == 0:
            @pl.when(g == 0)
            def _():
                loaded = w_ref.at[pl.ds(pl.multiple_of(src * feat, 64), feat)]
                pltpu.make_async_copy(loaded, loaded, w_sem.at[src]).wait()


        @pl.when(jnp.logical_not(last))
        def _():
            acc_ref[p] += jnp.dot(xg_ref[...], w_ref[half_span(spot)], preferred_element_type=F32)

        @pl.when(last)
        def _():
            acc_ref[p, :, 0:kv_width] += jnp.dot(
                xg_ref[...], w_ref[half_span(spot), 0:kv_width], preferred_element_type=F32
            )

    middle = jnp.logical_not(edge)
    lag = jnp.where(middle, 1, 0)

    def first_gather(step, carry):
        i = step // HALVES
        g = step % HALVES

        @pl.when((edge & (i < TP)) | (middle & (i != 1) & (i < TP - 1)))
        def _():
            arrive(0, jnp.where(middle & (i == 2), TP - 1, i), g)

        @pl.when(middle & (i == 1))
        def _():
            for j in range(per_half):
                arrive_both(0, g * per_half + j)

        @pl.when((g == HALVES - 1) & ((i == 1) | (middle & (i == 2))))
        def _():
            begin_second(i == 1, edge | (i == 2))

        @pl.when(step == 0)
        def _():
            @pl.when(carrier)
            def _():
                own_copy.wait()

            prepare_gains()

        @pl.when((g == 0) & (i == jnp.where(edge, 1, TP)))
        def _():
            prepare_trig(0)

        @pl.when((i >= lag) & (i < TP + lag))
        def _():
            project(0, i - lag, g)

        return carry

    lax.fori_loop(0, (TP + lag) * HALVES, first_gather, 0)

    def kv_copy(p, j):
        here = kvbuf.at[2 * p + side, j]
        return pltpu.make_async_remote_copy(
            src_ref=here,
            dst_ref=here,
            send_sem=kv_send.at[p],
            recv_sem=kv_recv.at[2 * p + side, j],
            device_id={"ctx": far},
            device_id_type=MESH,
        )

    def kv_arrived(block, j):
        there = kvbuf.at[block, j]
        pltpu.make_async_copy(there, there, kv_recv.at[block, j]).wait()

    def attn_copy(p, h):
        here = attn_ref.at[p, kv_heads * core + h]
        return pltpu.make_async_remote_copy(
            src_ref=here,
            dst_ref=here,
            send_sem=at_send.at[p],
            recv_sem=at_recv.at[p],
            device_id={"ctx": partner},
            device_id_type=MESH,
        )

    def attn_wait(p, owner, sem):
        both = attn_ref.at[p, pl.ds(kv_heads * owner, kv_heads)]
        pltpu.make_async_copy(both, both, sem.at[p]).wait()

    def attend(p, ready, late):
        own_block = ready[0]
        first = as_column(meta_ref[p, 1:2].astype(F32)).astype(jnp.int32)

        def hidden(block):
            visible = block * rows + c_iota >= first
            if block == own_block:
                visible = visible & (c_iota <= r_iota)
            bias = jnp.where(visible, 0.0, -1e30)
            return jnp.concatenate([bias, bias], axis=0)

        def score(h, block, bias):
            return bias + lax.dot_general(
                q_ref[h], kvbuf[block, 0, h], (((1,), (1,)), ((), ())), preferred_element_type=F32
            )

        def mix(h, weights, blocks):
            weights = weights.astype(BF16)
            return sum(
                jnp.dot(
                    weights[:, j * rows : (j + 1) * rows], kvbuf[block, 1, h],
                    preferred_element_type=F32,
                )
                for j, block in enumerate(blocks)
            )

        biases = [hidden(block) for block in ready]
        states = []
        for h in range(kv_heads):
            s = jnp.concatenate([score(h, b, bias) for b, bias in zip(ready, biases)], axis=1)
            top = jnp.max(s, axis=1, keepdims=True)
            weights = jnp.exp(s - top)
            states.append((top, jnp.sum(weights, axis=1, keepdims=True), mix(h, weights, ready)))
        if late is not None:
            late_bias = hidden(late)
            kv_arrived(late, 0)
            late_weights = []
            for h in range(kv_heads):
                top, total, mixed = states[h]
                s = score(h, late, late_bias)
                higher = jnp.maximum(top, jnp.max(s, axis=1, keepdims=True))
                fade = jnp.exp(top - higher)
                weights = jnp.exp(s - higher)
                total = total * fade + jnp.sum(weights, axis=1, keepdims=True)
                states[h] = (higher, total, mixed * fade)
                late_weights.append(weights)
            kv_arrived(late, 1)
        for h in range(kv_heads):
            _, total, mixed = states[h]
            if late is not None:
                mixed = mixed + mix(h, late_weights[h], [late])
            mixed = (mixed / total).astype(BF16)
            attn_ref[p, kv_heads * core + h] = jnp.concatenate([mixed[:rows], mixed[rows:]], axis=1)
            attn_copy(p, h).start()

    def attention(p):
        inv = lax.rsqrt(as_column(ssq_ref[p]) * (1.0 / model) + EPSILON) * (1.0 / PRESCALE)

        def normed_rotated(raw, gain_vec):
            raw = raw * inv
            scaled = raw * lax.rsqrt(jnp.mean(raw * raw, axis=1, keepdims=True) + EPSILON) * gain_vec
            return scaled * cos_ref[p] + pltpu.roll(scaled, hd // 2, 1) * sin_ref[p]

        block = 2 * p + side
        for h in range(kv_heads):
            cols = slice(h * hd, (h + 1) * hd)
            kvbuf[block, 0, h] = normed_rotated(acc_ref[p, :, cols], kg_ref[...]).astype(BF16)

        @pl.when((p == 0) | (side == 0))
        def _():
            kv_copy(p, 0).start()

        for h in range(kv_heads):
            cols = slice(kv_cols + h * hd, kv_cols + (h + 1) * hd)
            kvbuf[block, 1, h] = (acc_ref[p, :, cols] * inv).astype(BF16)

        @pl.when((p == 0) | (side == 0))
        def _():
            kv_copy(p, 1).start()

        spot = source(TP - 1) * HALVES + HALVES - 1
        acc_ref[p, :, kv_width:] += jnp.dot(
            xg_ref[...], w_ref[half_span(spot), kv_width:], preferred_element_type=F32
        )
        for h in range(q_heads):
            cols = slice(kv_width + h * hd, kv_width + (h + 1) * hd)
            q_ref[h // 2, (h % 2) * rows : (h % 2 + 1) * rows] = (
                normed_rotated(acc_ref[p, :, cols], qg_ref[...]) * (D // H) ** (-0.5)
            ).astype(BF16)

        if p == 0:
            @pl.when(middle)
            def _():
                for ch in range(HOPS):
                    arrive_both(1, ch)

                def own_block(g, carry):
                    arrive(1, 0, g)
                    project(1, 0, g)
                    return carry

                lax.fori_loop(0, HALVES, own_block, 0)
        else:
            sum_terms(0, 2, TP - 1)

        @pl.when(side == 0)
        def _():
            if p == 1:
                for j in range(2):
                    kv_arrived(1, j)
            attend(p, [2 * p, *range(2 * p)], None)

        @pl.when(side == 1)
        def _():
            attend(p, [2 * p + 1, *range(2 * p)], 2 * p)

    def rs_copy(p, dest, ch, buf, recv, target):
        start = pl.multiple_of(turn_of(dest) * extra + ch * chunk, 16)
        return pltpu.make_async_remote_copy(
            src_ref=part.at[p, dest, pl.ds(start, chunk)],
            dst_ref=buf.at[p, dest, pl.ds(pl.multiple_of(ch * chunk, 16), chunk)],
            send_sem=rs_send.at[p],
            recv_sem=recv.at[p, dest, ch],
            device_id=target,
            device_id_type=MESH,
        )

    def rs_up(p, dest, ch):
        return rs_copy(p, dest, ch, rup, rs_up_recv, up)

    def rs_dn(p, dest, ch):
        return rs_copy(p, dest, ch, rdn, rs_dn_recv, down)

    def output_terms(p):
        def half_product(dest, owner):
            span = pl.ds(pl.multiple_of(owner * q_cols, 128), q_cols)
            mixed = jnp.concatenate(
                [attn_ref[p, kv_heads * owner + j] for j in range(kv_heads)], axis=1
            )
            return jnp.dot(mixed, wo_ref[dest, span], preferred_element_type=F32)

        def send_term(dest, term):
            part[p, dest] = term.T.astype(BF16)
            for ch in range(RS_CHUNKS):
                @pl.when((z == 0) & (dest > 0))
                def _():
                    rs_up(p, dest, ch).start()

                @pl.when((z == TP - 1) & (dest < TP - 1))
                def _():
                    rs_dn(p, dest, ch).start()

        first = out_order(0)
        if p == 0:
            wo_copy(first).wait()
        near = half_product(first, core)
        attn_wait(p, 1 - core, at_recv)
        send_term(first, near + half_product(first, 1 - core))

        def out_step(i, carry):
            dest = out_order(i)
            if p == 0:
                wo_copy(dest).wait()
            mixed = jnp.concatenate([attn_ref[p, j] for j in range(2 * kv_heads)], axis=1)
            send_term(dest, jnp.dot(mixed, wo_ref[dest], preferred_element_type=F32))
            return carry

        lax.fori_loop(1, TP, out_step, 0)
        own[p] = part[p, z, pl.ds(pl.multiple_of(turn_of(z) * extra, 16), half)].astype(F32)

    def fin_copy(p, ch):
        span = pl.ds(pl.multiple_of(ch * chunk, 16), chunk)
        return pltpu.make_async_remote_copy(
            src_ref=fin_mine.at[p, span],
            dst_ref=fin_ref.at[core, span],
            send_sem=fin_send.at[p],
            recv_sem=fin_recv.at[core, ch],
            device_id={"ctx": 2 * p + side},
            device_id_type=MESH,
        )

    def sq_copy(p, d):
        return pltpu.make_async_remote_copy(
            src_ref=sq_mine.at[p],
            dst_ref=sq_all.at[HALVES * z + core],
            send_sem=sq_send.at[p],
            recv_sem=sq_recv,
            device_id={"ctx": 2 * p + side, "tp": lax.rem(z + d, TP)},
            device_id_type=MESH,
        )

    def sum_terms(p, begin, end):
        mine = c == 2 * p + side

        def sum_step(k, carry):
            from_low = z + TP - 1 - k
            from_high = z + k - (TP - 1)
            for ch in range(RS_CHUNKS):
                span = slice(ch * chunk, (ch + 1) * chunk)
                low = (z > 0) & (from_low < TP)
                high = (z < TP - 1) & (from_high >= 0)
                for dest, has, buf, copy in (
                    (from_high, high & (z == 1), rdn, rs_dn),
                    (from_low, low, rup, rs_up),
                    (from_high, high & (z != 1), rdn, rs_dn),
                ):
                    @pl.when(has)
                    def _():
                        copy(p, dest, ch).wait_recv()

                        @pl.when(dest != z)
                        def _():
                            start = pl.multiple_of(turn_of(dest) * extra + ch * chunk, 16)
                            there = pl.ds(start, chunk)
                            part[p, dest, there] = (
                                part[p, dest, there].astype(F32) + buf[p, dest, span].astype(F32)
                            ).astype(BF16)
                            copy(p, dest, ch).start()

                        @pl.when(dest == z)
                        def _():
                            own[p, span] += buf[p, dest, span].astype(F32)

                @pl.when(k == TP - 1)
                def _():
                    rounded = own[p, span].astype(BF16)

                    @pl.when(mine)
                    def _():
                        fin_ref[core, span] = rounded

                    @pl.when(jnp.logical_not(mine))
                    def _():
                        fin_mine[p, span] = rounded
                        fin_copy(p, ch).start()

            return carry

        lax.fori_loop(begin, end, sum_step, 0)

    def pair_copy():
        return pltpu.make_async_remote_copy(
            src_ref=sq_mine.at[0],
            dst_ref=sq_pair.at[core],
            send_sem=sq_send.at[0],
            recv_sem=pair_recv,
            device_id={"ctx": 1},
            device_id_type=MESH,
        )

    def share_copy(d):
        return pltpu.make_async_remote_copy(
            src_ref=sq_sum,
            dst_ref=sq_all.at[z],
            send_sem=share_send,
            recv_sem=sq_recv,
            device_id={"tp": lax.rem(z + d, TP)},
            device_id_type=MESH,
        )

    def send_squares(p):
        mine = c == 2 * p + side
        as_row = jnp.sum(own[p] * own[p], axis=0, keepdims=True)
        sq_mine[p] = jnp.broadcast_to(as_row, sq_mine.shape[1:])

        @pl.when(mine)
        def _():
            sq_all[HALVES * z + core] = sq_mine[p]

        def send_direct():
            @pl.when(jnp.logical_not(mine))
            def _():
                sq_copy(p, 0).start()

            for d in range(1, TP):
                sq_copy(p, d).start()

        if p == 0:
            pl.when(side == 0)(send_direct)

            @pl.when(side == 1)
            def _():
                pair_copy().start()
        else:
            send_direct()

    attention(0)

    @pl.when(middle)
    def _():
        for g in range(HALVES):
            arrive(1, TP - 1, g)

    output_terms(0)
    prepare_trig(1)
    before_sums = HALVES * jnp.where(side == 0, BEFORE_0, BEFORE_1)

    def second_gather(step, carry):
        i = step // HALVES
        g = step % HALVES

        @pl.when(step == before_sums)
        def _():
            sum_terms(0, 1, 2)

        @pl.when(edge)
        def _():
            arrive(1, i, g)

        project(1, i, g)
        return carry

    lax.fori_loop(jnp.where(edge, 0, HALVES), TP * HALVES, second_gather, 0)
    attention(1)
    output_terms(1)
    sum_terms(0, TP - 1, TP)
    send_squares(0)
    post_gains = pg_ref[...].reshape(1, model)
    for i in range(TP):
        gain_post[i] = post_gains[:, i * feat : (i + 1) * feat]
    gain_out[...] = jnp.broadcast_to(gain_post[z], (rows, feat)).T
    sum_terms(1, 1, TP - 1)

    def landed(whole, sem):
        pltpu.make_async_copy(whole, whole, sem).wait()

    tok_copy.wait()

    @pl.when(jnp.logical_not(carrier))
    def _():
        landed(tok_ref, x_send)
        landed(meta_ref, meta_send)

    @pl.when(carrier)
    def _():
        landed(meta_mine, meta_send)

    for p in range(PHASES):
        @pl.when(carrier)
        def _():
            for n in range(1, TP):
                @pl.when(z == n - 1)
                def _():
                    landed(xbuf.at[p, 0:n], ag_up.at[p])

                @pl.when(z == TP - n)
                def _():
                    landed(xbuf.at[p, 0:n], ag_dn.at[p])

            landed(xbuf.at[p], ag_pt.at[p])

        @pl.when((p == 0) | (side == 0))
        def _():
            landed(kvbuf.at[2 * p + side], kv_send.at[p])

        attn_wait(p, core, at_send)

    sum_terms(1, TP - 1, TP)
    send_squares(1)

    for p in range(PHASES):
        landed(rup.at[p, 0 : TP - 1], rs_send.at[p])

    source_side = c % 2

    @pl.when(c == 1)
    def _():
        landed(sq_pair, pair_recv)
        sq_sum[...] = sq_pair[0] + sq_pair[1]
        for d in range(1, TP):
            share_copy(d).start()
        sq_all[z] = sq_sum[...]
        sq_all[TP:] = jnp.zeros((TP * HALVES - TP, *sq_sum.shape), F32)

    for kk in range(HALVES):
        for ch in range(RS_CHUNKS):
            @pl.when(2 * source_side + kk != c)
            def _():
                landed(fin_ref.at[kk, slice(ch * chunk, (ch + 1) * chunk)], fin_recv.at[kk, ch])

            span = slice(kk * half + ch * chunk, kk * half + (ch + 1) * chunk)
            gain_out[span] = fin_ref[kk, ch * chunk : (ch + 1) * chunk].astype(F32) * gain_out[span]

    @pl.when(carrier)
    def _():
        landed(sq_all.at[0 : TP * HALVES - 1], sq_recv)

    @pl.when(c == 1)
    def _():
        landed(sq_all.at[0 : TP - 1], sq_recv)

    @pl.when(c == 2)
    def _():
        landed(sq_all, sq_recv)

    total = jnp.sum(sq_all[...], axis=0)[0:1]
    inv_post = lax.rsqrt(total * (1.0 / model) + EPSILON)
    out_ref[...] = (tok_ref[...].astype(F32) + gain_out[...] * inv_post).astype(BF16)

    for p in range(PHASES):
        paired = (side == 1) if p == 0 else False

        @pl.when(c != 2 * p + side)
        def _():
            landed(fin_mine.at[p], fin_send.at[p])

            @pl.when(jnp.logical_not(paired))
            def _():
                landed(sq_all.at[0:TP], sq_send.at[p])

        @pl.when(paired)
        def _():
            landed(sq_mine.at[0], sq_send.at[0])

        @pl.when(c == 2 * p + side)
        def _():
            landed(sq_all.at[0 : TP - 1], sq_send.at[p])

    @pl.when(c == 1)
    def _():
        landed(sq_all.at[0 : TP - 1], share_send)


def per_device_fused(
    tokens, positions, first_key, input_gain, query_weight, kv_weight, query_gain, key_gain,
    out_weight, post_gain,
):
    feat, rows = tokens.shape[1], tokens.shape[0]
    half = feat // HALVES
    hd = query_gain.shape[0]
    model = query_weight.shape[0]
    q_cols = query_weight.shape[1] // 2
    kv_cols = kv_weight.shape[2] // 2
    kv_heads = kv_cols // hd
    wide = half + 128 - half % 128
    vmem = pl.BlockSpec(memory_space=pltpu.VMEM)
    anywhere = pl.BlockSpec(memory_space=pl.ANY)
    dma = pltpu.SemaphoreType.DMA
    return pl.pallas_call(
        fused_kernel,
        out_shape=pltpu.VMEM((feat, rows), BF16),
        in_specs=[anywhere] * 10,
        out_specs=vmem,
        scratch_shapes=[
            pltpu.VMEM((1, rows), jnp.int32),
            pltpu.VMEM((1, rows), jnp.int32),
            pltpu.VMEM((model,), F32),
            pltpu.VMEM((1, hd), F32),
            pltpu.VMEM((1, hd), F32),
            pltpu.VMEM((model,), F32),
            pltpu.VMEM((feat, rows), BF16),
            pltpu.VMEM((PHASES, TP, feat, rows), BF16),
            pltpu.VMEM((rows, half), BF16),
            pltpu.VMEM((model, q_cols + 2 * kv_cols), BF16),
            pltpu.VMEM((TP, 2 * q_cols, wide), BF16),
            pltpu.VMEM((TP * HALVES, 1, half), F32),
            pltpu.VMEM((TP, 1, feat), F32),
            pltpu.VMEM((feat, rows), F32),
            pltpu.VMEM((PHASES, 1, rows), F32),
            pltpu.VMEM((PHASES, rows, q_cols + 2 * kv_cols), F32),
            pltpu.VMEM((PHASES, rows, hd), F32),
            pltpu.VMEM((PHASES, rows, hd), F32),
            pltpu.VMEM((8, rows), jnp.int32),
            pltpu.VMEM((PHASES, 8, rows), jnp.int32),
            pltpu.VMEM((CTX, 2, kv_heads, rows, hd), BF16),
            pltpu.VMEM((kv_heads, 2 * rows, hd), BF16),
            pltpu.VMEM((PHASES, 2 * kv_heads, rows, 2 * hd), BF16),
            pltpu.VMEM((PHASES, TP, wide, rows), BF16),
            pltpu.VMEM((PHASES, TP, half, rows), BF16),
            pltpu.VMEM((PHASES, TP, half, rows), BF16),
            pltpu.VMEM((PHASES, half, rows), F32),
            pltpu.VMEM((PHASES, half, rows), BF16),
            pltpu.VMEM((HALVES, half, rows), BF16),
            pltpu.VMEM((PHASES, 8, rows), F32),
            pltpu.VMEM((TP * HALVES, 8, rows), F32),
            pltpu.VMEM((HALVES, 8, rows), F32),
            pltpu.VMEM((8, rows), F32),
            dma((6,)),
            dma,
            dma,
            dma((TP,)),
            dma((TP,)),
            dma,
            dma((PHASES,)),
            dma((PHASES,)),
            dma((PHASES,)),
            dma((PHASES, TP, HOPS)),
            dma,
            dma((PHASES,)),
            dma((PHASES,)),
            dma((CTX, 2)),
            dma((PHASES,)),
            dma((PHASES,)),
            dma((PHASES,)),
            dma((PHASES, TP, RS_CHUNKS)),
            dma((PHASES, TP, RS_CHUNKS)),
            dma((PHASES,)),
            dma((HALVES, RS_CHUNKS)),
            dma((PHASES,)),
            dma,
            dma,
            dma,
        ],
        compiler_params=pltpu.CompilerParams(
            collective_id=0, has_side_effects=True, vmem_limit_bytes=56 * 1024 * 1024
        ),
    )(
        positions.reshape(1, rows),
        first_key.reshape(1, rows),
        input_gain,
        query_gain.reshape(1, hd),
        key_gain.reshape(1, hd),
        post_gain,
        tokens.T,
        query_weight,
        kv_weight,
        out_weight,
    ).T


def solution(mesh):
    fused = mesh.shape["tp"] == TP and mesh.shape["ctx"] == CTX
    return jax.shard_map(
        per_device_fused if fused else per_device,
        mesh=mesh,
        in_specs=(
            P(("group", "ctx"), "tp"),
            P(("group", "ctx")),
            P(("group", "ctx")),
            P(),
            P(None, "tp"),
            P(None, None, "tp"),
            P(),
            P(),
            P("tp", None),
            P(),
        ),
        out_specs=P(("group", "ctx"), "tp"),
        check_vma=False,
    )
```

```python
import math

import jax
import jax.numpy as jnp
from jax import lax
from jax.experimental import pallas as pl
from jax.experimental.pallas import tpu as pltpu
from jax.sharding import PartitionSpec as P

D = 5376
H = 32
WINDOW = 1024


EPSILON = 1e-06


def from_partner(array, axis, distance):
    return lax.ppermute(array, axis, [(i, i ^ 1 << distance) for i in range(lax.axis_size(axis))])


def passed_along(block, axis, distance):
    devices = range(lax.axis_size(axis))
    route = [(i - distance, i) for i in devices if i - distance in devices]
    return lax.ppermute(block, axis, route)


def rms_norm(values, gain_vec):
    return (
        values * lax.rsqrt(jnp.mean(values * values, axis=-1, keepdims=True) + EPSILON) * gain_vec
    )


def rotate(values, positions_in):
    half_dim = values.shape[-1] // 2
    frequency = jnp.exp(
        jnp.arange(half_dim, dtype=jnp.float32) * (-2.0 * math.log(10000.0) / values.shape[-1])
    )
    angles = positions_in.astype(jnp.float32)[:, None] * frequency[None, :]
    cosines = jnp.cos(angles)[:, None, :]
    sine_part = jnp.sin(angles)[:, None, :]
    lower_half = values[..., :half_dim]
    upper_half = values[..., half_dim:]
    return jnp.concatenate(
        [
            lower_half * cosines - upper_half * sine_part,
            upper_half * cosines + lower_half * sine_part,
        ],
        axis=-1,
    )


def per_device(
    tokens,
    positions,
    first_key,
    input_gain,
    query_weight,
    kv_weight,
    query_gain,
    key_gain,
    out_weight,
    post_gain,
):
    tok_rows = tokens.shape[0]
    feat_dev = tokens.shape[1]
    head_dim = query_gain.shape[0]
    heads_dev = query_weight.shape[1] // head_dim
    tp_index = lax.axis_index("tp")
    ctx_index = lax.axis_index("ctx")
    ctx_count = lax.axis_size("ctx")
    local_x = tokens.astype(jnp.float32)
    kv_full = kv_weight
    if heads_dev == 1:
        partner = from_partner(kv_weight, "tp", 0)
        is_even = tp_index % 2 == 0
        kv_full = jnp.where(
            is_even,
            jnp.concatenate([kv_weight, partner], axis=2),
            jnp.concatenate([partner, kv_weight], axis=2),
        )
    gathered = lax.all_gather(tokens, "tp", axis=1, tiled=True).astype(jnp.float32)
    normed = rms_norm(gathered, input_gain).astype(jnp.bfloat16)
    query_raw = jnp.dot(normed, query_weight, preferred_element_type=jnp.float32)
    key_raw = jnp.dot(normed, kv_full[0], preferred_element_type=jnp.float32)
    value_raw = jnp.dot(normed, kv_full[1], preferred_element_type=jnp.float32)
    kv_heads = key_raw.shape[1] // head_dim
    group_size = heads_dev // kv_heads
    queries = (
        rotate(rms_norm(query_raw.reshape(tok_rows, heads_dev, head_dim), query_gain), positions)
        * (D // H) ** (-0.5)
    ).astype(jnp.bfloat16)
    keys = rotate(
        rms_norm(key_raw.reshape(tok_rows, kv_heads, head_dim), key_gain), positions
    ).astype(jnp.bfloat16)
    values_b = value_raw.reshape(tok_rows, kv_heads, head_dim).astype(jnp.bfloat16)
    kv_block = jnp.stack([keys, values_b])
    reach_blocks = min(ctx_count - 1, (WINDOW + tok_rows - 2) // tok_rows)
    received = []
    moving = kv_block
    for offset in range(reach_blocks):
        moving = passed_along(moving, "ctx", 1)
        received.append(moving)
    blocks = received[::-1] + [kv_block]
    keys_all = jnp.concatenate(blocks, axis=1)
    key_count = keys_all.shape[1]
    key_index = (ctx_index - reach_blocks) * tok_rows + jnp.arange(key_count, dtype=jnp.int32)
    query_index = ctx_index * tok_rows + jnp.arange(tok_rows, dtype=jnp.int32)
    visible = (key_index[None, :] >= first_key[:, None]) & (
        key_index[None, :] <= query_index[:, None]
    )
    grouped = queries.reshape(tok_rows, kv_heads, group_size, head_dim)
    scores = jnp.einsum("qkgd,tkd->kgqt", grouped, keys_all[0], preferred_element_type=jnp.float32)
    scores = jnp.where(visible[None, None], scores, -1e30)
    row_max = jnp.max(scores, axis=-1, keepdims=True)
    weights = jnp.exp(scores - row_max)
    denominator = jnp.sum(weights, axis=-1)
    mixed_out = jnp.einsum(
        "kgqt,tkd->qkgd",
        weights.astype(jnp.bfloat16),
        keys_all[1],
        preferred_element_type=jnp.float32,
    )
    mixed_out = mixed_out / jnp.transpose(denominator, (2, 0, 1))[..., None]
    attn = mixed_out.astype(jnp.bfloat16).reshape(tok_rows, heads_dev * head_dim)
    partial_value = jnp.dot(attn, out_weight, preferred_element_type=jnp.float32)
    summed = lax.psum(partial_value.astype(jnp.bfloat16), "tp").astype(jnp.float32)
    post_normed = rms_norm(summed, post_gain)
    own_cols = lax.dynamic_slice_in_dim(post_normed, tp_index * feat_dev, feat_dev, 1)
    return (local_x + own_cols).astype(jnp.bfloat16)


MESH = pl.DeviceIdType.MESH
F32 = jnp.float32
BF16 = jnp.bfloat16
TP = 4
CTX = 4
PHASES = 2
HALVES = 2
HOPS = 4
BEFORE_0 = 1
BEFORE_1 = 2
RS_CHUNKS = 2
PRESCALE = 2.0**-10


def fused_kernel(
    pos_hbm, fk_hbm, ig_hbm, qg_hbm, kg_hbm, pg_hbm, tok_hbm, qw_hbm, kvw_hbm, ow_hbm, out_ref,
    pos_ref, fk_ref, ig_ref, qg_ref, kg_ref, pg_ref, tok_ref, xbuf, xg_ref, w_ref, wo_ref, gain_in, gain_post, gain_out, ssq_ref, acc_ref, cos_ref, sin_ref,
    meta_mine, meta_ref, kvbuf, q_ref, attn_ref, part, rup, rdn, own, fin_mine, fin_ref, sq_mine, sq_all,
    sq_pair, sq_sum,
    in_sem, tok_sem, own_sem, w_sem, wo_sem, x_send, ag_up, ag_dn, ag_pt, ag_recv, meta_send, meta_recv, kv_send, kv_recv,
    at_send, at_recv, rs_send, rs_up_recv, rs_dn_recv, fin_send, fin_recv, sq_send, sq_recv,
    pair_recv, share_send,
):
    feat, rows = tok_ref.shape
    half = feat // HALVES
    hop = feat // HOPS
    per_half = HOPS // HALVES
    chunk = half // RS_CHUNKS
    hd = qg_ref.shape[1]
    kv_heads = kvbuf.shape[2]
    kv_cols = kv_heads * hd
    q_cols = w_ref.shape[1] - 2 * kv_cols
    q_heads = q_cols // hd
    model = feat * TP
    z = lax.axis_index("tp")
    c = lax.axis_index("ctx")
    side = c // 2
    core = c % 2
    carrier = side == core
    partner = c + 1 - 2 * core
    far = lax.rem(c + 2, CTX)
    edge = (z == 0) | (z == TP - 1)
    up = {"tp": lax.rem(z + 1, TP)}
    down = {"tp": lax.rem(z + TP - 1, TP)}

    barrier = pltpu.get_barrier_semaphore()

    @pl.when(z < TP - 1)
    def _():
        pl.semaphore_signal(barrier, inc=1, device_id=up, device_id_type=MESH)

    @pl.when(z > 0)
    def _():
        pl.semaphore_signal(barrier, inc=1, device_id=down, device_id_type=MESH)

    for other in (far, partner, CTX - 1 - c):
        pl.semaphore_signal(barrier, inc=1, device_id={"ctx": other}, device_id_type=MESH)

    pairs = (
        (pos_hbm, pos_ref), (fk_hbm, fk_ref), (ig_hbm, ig_ref),
        (qg_hbm, qg_ref), (kg_hbm, kg_ref), (pg_hbm, pg_ref),
    )
    small = [
        pltpu.make_async_copy(src, dst, in_sem.at[i]) for i, (src, dst) in enumerate(pairs)
    ]
    for copy in small:
        copy.start()

    def half_span(spot):
        return pl.ds(pl.multiple_of(spot * half, 32), half)

    def weight_copies(src):
        span = pl.ds(pl.multiple_of(src * feat, 64), feat)
        kv_from = pl.ds(pl.multiple_of(core * kv_cols, 128), kv_cols)
        q_from = pl.ds(pl.multiple_of(core * q_cols, 128), q_cols)
        return (
            pltpu.make_async_copy(
                kvw_hbm.at[0, span, kv_from], w_ref.at[span, 0:kv_cols], w_sem.at[src]
            ),
            pltpu.make_async_copy(
                kvw_hbm.at[1, span, kv_from], w_ref.at[span, kv_cols : 2 * kv_cols], w_sem.at[src]
            ),
            pltpu.make_async_copy(
                qw_hbm.at[span, q_from], w_ref.at[span, 2 * kv_cols :], w_sem.at[src]
            ),
        )

    def source(i):
        second = jnp.where(z % 2 == 0, 1, 2)
        third = jnp.where(z == 0, 2, jnp.where(z == 1, 0, jnp.where(z == 2, 3, 1)))
        fourth = jnp.where(z < TP // 2, TP - 1, 0)
        return jnp.where(i == 0, z, jnp.where(i == 1, second, jnp.where(i == 2, third, fourth)))

    extra = half % 128
    turns = 128 // extra
    wide = half + 128 - extra

    def turn_of(dest):
        return (dest * HALVES + core) % turns

    def wo_copy(dest):
        start = pl.multiple_of((dest * HALVES + core) * half - turn_of(dest) * extra, 128)
        return pltpu.make_async_copy(ow_hbm.at[:, pl.ds(start, wide)], wo_ref.at[dest], wo_sem.at[dest])

    def out_order(i):
        outer = TP - 1 - i
        inner = jnp.where(i == 0, 3, jnp.where(i == 1, 0, jnp.where(i == 2, 2, 1)))
        dest = jnp.where(edge, outer, inner)
        return jnp.where(z < TP // 2, dest, TP - 1 - dest)

    def begin_weights(i, carry):
        for copy in weight_copies(source(i)):
            copy.start()
        return carry

    def begin_wo(i, carry):
        wo_copy(out_order(i)).start()
        return carry

    small[0].wait()
    small[1].wait()
    meta_mine[0:1] = pos_ref[...]
    meta_mine[1:2] = fk_ref[...]

    tok_copy = pltpu.make_async_copy(tok_hbm, tok_ref, tok_sem)
    own_copy = pltpu.make_async_copy(tok_hbm, xbuf.at[side, z], own_sem)

    @pl.when(carrier)
    def _():
        own_copy.start()
        meta_ref[side] = meta_mine[...]

    pl.semaphore_wait(barrier, jnp.where(edge, 4, 5))

    def hop_span(ch):
        return pl.ds(pl.multiple_of(ch * hop, 16), hop)

    def x_copy(ch):
        return pltpu.make_async_remote_copy(
            src_ref=tok_hbm.at[hop_span(ch)],
            dst_ref=xbuf.at[side, z, hop_span(ch)],
            send_sem=x_send,
            recv_sem=ag_recv.at[side, z, ch],
            device_id={"ctx": far},
            device_id_type=MESH,
        )

    def ag_copy(p, src, ch, send, target, block=None):
        here = xbuf.at[p, src, hop_span(ch)]
        return pltpu.make_async_remote_copy(
            src_ref=here if block is None else block.at[hop_span(ch)],
            dst_ref=here,
            send_sem=send.at[p],
            recv_sem=ag_recv.at[p, src, ch],
            device_id=target,
            device_id_type=MESH,
        )

    def meta_copy(target):
        return pltpu.make_async_remote_copy(
            src_ref=meta_mine,
            dst_ref=meta_ref.at[side],
            send_sem=meta_send,
            recv_sem=meta_recv.at[side],
            device_id={"ctx": target},
            device_id_type=MESH,
        )

    def forward_up(p, src, ch):
        @pl.when(carrier & (src <= z) & (z < TP - 1))
        def _():
            ag_copy(p, src, ch, ag_up, up).start()

    def forward_down(p, src, ch):
        @pl.when(carrier & (src >= z) & (z > 0))
        def _():
            ag_copy(p, src, ch, ag_dn, down).start()

    def forward_partner(p, src, ch):
        @pl.when(carrier)
        def _():
            ag_copy(p, src, ch, ag_pt, {"ctx": partner}).start()

    def forward(p, src, ch):
        forward_up(p, src, ch)
        forward_down(p, src, ch)
        forward_partner(p, src, ch)

    @pl.when(jnp.logical_not(carrier))
    def _():
        for ch in range(HOPS):
            x_copy(ch).start()
        meta_copy(far).start()
        meta_copy(CTX - 1 - c).start()

    @pl.when(carrier & (side == 0))
    def _():
        for ch in range(HOPS):
            @pl.when(z < TP - 1)
            def _():
                ag_copy(0, z, ch, ag_up, up, tok_hbm).start()

            @pl.when(z > 0)
            def _():
                ag_copy(0, z, ch, ag_dn, down, tok_hbm).start()

            ag_copy(0, z, ch, ag_pt, {"ctx": partner}, tok_hbm).start()

    @pl.when(carrier)
    def _():
        meta_copy(partner).start()

    lax.fori_loop(0, TP, begin_weights, 0)
    lax.fori_loop(0, TP, begin_wo, 0)
    tok_copy.start()
    for copy in small[2:]:
        copy.wait()

    ssq_ref[...] = jnp.zeros_like(ssq_ref)
    acc_ref[...] = jnp.zeros_like(acc_ref)
    r_iota = lax.broadcasted_iota(jnp.int32, (rows, rows), 0)
    c_iota = lax.broadcasted_iota(jnp.int32, (rows, rows), 1)
    diagonal = r_iota == c_iota

    def as_column(row):
        return jnp.sum(jnp.where(diagonal, row, 0.0), axis=1, keepdims=True)

    def prepare_gains():
        gains = ig_ref[...].reshape(1, model) * PRESCALE
        for i in range(TP * HALVES):
            gain_in[i] = gains[:, i * half : (i + 1) * half]
        post_gains = pg_ref[...].reshape(1, model)
        for i in range(TP):
            gain_post[i] = post_gains[:, i * feat : (i + 1) * feat]
        gain_out[...] = jnp.broadcast_to(gain_post[z], (rows, feat)).T

    def prepare_trig(p):
        @pl.when(jnp.logical_not(carrier & (side == p)))
        def _():
            pltpu.make_async_copy(meta_mine, meta_ref.at[p], meta_recv.at[p]).wait()

        lane = lax.broadcasted_iota(jnp.int32, (rows, hd), 1)
        place = jnp.where(lane < hd // 2, lane, lane - hd // 2).astype(F32)
        angles = as_column(meta_ref[p, 0:1].astype(F32)) * jnp.exp(
            place * (-2.0 * math.log(10000.0) / hd)
        )
        cos_ref[p] = jnp.cos(angles)
        sines = jnp.sin(angles)
        sin_ref[p] = jnp.where(lane < hd // 2, -sines, sines)

    def arrive_hop(p, i, ch):
        src = source(i)
        local = carrier & (i == 0) & ((side == p) if p == 0 else True)

        @pl.when(jnp.logical_not(local))
        def _():
            ag_copy(p, src, ch, ag_pt, {"ctx": partner}).wait_recv()

        @pl.when(jnp.logical_not(local) if p == 0 else i > 0)
        def _():
            forward(p, src, ch)

    def arrive(p, i, g):
        for j in range(per_half):
            arrive_hop(p, i, g * per_half + j)

    def arrive_both(p, ch):
        arrive_hop(p, 1, ch)
        arrive_hop(p, 2, ch)

    def begin_second(inner, outer):
        for ch in range(HOPS):
            @pl.when(carrier & (side == 0) & inner)
            def _():
                ag_copy(1, z, ch, ag_pt, {"ctx": partner}).wait_recv()

            @pl.when(jnp.where(z < TP // 2, inner, outer))
            def _():
                forward_up(1, z, ch)

            @pl.when(jnp.where(z < TP // 2, outer, inner))
            def _():
                forward_down(1, z, ch)

            @pl.when(outer)
            def _():
                forward_partner(1, z, ch)

    kv_width = 2 * kv_cols

    def project(p, i, g):
        src = source(i)
        spot = src * HALVES + g
        x_t = xbuf[p, src, pl.ds(pl.multiple_of(g * half, 32), half)].astype(F32)
        ssq_ref[p] += jnp.sum(x_t * x_t, axis=0, keepdims=True)
        xg_ref[...] = (x_t.T * gain_in[spot]).astype(BF16)
        last = (i == TP - 1) & (g == HALVES - 1)
        if p == 0:
            @pl.when(g == 0)
            def _():
                loaded = w_ref.at[pl.ds(pl.multiple_of(src * feat, 64), feat)]
                pltpu.make_async_copy(loaded, loaded, w_sem.at[src]).wait()


        @pl.when(jnp.logical_not(last))
        def _():
            acc_ref[p] += jnp.dot(xg_ref[...], w_ref[half_span(spot)], preferred_element_type=F32)

        @pl.when(last)
        def _():
            acc_ref[p, :, 0:kv_width] += jnp.dot(
                xg_ref[...], w_ref[half_span(spot), 0:kv_width], preferred_element_type=F32
            )

    middle = jnp.logical_not(edge)
    lag = jnp.where(middle, 1, 0)

    def first_gather(step, carry):
        i = step // HALVES
        g = step % HALVES

        @pl.when((edge & (i < TP)) | (middle & (i != 1) & (i < TP - 1)))
        def _():
            arrive(0, jnp.where(middle & (i == 2), TP - 1, i), g)

        @pl.when(middle & (i == 1))
        def _():
            for j in range(per_half):
                arrive_both(0, g * per_half + j)

        @pl.when((g == HALVES - 1) & ((i == 1) | (middle & (i == 2))))
        def _():
            begin_second(i == 1, edge | (i == 2))

        @pl.when(step == 0)
        def _():
            @pl.when(carrier)
            def _():
                own_copy.wait()

            prepare_gains()

        @pl.when((g == 0) & (i == jnp.where(edge, 1, TP)))
        def _():
            prepare_trig(0)

        @pl.when((i >= lag) & (i < TP + lag))
        def _():
            project(0, i - lag, g)

        return carry

    lax.fori_loop(0, (TP + lag) * HALVES, first_gather, 0)

    def kv_copy(p, j):
        here = kvbuf.at[2 * p + side, j]
        return pltpu.make_async_remote_copy(
            src_ref=here,
            dst_ref=here,
            send_sem=kv_send.at[p],
            recv_sem=kv_recv.at[2 * p + side, j],
            device_id={"ctx": far},
            device_id_type=MESH,
        )

    def kv_arrived(block, j):
        there = kvbuf.at[block, j]
        pltpu.make_async_copy(there, there, kv_recv.at[block, j]).wait()

    def attn_copy(p, h):
        here = attn_ref.at[p, kv_heads * core + h]
        return pltpu.make_async_remote_copy(
            src_ref=here,
            dst_ref=here,
            send_sem=at_send.at[p],
            recv_sem=at_recv.at[p],
            device_id={"ctx": partner},
            device_id_type=MESH,
        )

    def attn_wait(p, owner, sem):
        both = attn_ref.at[p, pl.ds(kv_heads * owner, kv_heads)]
        pltpu.make_async_copy(both, both, sem.at[p]).wait()

    def attend(p, ready, late):
        own_block = ready[0]
        first = as_column(meta_ref[p, 1:2].astype(F32)).astype(jnp.int32)

        def hidden(block):
            visible = block * rows + c_iota >= first
            if block == own_block:
                visible = visible & (c_iota <= r_iota)
            bias = jnp.where(visible, 0.0, -1e30)
            return jnp.concatenate([bias, bias], axis=0)

        def score(h, block, bias):
            return bias + lax.dot_general(
                q_ref[h], kvbuf[block, 0, h], (((1,), (1,)), ((), ())), preferred_element_type=F32
            )

        def mix(h, weights, blocks):
            weights = weights.astype(BF16)
            return sum(
                jnp.dot(
                    weights[:, j * rows : (j + 1) * rows], kvbuf[block, 1, h],
                    preferred_element_type=F32,
                )
                for j, block in enumerate(blocks)
            )

        biases = [hidden(block) for block in ready]
        states = []
        for h in range(kv_heads):
            s = jnp.concatenate([score(h, b, bias) for b, bias in zip(ready, biases)], axis=1)
            top = jnp.max(s, axis=1, keepdims=True)
            weights = jnp.exp(s - top)
            states.append((top, jnp.sum(weights, axis=1, keepdims=True), mix(h, weights, ready)))
        if late is not None:
            late_bias = hidden(late)
            kv_arrived(late, 0)
            late_weights = []
            for h in range(kv_heads):
                top, total, mixed = states[h]
                s = score(h, late, late_bias)
                higher = jnp.maximum(top, jnp.max(s, axis=1, keepdims=True))
                fade = jnp.exp(top - higher)
                weights = jnp.exp(s - higher)
                total = total * fade + jnp.sum(weights, axis=1, keepdims=True)
                states[h] = (higher, total, mixed * fade)
                late_weights.append(weights)
            kv_arrived(late, 1)
        for h in range(kv_heads):
            _, total, mixed = states[h]
            if late is not None:
                mixed = mixed + mix(h, late_weights[h], [late])
            mixed = (mixed / total).astype(BF16)
            attn_ref[p, kv_heads * core + h] = jnp.concatenate([mixed[:rows], mixed[rows:]], axis=1)
            attn_copy(p, h).start()

    def attention(p):
        inv = lax.rsqrt(as_column(ssq_ref[p]) * (1.0 / model) + EPSILON) * (1.0 / PRESCALE)

        def normed_rotated(raw, gain_vec):
            raw = raw * inv
            scaled = raw * lax.rsqrt(jnp.mean(raw * raw, axis=1, keepdims=True) + EPSILON) * gain_vec
            return scaled * cos_ref[p] + pltpu.roll(scaled, hd // 2, 1) * sin_ref[p]

        block = 2 * p + side
        for h in range(kv_heads):
            cols = slice(h * hd, (h + 1) * hd)
            kvbuf[block, 0, h] = normed_rotated(acc_ref[p, :, cols], kg_ref[...]).astype(BF16)

        @pl.when((p == 0) | (side == 0))
        def _():
            kv_copy(p, 0).start()

        for h in range(kv_heads):
            cols = slice(kv_cols + h * hd, kv_cols + (h + 1) * hd)
            kvbuf[block, 1, h] = (acc_ref[p, :, cols] * inv).astype(BF16)

        @pl.when((p == 0) | (side == 0))
        def _():
            kv_copy(p, 1).start()

        spot = source(TP - 1) * HALVES + HALVES - 1
        acc_ref[p, :, kv_width:] += jnp.dot(
            xg_ref[...], w_ref[half_span(spot), kv_width:], preferred_element_type=F32
        )
        for h in range(q_heads):
            cols = slice(kv_width + h * hd, kv_width + (h + 1) * hd)
            q_ref[h // 2, (h % 2) * rows : (h % 2 + 1) * rows] = (
                normed_rotated(acc_ref[p, :, cols], qg_ref[...]) * (D // H) ** (-0.5)
            ).astype(BF16)

        if p == 0:
            @pl.when(middle)
            def _():
                for ch in range(HOPS):
                    arrive_both(1, ch)

                def own_block(g, carry):
                    arrive(1, 0, g)
                    project(1, 0, g)
                    return carry

                lax.fori_loop(0, HALVES, own_block, 0)
        else:
            sum_terms(0, 2, TP - 1)

        @pl.when(side == 0)
        def _():
            if p == 1:
                for j in range(2):
                    kv_arrived(1, j)
            attend(p, [2 * p, *range(2 * p)], None)

        @pl.when(side == 1)
        def _():
            attend(p, [2 * p + 1, *range(2 * p)], 2 * p)

    def rs_copy(p, dest, ch, buf, recv, target):
        start = pl.multiple_of(turn_of(dest) * extra + ch * chunk, 16)
        return pltpu.make_async_remote_copy(
            src_ref=part.at[p, dest, pl.ds(start, chunk)],
            dst_ref=buf.at[p, dest, pl.ds(pl.multiple_of(ch * chunk, 16), chunk)],
            send_sem=rs_send.at[p],
            recv_sem=recv.at[p, dest, ch],
            device_id=target,
            device_id_type=MESH,
        )

    def rs_up(p, dest, ch):
        return rs_copy(p, dest, ch, rup, rs_up_recv, up)

    def rs_dn(p, dest, ch):
        return rs_copy(p, dest, ch, rdn, rs_dn_recv, down)

    def output_terms(p):
        def half_product(dest, owner):
            span = pl.ds(pl.multiple_of(owner * q_cols, 128), q_cols)
            mixed = jnp.concatenate(
                [attn_ref[p, kv_heads * owner + j] for j in range(kv_heads)], axis=1
            )
            return jnp.dot(mixed, wo_ref[dest, span], preferred_element_type=F32)

        def send_term(dest, term):
            part[p, dest] = term.T.astype(BF16)
            for ch in range(RS_CHUNKS):
                @pl.when((z == 0) & (dest > 0))
                def _():
                    rs_up(p, dest, ch).start()

                @pl.when((z == TP - 1) & (dest < TP - 1))
                def _():
                    rs_dn(p, dest, ch).start()

        first = out_order(0)
        if p == 0:
            wo_copy(first).wait()
        near = half_product(first, core)
        attn_wait(p, 1 - core, at_recv)
        send_term(first, near + half_product(first, 1 - core))

        def out_step(i, carry):
            dest = out_order(i)
            if p == 0:
                wo_copy(dest).wait()
            mixed = jnp.concatenate([attn_ref[p, j] for j in range(2 * kv_heads)], axis=1)
            send_term(dest, jnp.dot(mixed, wo_ref[dest], preferred_element_type=F32))
            return carry

        lax.fori_loop(1, TP, out_step, 0)
        own[p] = part[p, z, pl.ds(pl.multiple_of(turn_of(z) * extra, 16), half)].astype(F32)

    def fin_copy(p, ch):
        span = pl.ds(pl.multiple_of(ch * chunk, 16), chunk)
        return pltpu.make_async_remote_copy(
            src_ref=fin_mine.at[p, span],
            dst_ref=fin_ref.at[core, span],
            send_sem=fin_send.at[p],
            recv_sem=fin_recv.at[core, ch],
            device_id={"ctx": 2 * p + side},
            device_id_type=MESH,
        )

    def sq_copy(p, d):
        return pltpu.make_async_remote_copy(
            src_ref=sq_mine.at[p],
            dst_ref=sq_all.at[HALVES * z + core],
            send_sem=sq_send.at[p],
            recv_sem=sq_recv,
            device_id={"ctx": 2 * p + side, "tp": lax.rem(z + d, TP)},
            device_id_type=MESH,
        )

    def sum_terms(p, begin, end):
        mine = c == 2 * p + side

        def sum_step(k, carry):
            from_low = z + TP - 1 - k
            from_high = z + k - (TP - 1)
            for ch in range(RS_CHUNKS):
                span = slice(ch * chunk, (ch + 1) * chunk)
                low = (z > 0) & (from_low < TP)
                high = (z < TP - 1) & (from_high >= 0)
                for dest, has, buf, copy in (
                    (from_high, high & (z == 1), rdn, rs_dn),
                    (from_low, low, rup, rs_up),
                    (from_high, high & (z != 1), rdn, rs_dn),
                ):
                    @pl.when(has)
                    def _():
                        copy(p, dest, ch).wait_recv()

                        @pl.when(dest != z)
                        def _():
                            start = pl.multiple_of(turn_of(dest) * extra + ch * chunk, 16)
                            there = pl.ds(start, chunk)
                            part[p, dest, there] = (
                                part[p, dest, there].astype(F32) + buf[p, dest, span].astype(F32)
                            ).astype(BF16)
                            copy(p, dest, ch).start()

                        @pl.when(dest == z)
                        def _():
                            own[p, span] += buf[p, dest, span].astype(F32)

                @pl.when(k == TP - 1)
                def _():
                    rounded = own[p, span].astype(BF16)

                    @pl.when(mine)
                    def _():
                        fin_ref[core, span] = rounded

                    @pl.when(jnp.logical_not(mine))
                    def _():
                        fin_mine[p, span] = rounded
                        fin_copy(p, ch).start()

            return carry

        lax.fori_loop(begin, end, sum_step, 0)

    def pair_copy():
        return pltpu.make_async_remote_copy(
            src_ref=sq_mine.at[0],
            dst_ref=sq_pair.at[core],
            send_sem=sq_send.at[0],
            recv_sem=pair_recv,
            device_id={"ctx": 1},
            device_id_type=MESH,
        )

    def share_copy(d):
        return pltpu.make_async_remote_copy(
            src_ref=sq_sum,
            dst_ref=sq_all.at[z],
            send_sem=share_send,
            recv_sem=sq_recv,
            device_id={"tp": lax.rem(z + d, TP)},
            device_id_type=MESH,
        )

    def send_squares(p):
        mine = c == 2 * p + side
        as_row = jnp.sum(own[p] * own[p], axis=0, keepdims=True)
        sq_mine[p] = jnp.broadcast_to(as_row, sq_mine.shape[1:])

        @pl.when(mine)
        def _():
            sq_all[HALVES * z + core] = sq_mine[p]

        def send_direct():
            @pl.when(jnp.logical_not(mine))
            def _():
                sq_copy(p, 0).start()

            for d in range(1, TP):
                sq_copy(p, d).start()

        if p == 0:
            pl.when(side == 0)(send_direct)

            @pl.when(side == 1)
            def _():
                pair_copy().start()
        else:
            send_direct()

    attention(0)

    @pl.when(middle)
    def _():
        for g in range(HALVES):
            arrive(1, TP - 1, g)

    output_terms(0)
    prepare_trig(1)
    before_sums = HALVES * jnp.where(side == 0, BEFORE_0, BEFORE_1)

    def second_gather(step, carry):
        i = step // HALVES
        g = step % HALVES

        @pl.when(step == before_sums)
        def _():
            sum_terms(0, 1, 2)

        @pl.when(edge)
        def _():
            arrive(1, i, g)

        project(1, i, g)
        return carry

    lax.fori_loop(jnp.where(edge, 0, HALVES), TP * HALVES, second_gather, 0)
    attention(1)
    output_terms(1)
    sum_terms(0, TP - 1, TP)
    send_squares(0)
    sum_terms(1, 1, TP - 1)

    def landed(whole, sem):
        pltpu.make_async_copy(whole, whole, sem).wait()

    tok_copy.wait()

    @pl.when(jnp.logical_not(carrier))
    def _():
        landed(tok_ref, x_send)
        landed(meta_ref, meta_send)

    @pl.when(carrier)
    def _():
        landed(meta_mine, meta_send)

    for p in range(PHASES):
        @pl.when(carrier)
        def _():
            for n in range(1, TP):
                @pl.when(z == n - 1)
                def _():
                    landed(xbuf.at[p, 0:n], ag_up.at[p])

                @pl.when(z == TP - n)
                def _():
                    landed(xbuf.at[p, 0:n], ag_dn.at[p])

            landed(xbuf.at[p], ag_pt.at[p])

        @pl.when((p == 0) | (side == 0))
        def _():
            landed(kvbuf.at[2 * p + side], kv_send.at[p])

        attn_wait(p, core, at_send)

    sum_terms(1, TP - 1, TP)
    send_squares(1)

    for p in range(PHASES):
        landed(rup.at[p, 0 : TP - 1], rs_send.at[p])

    source_side = c % 2

    @pl.when(c == 1)
    def _():
        landed(sq_pair, pair_recv)
        sq_sum[...] = sq_pair[0] + sq_pair[1]
        for d in range(1, TP):
            share_copy(d).start()
        sq_all[z] = sq_sum[...]
        sq_all[TP:] = jnp.zeros((TP * HALVES - TP, *sq_sum.shape), F32)

    for kk in range(HALVES):
        for ch in range(RS_CHUNKS):
            @pl.when(2 * source_side + kk != c)
            def _():
                landed(fin_ref.at[kk, slice(ch * chunk, (ch + 1) * chunk)], fin_recv.at[kk, ch])

            span = slice(kk * half + ch * chunk, kk * half + (ch + 1) * chunk)
            gain_out[span] = fin_ref[kk, ch * chunk : (ch + 1) * chunk].astype(F32) * gain_out[span]

    @pl.when(carrier)
    def _():
        landed(sq_all.at[0 : TP * HALVES - 1], sq_recv)

    @pl.when(c == 1)
    def _():
        landed(sq_all.at[0 : TP - 1], sq_recv)

    @pl.when(c == 2)
    def _():
        landed(sq_all, sq_recv)

    total = jnp.sum(sq_all[...], axis=0)[0:1]
    inv_post = lax.rsqrt(total * (1.0 / model) + EPSILON)
    out_ref[...] = (tok_ref[...].astype(F32) + gain_out[...] * inv_post).astype(BF16)

    for p in range(PHASES):
        paired = (side == 1) if p == 0 else False

        @pl.when(c != 2 * p + side)
        def _():
            landed(fin_mine.at[p], fin_send.at[p])

            @pl.when(jnp.logical_not(paired))
            def _():
                landed(sq_all.at[0:TP], sq_send.at[p])

        @pl.when(paired)
        def _():
            landed(sq_mine.at[0], sq_send.at[0])

        @pl.when(c == 2 * p + side)
        def _():
            landed(sq_all.at[0 : TP - 1], sq_send.at[p])

    @pl.when(c == 1)
    def _():
        landed(sq_all.at[0 : TP - 1], share_send)


def per_device_fused(
    tokens, positions, first_key, input_gain, query_weight, kv_weight, query_gain, key_gain,
    out_weight, post_gain,
):
    feat, rows = tokens.shape[1], tokens.shape[0]
    half = feat // HALVES
    hd = query_gain.shape[0]
    model = query_weight.shape[0]
    q_cols = query_weight.shape[1] // 2
    kv_cols = kv_weight.shape[2] // 2
    kv_heads = kv_cols // hd
    wide = half + 128 - half % 128
    vmem = pl.BlockSpec(memory_space=pltpu.VMEM)
    anywhere = pl.BlockSpec(memory_space=pl.ANY)
    dma = pltpu.SemaphoreType.DMA
    return pl.pallas_call(
        fused_kernel,
        out_shape=pltpu.VMEM((feat, rows), BF16),
        in_specs=[anywhere] * 10,
        out_specs=vmem,
        scratch_shapes=[
            pltpu.VMEM((1, rows), jnp.int32),
            pltpu.VMEM((1, rows), jnp.int32),
            pltpu.VMEM((model,), F32),
            pltpu.VMEM((1, hd), F32),
            pltpu.VMEM((1, hd), F32),
            pltpu.VMEM((model,), F32),
            pltpu.VMEM((feat, rows), BF16),
            pltpu.VMEM((PHASES, TP, feat, rows), BF16),
            pltpu.VMEM((rows, half), BF16),
            pltpu.VMEM((model, q_cols + 2 * kv_cols), BF16),
            pltpu.VMEM((TP, 2 * q_cols, wide), BF16),
            pltpu.VMEM((TP * HALVES, 1, half), F32),
            pltpu.VMEM((TP, 1, feat), F32),
            pltpu.VMEM((feat, rows), F32),
            pltpu.VMEM((PHASES, 1, rows), F32),
            pltpu.VMEM((PHASES, rows, q_cols + 2 * kv_cols), F32),
            pltpu.VMEM((PHASES, rows, hd), F32),
            pltpu.VMEM((PHASES, rows, hd), F32),
            pltpu.VMEM((8, rows), jnp.int32),
            pltpu.VMEM((PHASES, 8, rows), jnp.int32),
            pltpu.VMEM((CTX, 2, kv_heads, rows, hd), BF16),
            pltpu.VMEM((kv_heads, 2 * rows, hd), BF16),
            pltpu.VMEM((PHASES, 2 * kv_heads, rows, 2 * hd), BF16),
            pltpu.VMEM((PHASES, TP, wide, rows), BF16),
            pltpu.VMEM((PHASES, TP, half, rows), BF16),
            pltpu.VMEM((PHASES, TP, half, rows), BF16),
            pltpu.VMEM((PHASES, half, rows), F32),
            pltpu.VMEM((PHASES, half, rows), BF16),
            pltpu.VMEM((HALVES, half, rows), BF16),
            pltpu.VMEM((PHASES, 8, rows), F32),
            pltpu.VMEM((TP * HALVES, 8, rows), F32),
            pltpu.VMEM((HALVES, 8, rows), F32),
            pltpu.VMEM((8, rows), F32),
            dma((6,)),
            dma,
            dma,
            dma((TP,)),
            dma((TP,)),
            dma,
            dma((PHASES,)),
            dma((PHASES,)),
            dma((PHASES,)),
            dma((PHASES, TP, HOPS)),
            dma,
            dma((PHASES,)),
            dma((PHASES,)),
            dma((CTX, 2)),
            dma((PHASES,)),
            dma((PHASES,)),
            dma((PHASES,)),
            dma((PHASES, TP, RS_CHUNKS)),
            dma((PHASES, TP, RS_CHUNKS)),
            dma((PHASES,)),
            dma((HALVES, RS_CHUNKS)),
            dma((PHASES,)),
            dma,
            dma,
            dma,
        ],
        compiler_params=pltpu.CompilerParams(
            collective_id=0, has_side_effects=True, vmem_limit_bytes=56 * 1024 * 1024
        ),
    )(
        positions.reshape(1, rows),
        first_key.reshape(1, rows),
        input_gain,
        query_gain.reshape(1, hd),
        key_gain.reshape(1, hd),
        post_gain,
        tokens.T,
        query_weight,
        kv_weight,
        out_weight,
    ).T


def solution(mesh):
    fused = mesh.shape["tp"] == TP and mesh.shape["ctx"] == CTX
    return jax.shard_map(
        per_device_fused if fused else per_device,
        mesh=mesh,
        in_specs=(
            P(("group", "ctx"), "tp"),
            P(("group", "ctx")),
            P(("group", "ctx")),
            P(),
            P(None, "tp"),
            P(None, None, "tp"),
            P(),
            P(),
            P("tp", None),
            P(),
        ),
        out_specs=P(("group", "ctx"), "tp"),
        check_vma=False,
    )
```
